32 devices in a mesh: dp: 8 (over z, x), seq: 4 (over y, core).
Axes of the slice: x: 2, y: 2, z: 4, core: 2. Of those that a mesh axis runs over, the one named last changes fastest.
Arguments:
- tokens: bfloat16 [16, 1024, 768], P('dp', 'seq'), may hold values from -6 to 6
- early: bfloat16 [16, 1024, 768], P('dp', 'seq'), may hold values from -6 to 6
- cot_backbone: bfloat16 [16, 1024, 768], P('dp', 'seq'), may hold values from -6 to 6
- cot_head: bfloat16 [16, 1024, 768], P('dp', 'seq'), may hold values from -6 to 6
- lengths: int32 [16], P('dp'), may hold values from 1024 to 1024, as said below
- cls_pos: int32 [16], P('dp'), may hold values from 0 to 1023
- back_query: bfloat16 [768, 768], P(('dp', 'seq')), may hold values from -0.3125 to 0.3125
- back_query_bias: bfloat16 [768], P(('dp', 'seq')), may hold values from -3 to 3
- back_key: bfloat16 [768, 768], P(('dp', 'seq')), may hold values from -0.3125 to 0.3125
- back_value: bfloat16 [768, 768], P(('dp', 'seq')), may hold values from -0.21875 to 0.21875
- back_value_bias: bfloat16 [768], P(('dp', 'seq')), may hold values from -3 to 3
- back_output: bfloat16 [768, 768], P(('dp', 'seq')), may hold values from -0.75 to 0.75
- back_output_bias: bfloat16 [768], P(('dp', 'seq')), may hold values from -3 to 3
- back_attn_gain: bfloat16 [768], P(('dp', 'seq')), may hold values from 0.099609375 to 1.8984375
- back_attn_shift: bfloat16 [768], P(('dp', 'seq')), may hold values from -3 to 3
- back_expand: bfloat16 [768, 3072], P(('dp', 'seq')), may hold values from -0.21875 to 0.21875
- back_expand_bias: bfloat16 [3072], P(('dp', 'seq')), may hold values from -3 to 3
- back_reduce: bfloat16 [3072, 768], P(('dp', 'seq')), may hold values from -0.109375 to 0.109375
- back_reduce_bias: bfloat16 [768], P(('dp', 'seq')), may hold values from -3 to 3
- back_ffn_gain: bfloat16 [768], P(('dp', 'seq')), may hold values from 0.099609375 to 1.8984375
- back_ffn_shift: bfloat16 [768], P(('dp', 'seq')), may hold values from -3 to 3
- head_query: bfloat16 [768, 768], P(('dp', 'seq')), may hold values from -0.3125 to 0.3125
- head_query_bias: bfloat16 [768], P(('dp', 'seq')), may hold values from -3 to 3
- head_key: bfloat16 [768, 768], P(('dp', 'seq')), may hold values from -0.3125 to 0.3125
- head_value: bfloat16 [768, 768], P(('dp', 'seq')), may hold values from -0.21875 to 0.21875
- head_value_bias: bfloat16 [768], P(('dp', 'seq')), may hold values from -3 to 3
- head_output: bfloat16 [768, 768], P(('dp', 'seq')), may hold values from -0.75 to 0.75
- head_output_bias: bfloat16 [768], P(('dp', 'seq')), may hold values from -3 to 3
- head_attn_gain: bfloat16 [768], P(('dp', 'seq')), may hold values from 0.099609375 to 1.8984375
- head_attn_shift: bfloat16 [768], P(('dp', 'seq')), may hold values from -3 to 3
- head_expand: bfloat16 [768, 3072], P(('dp', 'seq')), may hold values from -0.21875 to 0.21875
- head_expand_bias: bfloat16 [3072], P(('dp', 'seq')), may hold values from -3 to 3
- head_reduce: bfloat16 [3072, 768], P(('dp', 'seq')), may hold values from -0.109375 to 0.109375
- head_reduce_bias: bfloat16 [768], P(('dp', 'seq')), may hold values from -3 to 3
- head_ffn_gain: bfloat16 [768], P(('dp', 'seq')), may hold values from 0.099609375 to 1.8984375
- head_ffn_shift: bfloat16 [768], P(('dp', 'seq')), may hold values from -3 to 3
Outputs:
- backbone_out: bfloat16 [16, 1024, 768], P('dp', 'seq')
- head_out: bfloat16 [16, 1024, 768], P('dp', 'seq')
- grad_tokens: bfloat16 [16, 1024, 768], P('dp', 'seq')
- grad_early: bfloat16 [16, 1024, 768], P('dp', 'seq')
- grad_back_query: float32 [768, 768], P(('dp', 'seq'))
- grad_back_query_bias: float32 [768], P(('dp', 'seq'))
- grad_back_key: float32 [768, 768], P(('dp', 'seq'))
- grad_back_value: float32 [768, 768], P(('dp', 'seq'))
- grad_back_value_bias: float32 [768], P(('dp', 'seq'))
- grad_back_output: float32 [768, 768], P(('dp', 'seq'))
- grad_back_output_bias: float32 [768], P(('dp', 'seq'))
- grad_back_attn_gain: float32 [768], P(('dp', 'seq'))
- grad_back_attn_shift: float32 [768], P(('dp', 'seq'))
- grad_back_expand: float32 [768, 3072], P(('dp', 'seq'))
- grad_back_expand_bias: float32 [3072], P(('dp', 'seq'))
- grad_back_reduce: float32 [3072, 768], P(('dp', 'seq'))
- grad_back_reduce_bias: float32 [768], P(('dp', 'seq'))
- grad_back_ffn_gain: float32 [768], P(('dp', 'seq'))
- grad_back_ffn_shift: float32 [768], P(('dp', 'seq'))
- grad_head_query: float32 [768, 768], P(('dp', 'seq'))
- grad_head_query_bias: float32 [768], P(('dp', 'seq'))
- grad_head_key: float32 [768, 768], P(('dp', 'seq'))
- grad_head_value: float32 [768, 768], P(('dp', 'seq'))
- grad_head_value_bias: float32 [768], P(('dp', 'seq'))
- grad_head_output: float32 [768, 768], P(('dp', 'seq'))
- grad_head_output_bias: float32 [768], P(('dp', 'seq'))
- grad_head_attn_gain: float32 [768], P(('dp', 'seq'))
- grad_head_attn_shift: float32 [768], P(('dp', 'seq'))
- grad_head_expand: float32 [768, 3072], P(('dp', 'seq'))
- grad_head_expand_bias: float32 [3072], P(('dp', 'seq'))
- grad_head_reduce: float32 [3072, 768], P(('dp', 'seq'))
- grad_head_reduce_bias: float32 [768], P(('dp', 'seq'))
- grad_head_ffn_gain: float32 [768], P(('dp', 'seq'))
- grad_head_ffn_shift: float32 [768], P(('dp', 'seq'))
The draws below stay inside these ranges and needn't reach their ends.
Inputs may be any that keep to these rules, and one draw needn't show every extreme that they name: `lengths`: the first length positions of a sequence hold tokens, the rest is padding; every sequence has length 1024 (no padding).
All inputs are finite; a program needn't handle non-finite values.
Results may differ from the reference program's by a relative error of at most 0.03.
Values may be sent and summed in bfloat16 or wider, within the bound.
A program may use at most 256 MiB of HBM per device.

```python
import math
import jax
import jax.numpy as jnp
from jax import lax

D = 768
H = 12
HD = 64
FF = 3072
MIN_LEN = 1024
SEQLEN = 1024
SEQS = 16


def draw_lengths(key, part):
    drawn = jax.random.randint(key, (SEQS,), MIN_LEN, SEQLEN + 1, dtype=jnp.int32)
    return drawn.at[0].set(SEQLEN).at[1].set(MIN_LEN)


def touch_ends(values, stream_key, low, largest):
    index_at = [jax.random.randint(jax.random.fold_in(stream_key, axis), (), 0, length) for axis, length in enumerate(values.shape)]
    widest = values.shape.index(max(values.shape))
    beside = index_at[:widest] + [(index_at[widest] + 1) % values.shape[widest]] + index_at[widest + 1:]
    return values.at[tuple(index_at)].set(low).at[tuple(beside)].set(largest)


def raised(values, stream_key, source, target, parts, factor):
    owner, partner = [(jnp.arange(values.shape[dim]) // (values.shape[dim] // parts)).reshape([-1 if axis == dim else 1 for axis in range(values.ndim)]) for dim in (source, target)]
    chosen = jax.random.permutation(stream_key, parts)[partner]
    strong = (owner == chosen) | (owner == (partner + parts // 2) % parts)
    return jnp.where(strong, factor * values, values)


def block_levels(own_key, dims, pieces, smallest, high):
    def one(position, shards_of):
        heights = jax.random.uniform(jax.random.fold_in(jax.random.fold_in(own_key, 6), position), (shards_of,), jnp.float32, smallest / len(pieces), high / len(pieces))
        return jnp.repeat(jnp.exp(heights), dims[position] // shards_of).reshape((-1,) + (1,) * (len(dims) - position - 1))

    level = one(*pieces[0])
    for cut in pieces[1:]:
        level = level * one(*cut)
    return level


def gaussian(rng, extent, scale, limit, pieces=(), kind=jnp.bfloat16):
    level = block_levels(rng, extent, pieces, -0.22, 0.18) if pieces else 1.0
    entries = jax.random.normal(rng, extent, jnp.float32) * scale * level
    return jnp.minimum(jnp.maximum(entries, -limit), limit).astype(kind)


def gaussian_with(stream_key, dims, scale, bound, pieces, heavy, kind=jnp.bfloat16):
    array = scale * jax.random.normal(stream_key, dims, jnp.float32)
    if pieces:
        array = array * block_levels(stream_key, dims, pieces, -0.22, 0.18)
    return jnp.clip(raised(array, jax.random.fold_in(stream_key, 3), *heavy), -bound, bound).astype(kind)


def setup_inputs(seed: int = 0) -> dict:
    key_of = jax.random.split(jax.random.key(seed), 37)
    return {
        "tokens": gaussian_with(key_of[0], (SEQS, SEQLEN, D), 1.0, 6.0, ((0, 8), (1, 4)), (0, 2, 8, 2.0)),
        "early": gaussian_with(key_of[1], (SEQS, SEQLEN, D), 1.0, 6.0, ((0, 8), (1, 4)), (0, 2, 8, 2.0)),
        "cot_backbone": gaussian(key_of[2], (SEQS, SEQLEN, D), 1.0, 6.0, ((0, 8), (1, 4))),
        "cot_head": gaussian(key_of[3], (SEQS, SEQLEN, D), 1.0, 6.0, ((0, 8), (1, 4))),
        "lengths": draw_lengths(jax.random.fold_in(key_of[36], 71), 0),
        "cls_pos": touch_ends(jax.random.randint(key_of[5], (SEQS,), 0, MIN_LEN), jax.random.fold_in(key_of[5], 1), 0, MIN_LEN - 1).astype(jnp.int32),
        "back_query": gaussian(key_of[6], (D, D), (D // 2) ** -0.5, 0.3125, ((0, 32),)),
        "back_query_bias": gaussian(key_of[7], (D,), 0.5, 3.0, ((0, 32),)),
        "back_key": gaussian(key_of[8], (D, D), (D // 2) ** -0.5, 0.3125, ((0, 32),)),
        "back_value": gaussian(key_of[9], (D, D), D ** -0.5, 0.21875, ((0, 32),)),
        "back_value_bias": gaussian(key_of[10], (D,), 0.5, 3.0, ((0, 32),)),
        "back_output": gaussian(key_of[11], (D, D), (D // 12) ** -0.5, 0.75, ((0, 32),)),
        "back_output_bias": gaussian(key_of[12], (D,), 0.5, 3.0, ((0, 32),)),
        "back_attn_gain": jnp.clip(1.0 + 0.18 * jax.random.normal(key_of[13], (D,), jnp.float32), 0.099609375, 1.8984375).astype(jnp.bfloat16),
        "back_attn_shift": gaussian(key_of[14], (D,), 0.5, 3.0, ((0, 32),)),
        "back_expand": gaussian(key_of[15], (D, FF), D ** -0.5, 0.21875, ((0, 32),)),
        "back_expand_bias": gaussian(key_of[16], (FF,), 0.5, 3.0, ((0, 32),)),
        "back_reduce": gaussian(key_of[17], (FF, D), FF ** -0.5, 0.109375, ((0, 32),)),
        "back_reduce_bias": gaussian(key_of[18], (D,), 0.5, 3.0, ((0, 32),)),
        "back_ffn_gain": jnp.clip(1.0 + 0.18 * jax.random.normal(key_of[19], (D,), jnp.float32), 0.099609375, 1.8984375).astype(jnp.bfloat16),
        "back_ffn_shift": gaussian(key_of[20], (D,), 0.5, 3.0, ((0, 32),)),
        "head_query": gaussian(key_of[21], (D, D), (D // 2) ** -0.5, 0.3125, ((0, 32),)),
        "head_query_bias": gaussian(key_of[22], (D,), 0.5, 3.0, ((0, 32),)),
        "head_key": gaussian(key_of[23], (D, D), (D // 2) ** -0.5, 0.3125, ((0, 32),)),
        "head_value": gaussian(key_of[24], (D, D), D ** -0.5, 0.21875, ((0, 32),)),
        "head_value_bias": gaussian(key_of[25], (D,), 0.5, 3.0, ((0, 32),)),
        "head_output": gaussian(key_of[26], (D, D), (D // 12) ** -0.5, 0.75, ((0, 32),)),
        "head_output_bias": gaussian(key_of[27], (D,), 0.5, 3.0, ((0, 32),)),
        "head_attn_gain": jnp.clip(1.0 + 0.18 * jax.random.normal(key_of[28], (D,), jnp.float32), 0.099609375, 1.8984375).astype(jnp.bfloat16),
        "head_attn_shift": gaussian(key_of[29], (D,), 0.5, 3.0, ((0, 32),)),
        "head_expand": gaussian(key_of[30], (D, FF), D ** -0.5, 0.21875, ((0, 32),)),
        "head_expand_bias": gaussian(key_of[31], (FF,), 0.5, 3.0, ((0, 32),)),
        "head_reduce": gaussian(key_of[32], (FF, D), FF ** -0.5, 0.109375, ((0, 32),)),
        "head_reduce_bias": gaussian(key_of[33], (D,), 0.5, 3.0, ((0, 32),)),
        "head_ffn_gain": jnp.clip(1.0 + 0.18 * jax.random.normal(key_of[34], (D,), jnp.float32), 0.099609375, 1.8984375).astype(jnp.bfloat16),
        "head_ffn_shift": gaussian(key_of[35], (D,), 0.5, 3.0, ((0, 32),)),
    }


EPS = 1e-12
NEG = -1e+30
HIGH = lax.Precision.HIGHEST

@jax.custom_vjp
def low(v):
    return lax.optimization_barrier(v.astype(jnp.bfloat16)).astype(jnp.float32)

@jax.custom_vjp
def low_back(v):
    return v

def low_keep(v):
    return (low(v), None)

def low_pass(kept, grad):
    return (grad,)

def back_keep(v):
    return (v, None)

def back_low(kept, grad):
    return (low(grad),)
low.defvjp(low_keep, low_pass)
low_back.defvjp(back_keep, back_low)

def both_low(value):
    return low_back(low(value))

def layer_norm(value, gain, shift):
    mean = lax.optimization_barrier(jnp.mean(value, axis=-1, keepdims=True))
    centred = value - mean
    spread = lax.optimization_barrier(jnp.mean(centred * centred, axis=-1, keepdims=True))
    return centred * lax.rsqrt(spread + EPS) * gain + shift

def product(left, right):
    return jnp.dot(left, right, preferred_element_type=jnp.float32, precision=HIGH)

def attention(query, key, value, valid):
    length_rows = query.shape[0]
    block = math.gcd(length_rows, 512)
    queries = query.reshape(length_rows // block, block, H, HD)
    keys = key.reshape(length_rows, H, HD)
    values = value.reshape(length_rows, H, HD)

    def one_block(query_block):
        score = low_back(jnp.einsum('bhe,khe->hbk', query_block, keys, precision=HIGH) * HD ** (-0.5))
        score = jnp.where(valid, score, NEG)
        top = lax.optimization_barrier(jnp.max(score, axis=-1, keepdims=True))
        weight = jnp.where(valid, jnp.exp(score - top), 0.0)
        chance = low(weight / lax.optimization_barrier(jnp.sum(weight, axis=-1, keepdims=True)))
        return jnp.einsum('hbk,khe->bhe', chance, values, precision=HIGH)
    result = lax.map(jax.checkpoint(one_block), queries)
    return result.reshape(length_rows, H * HD)

def layer(params, rows, valid):
    query_w, query_bias, key_w, value_w, value_bias, output_w, output_bias, attn_gain, attn_shift, expand_w, expand_bias, reduce_w, reduce_bias, ffn_gain, ffn_shift = params
    query = both_low(product(rows, query_w) + query_bias)
    key = both_low(product(rows, key_w))
    value = both_low(product(rows, value_w) + value_bias)
    attended = both_low(attention(query, key, value, valid))
    summed = rows + low_back(product(attended, output_w) + output_bias)
    hidden = layer_norm(summed, attn_gain, attn_shift)
    inner = low_back(product(low(hidden), expand_w) + expand_bias)
    active = low(jax.nn.gelu(inner, approximate=False))
    return layer_norm(hidden + low_back(product(active, reduce_w) + reduce_bias), ffn_gain, ffn_shift)

def reference(tokens, early, cot_backbone, cot_head, lengths, cls_pos, back_query, back_query_bias, back_key, back_value, back_value_bias, back_output, back_output_bias, back_attn_gain, back_attn_shift, back_expand, back_expand_bias, back_reduce, back_reduce_bias, back_ffn_gain, back_ffn_shift, head_query, head_query_bias, head_key, head_value, head_value_bias, head_output, head_output_bias, head_attn_gain, head_attn_shift, head_expand, head_expand_bias, head_reduce, head_reduce_bias, head_ffn_gain, head_ffn_shift):
    back_set = (back_query, back_query_bias, back_key, back_value, back_value_bias, back_output, back_output_bias, back_attn_gain, back_attn_shift, back_expand, back_expand_bias, back_reduce, back_reduce_bias, back_ffn_gain, back_ffn_shift)
    head_set = (head_query, head_query_bias, head_key, head_value, head_value_bias, head_output, head_output_bias, head_attn_gain, head_attn_shift, head_expand, head_expand_bias, head_reduce, head_reduce_bias, head_ffn_gain, head_ffn_shift)
    params = (tuple((entry.astype(jnp.float32) for entry in back_set)), tuple((entry.astype(jnp.float32) for entry in head_set)))
    tokens_full = tokens.astype(jnp.float32)
    early_full = early.astype(jnp.float32)

    def forward_all(params, tokens_full, early_full):

        def one(item):
            rows, early_rows, length, cls = item
            positions = jnp.arange(rows.shape[0])
            valid = positions < length
            backbone = low(layer(params[0], rows, valid))
            mixed = jnp.where((positions == cls)[:, None], backbone, early_rows)
            return (backbone, layer(params[1], mixed, valid))
        return lax.map(jax.checkpoint(one), (tokens_full, early_full, lengths, cls_pos))
    (backbone, head), pullback = jax.vjp(forward_all, params, tokens_full, early_full)
    valid_rows = (jnp.arange(SEQLEN)[None, :] < lengths[:, None])[:, :, None]
    grad_params, grad_tokens, grad_early = pullback((jnp.where(valid_rows, cot_backbone.astype(jnp.float32), 0.0), jnp.where(valid_rows, cot_head.astype(jnp.float32), 0.0)))
    first = grad_params[0]
    second = grad_params[1]
    return (backbone.astype(jnp.bfloat16), head.astype(jnp.bfloat16), grad_tokens.astype(jnp.bfloat16), grad_early.astype(jnp.bfloat16), first[0], first[1], first[2], first[3], first[4], first[5], first[6], first[7], first[8], first[9], first[10], first[11], first[12], first[13], first[14], second[0], second[1], second[2], second[3], second[4], second[5], second[6], second[7], second[8], second[9], second[10], second[11], second[12], second[13], second[14])
```

```python
from functools import partial
import math

import jax
import jax.numpy as jnp
from jax import lax
from jax.experimental import pallas as pl
from jax.experimental.pallas import tpu as pltpu
from jax.sharding import PartitionSpec as P

H = 12
HD = 64
EPS = 1e-12
NEG = -1e30
MIN_LEN = 1024
BF = jnp.bfloat16
F32 = jnp.float32
MESH = pl.DeviceIdType.MESH
VMEM_LIMIT = 60 * 1024 * 1024


def mm(left, right):
    return lax.dot_general(left, right, (((1,), (0,)), ((), ())), preferred_element_type=F32)


def mm_nt(left, right):
    return lax.dot_general(left, right, (((1,), (1,)), ((), ())), preferred_element_type=F32)


def mm_tn(left, right):
    return lax.dot_general(left, right, (((0,), (0,)), ((), ())), preferred_element_type=F32)


def whole(shape):
    return pl.BlockSpec(shape, lambda *_: (0,) * len(shape))


def params_of(semantics):
    return pltpu.CompilerParams(dimension_semantics=semantics, vmem_limit_bytes=VMEM_LIMIT)


def qkv_kernel(x_ref, w_ref, p_ref, q_ref, kv_ref):
    j = pl.program_id(0)
    out = mm(x_ref[...], w_ref[0])

    @pl.when(j == 0)
    def _():
        q_ref[...] = (out + p_ref[0:1, :]).astype(BF)

    @pl.when(j == 1)
    def _():
        kv_ref[0] = out.astype(BF)

    @pl.when(j == 2)
    def _():
        kv_ref[0] = (out + p_ref[1:2, :]).astype(BF)


def qkv(x, w4, params):
    n, d = x.shape
    return pl.pallas_call(
        qkv_kernel,
        name="qkv",
        grid=(3,),
        in_specs=[
            whole((n, d)),
            pl.BlockSpec((1, d, d), lambda j: (j, 0, 0)),
            whole(params.shape),
        ],
        out_specs=[
            whole((n, d)),
            pl.BlockSpec((1, n, d), lambda j: (jnp.maximum(j - 1, 0), 0, 0)),
        ],
        out_shape=[
            jax.ShapeDtypeStruct((n, d), BF),
            jax.ShapeDtypeStruct((2, n, d), BF),
        ],
        compiler_params=params_of(("arbitrary",)),
        cost_estimate=pl.CostEstimate(flops=6 * n * d * d, bytes_accessed=6 * d * d + 8 * n * d, transcendentals=0),
    )(x, w4, params)


def half_masks(n):
    lane = lax.broadcasted_iota(jnp.int32, (n, 2 * HD), 1)
    return lane < HD


def attend_kernel(pieces, masked, chunk, *refs):
    q_ref = refs[0]
    kv_refs = refs[1 : 1 + pieces]
    refs = refs[1 + pieces :]
    bias_ref = None
    if masked:
        bias_ref, refs = refs[0], refs[1:]
    att_ref, lse_ref = refs
    n = q_ref.shape[0]
    for start in range(0, n, chunk):
        rows = pl.ds(start, chunk)
        low = half_masks(chunk)
        q = q_ref[rows, :] * jnp.asarray(HD**-0.5, BF)
        outs = []
        logs = []
        for side in range(2):
            qm = jnp.where(low if side == 0 else ~low, q, jnp.zeros_like(q))
            scores = []
            for t in range(pieces):
                s = mm_nt(qm, kv_refs[t][0])
                if masked:
                    s = s + bias_ref[t]
                scores.append(s)
            top = scores[0].max(axis=-1, keepdims=True)
            for s in scores[1:]:
                top = jnp.maximum(top, s.max(axis=-1, keepdims=True))
            total = jnp.zeros((chunk, 1), F32)
            numer = jnp.zeros((chunk, 2 * HD), F32)
            for t in range(pieces):
                weight = jnp.exp(scores[t] - top)
                total = total + weight.sum(axis=-1, keepdims=True)
                numer = numer + mm(weight.astype(BF), kv_refs[t][1])
            outs.append(numer / total)
            logs.append(top + jnp.log(total))
        att_ref[rows, :] = jnp.where(low, outs[0], outs[1]).astype(BF)
        lse_ref[rows, :] = jnp.where(low, logs[0], logs[1])


def attend(q, kvs, biases):
    n, d = q.shape
    pieces = len(kvs)
    masked = biases is not None
    pair = 2 * HD
    col = pl.BlockSpec((n, pair), lambda j: (0, j))
    kv_spec = pl.BlockSpec((2, n, pair), lambda j: (0, 0, j))
    extra = (biases,) if masked else ()
    return pl.pallas_call(
        partial(attend_kernel, pieces, masked, min(n, 512)),
        name="attend",
        grid=(d // pair,),
        in_specs=[col] + [kv_spec] * pieces + [whole(b.shape) for b in extra],
        out_specs=[col, col],
        out_shape=[jax.ShapeDtypeStruct((n, d), BF), jax.ShapeDtypeStruct((n, d), F32)],
        compiler_params=params_of(("arbitrary",)),
        cost_estimate=pl.CostEstimate(
            flops=4 * n * n * pieces * d, bytes_accessed=(8 + 4 * pieces) * n * d, transcendentals=n * n * pieces * H
        ),
    )(q, *kvs, *extra)


def attend_back_kernel(pieces, masked, *refs):
    q_ref, do_ref, att_ref, lse_ref = refs[:4]
    kv_refs = refs[4 : 4 + pieces]
    refs = refs[4 + pieces :]
    bias_ref = None
    if masked:
        bias_ref, refs = refs[0], refs[1:]
    dq_ref = refs[0]
    dkv_refs = refs[1:]
    n = q_ref.shape[0]
    scale = HD**-0.5
    low = half_masks(n)
    q = q_ref[...] * jnp.asarray(scale, BF)
    do = do_ref[...]
    prod = do.astype(F32) * att_ref[...].astype(F32)
    dq = jnp.zeros((n, 2 * HD), F32)
    qms, doms, deltas, lses = [], [], [], []
    for side in range(2):
        mask = low if side == 0 else ~low
        qms.append(jnp.where(mask, q, jnp.zeros_like(q)))
        doms.append(jnp.where(mask, do, jnp.zeros_like(do)))
        deltas.append(jnp.sum(jnp.where(mask, prod, 0.0), axis=-1, keepdims=True))
        lses.append(lse_ref[:, side * HD : side * HD + 1])
    dqs = [jnp.zeros((n, 2 * HD), F32) for _ in range(2)]
    for t in range(pieces):
        k = kv_refs[t][0]
        v = kv_refs[t][1]
        dk = jnp.zeros((n, 2 * HD), F32)
        dv = jnp.zeros((n, 2 * HD), F32)
        for side in range(2):
            s = mm_nt(qms[side], k)
            if masked:
                s = s + bias_ref[t]
            p = jnp.exp(s - lses[side])
            dp = mm_nt(doms[side], v)
            ds = (p * (dp - deltas[side])).astype(BF)
            dv = dv + mm_tn(p.astype(BF), doms[side])
            dk = dk + mm_tn(ds, qms[side])
            dqs[side] = dqs[side] + mm(ds, k)
        dkv_refs[t][0] = dk.astype(BF)
        dkv_refs[t][1] = dv.astype(BF)
    dq_ref[...] = (jnp.where(low, dqs[0], dqs[1]) * scale).astype(BF)


def attend_back(q, do, att, lse, kvs, biases):
    n, d = q.shape
    pieces = len(kvs)
    masked = biases is not None
    pair = 2 * HD
    col = pl.BlockSpec((n, pair), lambda j: (0, j))
    kv_spec = pl.BlockSpec((2, n, pair), lambda j: (0, 0, j))
    extra = (biases,) if masked else ()
    out = pl.pallas_call(
        partial(attend_back_kernel, pieces, masked),
        name="attend_back",
        grid=(d // pair,),
        in_specs=[col] * 4 + [kv_spec] * pieces + [whole(b.shape) for b in extra],
        out_specs=[col] + [kv_spec] * pieces,
        out_shape=[jax.ShapeDtypeStruct((n, d), BF)] + [jax.ShapeDtypeStruct((2, n, d), BF)] * pieces,
        compiler_params=params_of(("arbitrary",)),
        cost_estimate=pl.CostEstimate(
            flops=10 * n * n * pieces * d, bytes_accessed=(12 + 8 * pieces) * n * d, transcendentals=n * n * pieces * H
        ),
    )(q, do, att, lse, *kvs, *extra)
    return out[0], out[1:]


def normed(value):
    mean = jnp.mean(value, axis=-1, keepdims=True)
    centred = value - mean
    spread = jnp.mean(centred * centred, axis=-1, keepdims=True)
    scale = lax.rsqrt(spread + EPS)
    return centred * scale, scale


def norm_back(grad, xhat, scale):
    mean_grad = jnp.mean(grad, axis=-1, keepdims=True)
    mean_dot = jnp.mean(grad * xhat, axis=-1, keepdims=True)
    return scale * (grad - mean_grad - xhat * mean_dot)


def gelu_pair(value):
    cdf = 0.5 + 0.5 * lax.erf(value * (0.5**0.5))
    pdf = jnp.exp(-0.5 * value * value) * ((2.0 * math.pi) ** -0.5)
    return value * cdf, cdf + value * pdf


def post_kernel(
    x_ref, att_ref, w_ref, e_ref, eb_ref, r_ref, p_ref,
    out_ref, xhat1_ref, scale1_ref, act_ref, slope_ref, xhat2_ref, scale2_ref,
    hidden_ref, low_ref, total_ref,
):
    j = pl.program_id(0)
    lanes = scale1_ref.shape

    @pl.when(j == 0)
    def _():
        summed = x_ref[...].astype(F32) + mm(att_ref[...], w_ref[0]) + p_ref[2:3, :]
        xhat, scale = normed(summed)
        xhat1_ref[...] = xhat
        scale1_ref[...] = jnp.broadcast_to(scale, lanes)
        hidden = xhat * p_ref[3:4, :] + p_ref[4:5, :]
        hidden_ref[...] = hidden
        low_ref[...] = hidden.astype(BF)
        total_ref[...] = jnp.zeros_like(total_ref)

    inner = mm(low_ref[...], e_ref[...]) + eb_ref[...]
    active, slope = gelu_pair(inner)
    active = active.astype(BF)
    act_ref[...] = active
    slope_ref[...] = slope.astype(BF)
    total_ref[...] += mm(active, r_ref[...])

    @pl.when(j == pl.num_programs(0) - 1)
    def _():
        pre = hidden_ref[...] + total_ref[...] + p_ref[5:6, :]
        xhat, scale = normed(pre)
        xhat2_ref[...] = xhat
        scale2_ref[...] = jnp.broadcast_to(scale, lanes)
        out_ref[...] = (xhat * p_ref[6:7, :] + p_ref[7:8, :]).astype(BF)


def post(x, att, w4, e, eb, r, params):
    n, d = x.shape
    ff = e.shape[1]
    fc = min(ff, 512)
    full = whole((n, d))
    thin = whole((n, 128))
    tall = pl.BlockSpec((n, fc), lambda j: (0, j))
    return pl.pallas_call(
        post_kernel,
        name="post",
        grid=(ff // fc,),
        in_specs=[
            full, full,
            pl.BlockSpec((1, d, d), lambda j: (3, 0, 0)),
            pl.BlockSpec((d, fc), lambda j: (0, j)),
            pl.BlockSpec((1, fc), lambda j: (0, j)),
            pl.BlockSpec((fc, d), lambda j: (j, 0)),
            whole(params.shape),
        ],
        out_specs=[full, full, thin, tall, tall, full, thin],
        out_shape=[
            jax.ShapeDtypeStruct((n, d), BF),
            jax.ShapeDtypeStruct((n, d), F32),
            jax.ShapeDtypeStruct((n, 128), F32),
            jax.ShapeDtypeStruct((n, ff), BF),
            jax.ShapeDtypeStruct((n, ff), BF),
            jax.ShapeDtypeStruct((n, d), F32),
            jax.ShapeDtypeStruct((n, 128), F32),
        ],
        scratch_shapes=[pltpu.VMEM((n, d), F32), pltpu.VMEM((n, d), BF), pltpu.VMEM((n, d), F32)],
        compiler_params=params_of(("arbitrary",)),
        cost_estimate=pl.CostEstimate(
            flops=2 * n * d * (d + 2 * ff), bytes_accessed=2 * d * (d + 2 * ff) + 4 * n * ff + 16 * n * d, transcendentals=2 * n * ff
        ),
    )(x, att, w4, e, eb, r, params)


def rows_sum(value):
    return jnp.sum(value, axis=0, keepdims=True)


def ffn_back_kernel(
    g_ref, xhat2_ref, scale2_ref, p_ref, act_ref, slope_ref, r_ref, e_ref, xhat1_ref, scale1_ref, att_ref, w_ref,
    gr_ref, ge_ref, geb_ref, dsum_ref, go_ref, datt_ref, small_ref,
    outer_ref, low_ref, total_ref,
):
    j = pl.program_id(0)

    @pl.when(j == 0)
    def _():
        g = g_ref[...].astype(F32)
        xhat = xhat2_ref[...]
        d_pre = norm_back(g * p_ref[6:7, :], xhat, scale2_ref[:, 0:1])
        outer = d_pre.astype(BF)
        outer_ref[...] = outer
        total_ref[...] = d_pre
        small_ref[0:1, :] = jnp.zeros_like(small_ref[0:1, :])
        small_ref[1:2, :] = jnp.zeros_like(small_ref[1:2, :])
        small_ref[5:6, :] = rows_sum(outer.astype(F32))
        small_ref[6:7, :] = rows_sum(g * xhat)
        small_ref[7:8, :] = rows_sum(g)
        low_ref[...] = (xhat1_ref[...] * p_ref[3:4, :] + p_ref[4:5, :]).astype(BF)

    outer = outer_ref[...]
    d_active = mm_nt(outer, r_ref[...])
    d_inner_full = d_active * slope_ref[...].astype(F32)
    d_inner = d_inner_full.astype(BF)
    gr_ref[...] = mm_tn(act_ref[...], outer).astype(BF)
    ge_ref[...] = mm_tn(low_ref[...], d_inner).astype(BF)
    geb_ref[...] = rows_sum(d_inner.astype(F32))
    total_ref[...] += mm_nt(d_inner, e_ref[...])

    @pl.when(j == pl.num_programs(0) - 1)
    def _():
        d_hidden = total_ref[...]
        xhat = xhat1_ref[...]
        d_summed = norm_back(d_hidden * p_ref[3:4, :], xhat, scale1_ref[:, 0:1])
        dsum_ref[...] = d_summed
        branch = d_summed.astype(BF)
        small_ref[2:3, :] = rows_sum(branch.astype(F32))
        small_ref[3:4, :] = rows_sum(d_hidden * xhat)
        small_ref[4:5, :] = rows_sum(d_hidden)
        go_ref[...] = mm_tn(att_ref[...], branch).astype(BF)
        datt_ref[...] = mm_nt(branch, w_ref[0]).astype(BF)


def ffn_back(g, saved, w4, e, r, params):
    x, att, xhat1, scale1, act, slope, xhat2, scale2 = saved
    n, d = x.shape
    ff = e.shape[1]
    fc = min(ff, 512)
    full = whole((n, d))
    thin = whole((n, 128))
    tall = pl.BlockSpec((n, fc), lambda j: (0, j))
    e_spec = pl.BlockSpec((d, fc), lambda j: (0, j))
    r_spec = pl.BlockSpec((fc, d), lambda j: (j, 0))
    return pl.pallas_call(
        ffn_back_kernel,
        name="ffn_back",
        grid=(ff // fc,),
        in_specs=[
            full, full, thin, whole(params.shape), tall, tall, r_spec, e_spec, full, thin, full,
            pl.BlockSpec((1, d, d), lambda j: (3, 0, 0)),
        ],
        out_specs=[
            r_spec, e_spec, pl.BlockSpec((1, fc), lambda j: (0, j)), full, whole((d, d)), full, whole((8, d)),
        ],
        out_shape=[
            jax.ShapeDtypeStruct((ff, d), BF),
            jax.ShapeDtypeStruct((d, ff), BF),
            jax.ShapeDtypeStruct((1, ff), F32),
            jax.ShapeDtypeStruct((n, d), F32),
            jax.ShapeDtypeStruct((d, d), BF),
            jax.ShapeDtypeStruct((n, d), BF),
            jax.ShapeDtypeStruct((8, d), F32),
        ],
        scratch_shapes=[pltpu.VMEM((n, d), BF), pltpu.VMEM((n, d), BF), pltpu.VMEM((n, d), F32)],
        compiler_params=params_of(("arbitrary",)),
        cost_estimate=pl.CostEstimate(
            flops=4 * n * d * (d + 2 * ff), bytes_accessed=4 * d * (d + 2 * ff) + 4 * n * ff + 24 * n * d, transcendentals=0
        ),
    )(g, xhat2, scale2, params, act, slope, r, e, xhat1, scale1, att, w4)


def input_back_kernel(others, x_ref, dq_ref, own_ref, *refs):
    other_refs = refs[:others]
    w_ref, dsum_ref, g3_ref, dx_ref, small_ref = refs[others:]
    j = pl.program_id(0)

    def step(grad, row):
        g3_ref[0] = mm_tn(x_ref[...], grad).astype(BF)
        if row is not None:
            small_ref[row : row + 1, :] = rows_sum(grad.astype(F32))
        return mm_nt(grad, w_ref[0])

    def joined(index):
        value = own_ref[index].astype(F32)
        for ref in other_refs:
            value = value + ref[index].astype(F32)
        return value.astype(BF)

    @pl.when(j == 0)
    def _():
        small_ref[...] = jnp.zeros_like(small_ref)
        dx_ref[...] = dsum_ref[...] + step(dq_ref[...], 0)

    @pl.when(j == 1)
    def _():
        dx_ref[...] += step(joined(0), None)

    @pl.when(j == 2)
    def _():
        dx_ref[...] += step(joined(1), 1)


def input_back(x, dq, own, others, w4, dsum):
    n, d = x.shape
    full = whole((n, d))
    return pl.pallas_call(
        partial(input_back_kernel, len(others)),
        name="input_back",
        grid=(3,),
        in_specs=[full, full, whole((2, n, d))]
        + [whole((2, n, d))] * len(others)
        + [pl.BlockSpec((1, d, d), lambda j: (j, 0, 0)), full],
        out_specs=[pl.BlockSpec((1, d, d), lambda j: (j, 0, 0)), full, whole((8, d))],
        out_shape=[
            jax.ShapeDtypeStruct((3, d, d), BF),
            jax.ShapeDtypeStruct((n, d), F32),
            jax.ShapeDtypeStruct((8, d), F32),
        ],
        compiler_params=params_of(("arbitrary",)),
        cost_estimate=pl.CostEstimate(flops=12 * n * d * d, bytes_accessed=12 * d * d + 16 * n * d, transcendentals=0),
    )(x, dq, own, *others, w4, dsum)


class Grid:
    def __init__(self, dp, seq):
        self.ny = max(seq // 2, 1)
        self.nc = seq // self.ny
        self.nx = self.ny if dp % self.ny == 0 else 1
        self.nz = dp // self.nx
        self.sizes = {"z": self.nz, "x": self.nx, "y": self.ny, "c": self.nc}

    def here(self):
        d = lax.axis_index("dp")
        s = lax.axis_index("seq")
        return {"z": d // self.nx, "x": lax.rem(d, self.nx), "y": s // self.nc, "c": lax.rem(s, self.nc)}

    def device(self, at):
        return (at["z"] * self.nx + at["x"], at["y"] * self.nc + at["c"])

    def shifted(self, me, axis, step):
        other = dict(me)
        other[axis] = lax.rem(me[axis] + step, self.sizes[axis])
        return other

    def shape(self):
        return (self.nz, self.nx, self.ny, self.nc)

    def peers(self):
        return [(axis, step) for axis in "zxyc" for step in range(1, self.sizes[axis])]

    def barrier(self, me):
        sem = pltpu.get_barrier_semaphore()
        for axis, step in self.peers():
            pl.semaphore_signal(
                sem, inc=1, device_id=self.device(self.shifted(me, axis, step)), device_id_type=MESH
            )
        pl.semaphore_wait(sem, len(self.peers()))


def picked(place, axes):
    return tuple(slice(None) if axis in axes else place[axis] for axis in "zxyc")


def cuts_of(shapes):
    pieces = []
    for number, shape in enumerate(shapes):
        columns = shape[-1]
        if columns % 256 or len(shape) == 2 and shape[0] % 8:
            pieces.append([(number, None, 0, columns)])
            continue
        step = 384 if columns % 384 == 0 else columns // 2
        leads = [None]
        if len(shape) == 3 and shape[0] > 1:
            middle = shape[0] // 2
            leads = [(0, middle), (middle, shape[0])]
        for lead in leads:
            for first in range(0, columns, 2 * step):
                pieces.append([(number, lead, first, step), (number, lead, first + step, step)])
    return pieces


def region(ref, shape, cut, index):
    _, lead, first, count = cut
    head = ()
    if len(shape) == 3:
        head = (slice(None) if lead is None else slice(*lead),)
    return ref.at[head + tuple(index) + (slice(None), slice(first, first + count))]


ORDERS = (("z", "x", "y", "c"), ("z", "y", "x", "c"))


def gather_kernel(grid, shapes, *refs):
    count = len(shapes)
    srcs, dsts = refs[:count], refs[count : 2 * count]
    send_sem, recv_sem, own_sem = refs[2 * count :]
    me = grid.here()
    grid.barrier(me)
    groups = cuts_of(shapes)
    number = [0]
    waits = []

    def send(src, dst, axis, step):
        k = number[0]
        number[0] += 1
        copy = pltpu.make_async_remote_copy(
            src_ref=src, dst_ref=dst, send_sem=send_sem.at[k], recv_sem=recv_sem.at[k],
            device_id=grid.device(grid.shifted(me, axis, step)), device_id_type=MESH,
        )
        copy.start()
        waits.append(copy)
        return copy

    own = []
    first = []
    for group in groups:
        copies = []
        for cut in group:
            shape = shapes[cut[0]]
            src = region(srcs[cut[0]], shape, cut, ())
            dst = region(dsts[cut[0]], shape, cut, picked(me, ""))
            copies.append([send(src, dst, "z", step) for step in range(1, grid.nz)])
        first.append(copies)
    for k in range(count):
        head = (slice(None),) if len(shapes[k]) == 3 else ()
        copy = pltpu.make_async_copy(srcs[k], dsts[k].at[head + picked(me, "")], own_sem.at[k])
        copy.start()
        own.append(copy)
    for copy in own:
        copy.wait()
    stages = {0: first}
    total = len(groups)
    depth = len(ORDERS[0])
    for turn in range(total + depth - 1):
        for stage in range(depth - 1, 0, -1):
            g = turn - (stage - 1)
            if not 0 <= g < total:
                continue
            copies = []
            for side, cut in enumerate(groups[g]):
                order = ORDERS[side % 2]
                for copy in stages[stage - 1][g][side]:
                    copy.wait_recv()
                block = region(dsts[cut[0]], shapes[cut[0]], cut, picked(me, order[:stage]))
                copies.append([send(block, block, order[stage], step) for step in range(1, grid.sizes[order[stage]])])
            stages.setdefault(stage, {})[g] = copies
        g = turn - (depth - 1)
        if 0 <= g < total:
            for copies in stages[depth - 1][g]:
                for copy in copies:
                    copy.wait_recv()
    for copy in waits:
        copy.wait_send()


def copies_in(grid, shapes):
    return sum(len(group) for group in cuts_of(shapes)) * len(grid.peers())


def gather(grid, arrays, name, collective_id):
    shapes = [a.shape for a in arrays]
    outs = [a.shape[:-2] + grid.shape() + a.shape[-2:] for a in arrays]
    count = copies_in(grid, shapes)
    got = pl.pallas_call(
        partial(gather_kernel, grid, shapes),
        name=name,
        in_specs=[pl.BlockSpec(memory_space=pltpu.VMEM)] * len(arrays),
        out_specs=[pl.BlockSpec(memory_space=pl.ANY)] * len(arrays),
        out_shape=[jax.ShapeDtypeStruct(s, a.dtype) for s, a in zip(outs, arrays)],
        scratch_shapes=[
            pltpu.SemaphoreType.DMA((count,)),
            pltpu.SemaphoreType.DMA((count,)),
            pltpu.SemaphoreType.DMA((len(arrays),)),
        ],
        compiler_params=pltpu.CompilerParams(
            collective_id=collective_id, has_side_effects=True, vmem_limit_bytes=VMEM_LIMIT
        ),
    )(*arrays)
    blocks = math.prod(grid.shape())
    return [o.reshape(a.shape[:-2] + (blocks * a.shape[-2], a.shape[-1])) for o, a in zip(got, arrays)]


BACK_ORDERS = (("c", "x", "y", "z"), ("c", "y", "x", "z"))


def left_axes(order, stage):
    return [axis for axis in "zxyc" if axis not in order[:stage]]


def scatter_kernel(grid, shapes, layouts, *refs):
    count = len(shapes)
    srcs, outs = refs[:count], refs[count : 2 * count]
    held = refs[2 * count : 2 * count + sum(len(stages) for stages in layouts)]
    send_sem, recv_sem, own_sem = refs[-3:]
    me = grid.here()
    grid.barrier(me)
    groups = cuts_of(shapes)
    number = [0]
    waits = []
    buffers = {}
    position = 0
    piece = 0
    for g, group in enumerate(groups):
        for side in range(len(group)):
            for stage in range(len(layouts[piece])):
                buffers[g, side, stage] = held[position]
                position += 1
            piece += 1

    def send(src, dst, axis, step):
        k = number[0]
        number[0] += 1
        copy = pltpu.make_async_remote_copy(
            src_ref=src, dst_ref=dst, send_sem=send_sem.at[k], recv_sem=recv_sem.at[k],
            device_id=grid.device(grid.shifted(me, axis, step)), device_id_type=MESH,
        )
        copy.start()
        waits.append(copy)
        return copy

    def part(cut, ref):
        return region(ref, shapes[cut[0]], cut, ())

    owns = {}
    flights = {}
    own_number = 0
    for g, group in enumerate(groups):
        for side, cut in enumerate(group):
            shape = shapes[cut[0]]
            order = BACK_ORDERS[side % 2]
            axis = order[0]
            buf = buffers[g, side, 0]
            mine = dict(me)
            copy = pltpu.make_async_copy(
                region(srcs[cut[0]], shape, cut, picked(mine, "zxy")), buf.at[0], own_sem.at[own_number]
            )
            copy.start()
            owns[g, side] = copy
            own_number += 1
            flights[g, side, 0] = [
                send(
                    region(srcs[cut[0]], shape, cut, picked(grid.shifted(me, axis, step), "zxy")),
                    buf.at[step], axis, step,
                )
                for step in range(1, grid.sizes[axis])
            ]
    depth = 4

    def lead_of(cut):
        return len(shapes[cut[0]]) == 3

    def add_into(buf, cut, stage, order):
        slots = buf.shape[0]
        lead = buf.shape[1] if lead_of(cut) else 1
        spread = buf.shape[2 if lead_of(cut) else 1 : -2]
        blocks = lead * math.prod(spread)
        flat = buf.shape[1:-2]

        def body(i, carry):
            index = []
            rest = i
            for size in reversed(flat):
                index.append(lax.rem(rest, size))
                rest = rest // size
            index = tuple(reversed(index))
            value = buf[(0,) + index].astype(F32)
            for slot in range(1, slots):
                value = value + buf[(slot,) + index].astype(F32)
            buf[(0,) + index] = value.astype(buf.dtype)
            return carry

        lax.fori_loop(0, blocks, body, 0)

    for turn in range(len(groups) + depth - 1):
        for stage in range(depth - 1, -1, -1):
            g = turn - stage
            if not 0 <= g < len(groups):
                continue
            for side, cut in enumerate(groups[g]):
                order = BACK_ORDERS[side % 2]
                buf = buffers[g, side, stage]
                for copy in flights[g, side, stage]:
                    copy.wait_recv()
                if stage == 0:
                    owns[g, side].wait()
                if stage == depth - 1:
                    out = part(cut, outs[cut[0]])
                    value = buffers[g, side, stage - 1]
                    rest = left_axes(order, stage)
                    head = (slice(None),) if lead_of(cut) else ()
                    total = value[(0,) + head + tuple(me[a] for a in rest)].astype(F32)
                    for slot in range(buf.shape[0]):
                        total = total + buf[slot].astype(F32)
                    out[...] = total
                    continue
                if stage == 0:
                    add_into(buf, cut, stage, order)
                    source = buf
                else:
                    source = buffers[g, side, stage - 1]
                    merge(source, buf, me, left_axes(order, stage), order[stage], lead_of(cut), grid)
                    source = buf
                rest = left_axes(order, stage + 1)
                axis = order[stage + 1]
                nxt = buffers[g, side, stage + 1]
                head = (slice(None),) if lead_of(cut) else ()
                flights[g, side, stage + 1] = []
                base = 0 if stage + 1 == depth - 1 else 1
                for step in range(1, grid.sizes[axis]):
                    there = grid.shifted(me, axis, step)
                    index = tuple(there[a] if a == axis else slice(None) for a in rest)
                    flights[g, side, stage + 1].append(
                        send(source.at[(0,) + head + index], nxt.at[step - 1 + base], axis, step)
                    )
    for copy in waits:
        copy.wait_send()


def merge(source, buf, me, axes, axis, lead, grid):
    flat = buf.shape[1:-2]
    blocks = math.prod(flat) if flat else 1
    where = axes.index(axis) + (1 if lead else 0)

    def body(i, carry):
        index = []
        rest = i
        for size in reversed(flat):
            index.append(lax.rem(rest, size))
            rest = rest // size
        index = tuple(reversed(index))
        wide = index[:where] + (me[axis],) + index[where:]
        value = source[(0,) + wide].astype(F32)
        for slot in range(1, buf.shape[0]):
            value = value + buf[(slot,) + index].astype(F32)
        buf[(0,) + index] = value.astype(buf.dtype)
        return carry

    lax.fori_loop(0, blocks, body, 0)


def scatter(grid, arrays, name, collective_id):
    blocks = math.prod(grid.shape())
    shapes = [a.shape[:-2] + (a.shape[-2] // blocks, a.shape[-1]) for a in arrays]
    views = [a.reshape(s[:-2] + grid.shape() + s[-2:]) for a, s in zip(arrays, shapes)]
    layouts = []
    scratch = []
    pieces = 0
    for group in cuts_of(shapes):
        for side, cut in enumerate(group):
            shape = shapes[cut[0]]
            order = BACK_ORDERS[side % 2]
            head = ()
            if len(shape) == 3:
                head = (shape[0] if cut[1] is None else cut[1][1] - cut[1][0],)
            stages = []
            for stage in range(4):
                rest = left_axes(order, stage + 1)
                slots = grid.sizes[order[stage]] - (1 if stage == 3 else 0)
                stages.append((slots,) + head + tuple(grid.sizes[a] for a in rest) + (shape[-2], cut[3]))
            layouts.append(stages)
            scratch += [pltpu.VMEM(s, arrays[cut[0]].dtype) for s in stages]
            pieces += 1
    count = copies_in(grid, shapes)
    return pl.pallas_call(
        partial(scatter_kernel, grid, shapes, layouts),
        name=name,
        in_specs=[pl.BlockSpec(memory_space=pl.ANY)] * len(arrays),
        out_specs=[pl.BlockSpec(memory_space=pltpu.VMEM)] * len(arrays),
        out_shape=[jax.ShapeDtypeStruct(s, F32) for s in shapes],
        scratch_shapes=scratch
        + [
            pltpu.SemaphoreType.DMA((count,)),
            pltpu.SemaphoreType.DMA((count,)),
            pltpu.SemaphoreType.DMA((pieces,)),
        ],
        compiler_params=pltpu.CompilerParams(
            collective_id=collective_id, has_side_effects=True, vmem_limit_bytes=VMEM_LIMIT
        ),
    )(*views)


ROWS = 8
ROW_AT = (1, 4, 6, 7, 8, 12, 13, 14)


def pack_small(layers):
    parts = []
    for params in layers:
        parts += [params[k] for k in ROW_AT] + [params[10]]
    flat = jnp.concatenate(parts)
    size = 1024 * -(-flat.shape[0] // 1024)
    return jnp.pad(flat, (0, size - flat.shape[0])).reshape(size // 128, 128)


def unpack_small(full, blocks, rows, layers):
    per = full.shape[0] // blocks * full.shape[1]
    flat = full.reshape(blocks, per)
    out = []
    width = (ROWS + 4) * rows
    for layer in range(layers):
        part = flat[:, layer * width : (layer + 1) * width].astype(F32)
        thin = part[:, : ROWS * rows].reshape(blocks, ROWS, rows).transpose(1, 0, 2).reshape(ROWS, blocks * rows)
        out.append((thin, part[:, ROWS * rows :].reshape(1, blocks * 4 * rows)))
    return out


def pack_grads(grads, blocks, rows):
    parts = []
    for thin, wide in grads:
        parts.append(thin.reshape(ROWS, blocks, rows).transpose(1, 0, 2).reshape(blocks, ROWS * rows))
        parts.append(wide.reshape(blocks, 4 * rows))
    flat = jnp.concatenate(parts, axis=1)
    size = 1024 * -(-flat.shape[1] // 1024)
    return jnp.pad(flat, ((0, 0), (0, size - flat.shape[1]))).reshape(blocks * (size // 128), 128)


def on_device(grid, tokens, early, cot_backbone, cot_head, lengths, cls_pos, *weights):
    layers = (weights[:15], weights[15:])
    members = lax.axis_size("seq")
    blocks = math.prod(grid.shape())
    seqs, rows, width = tokens.shape
    half = members // seqs
    spot = lax.axis_index("seq")
    mine = spot // half
    swap = [(i, (i + half) % members) for i in range(members)]
    far = lax.rem(spot + half, members)
    masked = rows * members > MIN_LEN

    def spread(value):
        kept = lax.dynamic_index_in_dim(value, mine, 0, keepdims=False)
        sent = lax.dynamic_index_in_dim(value, 1 - mine, 0, keepdims=False)
        return jnp.concatenate([kept, lax.ppermute(sent, "seq", swap)], axis=0)

    def collect(value):
        kept = value[:rows]
        got = lax.ppermute(value[rows:], "seq", swap)
        return jnp.where(mine == 0, jnp.stack([kept, got]), jnp.stack([got, kept]))

    def around(value, step):
        pairs = [(i, i // half * half + (i % half + step) % half) for i in range(members)]
        return lax.ppermute(value, "seq", pairs)

    length = lax.dynamic_index_in_dim(lengths, mine, 0, keepdims=False)
    cls = lax.dynamic_index_in_dim(cls_pos, mine, 0, keepdims=False)
    line = jnp.arange(rows, dtype=jnp.int32)
    positions = jnp.concatenate([spot * rows + line, far * rows + line])
    is_cls = (positions == cls)[:, None]
    valid = (positions < length)[:, None]
    biases = None
    if masked:
        steps = []
        for step in range(half):
            member = mine * half + lax.rem(lax.rem(spot, half) - step + half, half)
            other = lax.rem(member + half, members)
            place = jnp.concatenate([member * rows + line, other * rows + line])
            steps.append(jnp.where(place < length, 0.0, NEG)[None, :])
        biases = jnp.stack(steps)

    x_back = spread(tokens)
    x_early = spread(early)
    g_back = spread(cot_backbone)
    g_head = spread(cot_head)
    if masked:
        g_back = jnp.where(valid, g_back, jnp.zeros_like(g_back))
        g_head = jnp.where(valid, g_head, jnp.zeros_like(g_head))

    shard = layers[0][0].shape[0]
    stacked = [jnp.stack([p[0], p[2], p[3], p[5]]) for p in layers]
    small = pack_small(layers)
    w4_back, e_back, r_back, small_full = gather(
        grid, [stacked[0], layers[0][9], layers[0][11], small], "gather_back", 0
    )
    w4_head, e_head, r_head = gather(grid, [stacked[1], layers[1][9], layers[1][11]], "gather_head", 1)
    (p_back, eb_back), (p_head, eb_head) = unpack_small(small_full, blocks, shard, 2)

    def forward(x, w4, e, r, params, eb):
        q, kv = qkv(x, w4, params)
        kvs = [kv] + [around(kv, step) for step in range(1, half)]
        att, lse = attend(q, kvs, biases)
        out, xhat1, scale1, act, slope, xhat2, scale2 = post(x, att, w4, e, eb, r, params)
        return out, (q, kvs, lse, (x, att, xhat1, scale1, act, slope, xhat2, scale2))

    def backward(g, kept, w4, e, r, params):
        q, kvs, lse, saved = kept
        x, att = saved[:2]
        gr, ge, geb, dsum, go, datt, small_a = ffn_back(g, saved, w4, e, r, params)
        dq, dkvs = attend_back(q, datt, att, lse, kvs, biases)
        others = [around(dkvs[step], half - step) for step in range(1, half)]
        g3, dx, small_b = input_back(x, dq, dkvs[0], others, w4, dsum)
        return dx, (g3, go[None], ge, gr), (small_a + small_b, geb)

    back_low, back_kept = forward(x_back, w4_back, e_back, r_back, p_back, eb_back)
    head_in = jnp.where(is_cls, back_low, x_early)
    head_low, head_kept = forward(head_in, w4_head, e_head, r_head, p_head, eb_head)
    dx_head, big_head, small_head = backward(g_head, head_kept, w4_head, e_head, r_head, p_head)
    s3h, soh, seh, srh = scatter(grid, list(big_head), "scatter_head", 2)
    g_mixed = g_back.astype(F32) + jnp.where(is_cls, dx_head, 0.0)
    dx_back, big_back, small_back = backward(g_mixed, back_kept, w4_back, e_back, r_back, p_back)
    packed = pack_grads([small_back, small_head], blocks, shard)
    s3b, sob, seb, srb, small_sum = scatter(grid, list(big_back) + [packed], "scatter_back", 3)

    flat = small_sum.reshape(-1)

    def layer_grads(layer, s3, so, se, sr):
        base = layer * (ROWS + 4) * shard
        thin = [flat[base + k * shard : base + (k + 1) * shard] for k in range(ROWS)]
        wide = flat[base + ROWS * shard : base + (ROWS + 4) * shard]
        return (
            s3[0], thin[0], s3[1], s3[2], thin[1], so[0], thin[2], thin[3], thin[4],
            se, wide, sr, thin[5], thin[6], thin[7],
        )

    return (
        collect(back_low),
        collect(head_low),
        collect(dx_back.astype(BF)),
        collect(jnp.where(is_cls, 0.0, dx_head).astype(BF)),
    ) + layer_grads(0, s3b, sob, seb, srb) + layer_grads(1, s3h, soh, seh, srh)


def solution(mesh):
    rows = P("dp", "seq", None)
    wide = P(("dp", "seq"), None)
    thin = P(("dp", "seq"))
    layer = tuple(thin if k in (1, 4, 6, 7, 8, 10, 12, 13, 14) else wide for k in range(15))
    grid = Grid(mesh.shape["dp"], mesh.shape["seq"])
    return jax.shard_map(
        partial(on_device, grid),
        mesh=mesh,
        in_specs=(rows,) * 4 + (P("dp"),) * 2 + layer + layer,
        out_specs=(rows,) * 4 + layer + layer,
        check_vma=False,
    )
```

```python
from functools import partial
import math

import jax
import jax.numpy as jnp
from jax import lax
from jax.experimental import pallas as pl
from jax.experimental.pallas import tpu as pltpu
from jax.sharding import PartitionSpec as P

H = 12
HD = 64
EPS = 1e-12
NEG = -1e30
MIN_LEN = 1024
BF = jnp.bfloat16
F32 = jnp.float32
MESH = pl.DeviceIdType.MESH
VMEM_LIMIT = 60 * 1024 * 1024


def mm(left, right):
    return lax.dot_general(left, right, (((1,), (0,)), ((), ())), preferred_element_type=F32)


def mm_nt(left, right):
    return lax.dot_general(left, right, (((1,), (1,)), ((), ())), preferred_element_type=F32)


def mm_tn(left, right):
    return lax.dot_general(left, right, (((0,), (0,)), ((), ())), preferred_element_type=F32)


def whole(shape):
    return pl.BlockSpec(shape, lambda *_: (0,) * len(shape))


def params_of(semantics):
    return pltpu.CompilerParams(dimension_semantics=semantics, vmem_limit_bytes=VMEM_LIMIT)


def qkv_kernel(x_ref, w_ref, p_ref, q_ref, kv_ref):
    j = pl.program_id(0)
    out = mm(x_ref[...], w_ref[0])

    @pl.when(j == 0)
    def _():
        q_ref[...] = (out + p_ref[0:1, :]).astype(BF)

    @pl.when(j == 1)
    def _():
        kv_ref[0] = out.astype(BF)

    @pl.when(j == 2)
    def _():
        kv_ref[0] = (out + p_ref[1:2, :]).astype(BF)


def qkv(x, w4, params):
    n, d = x.shape
    return pl.pallas_call(
        qkv_kernel,
        name="qkv",
        grid=(3,),
        in_specs=[
            whole((n, d)),
            pl.BlockSpec((1, d, d), lambda j: (j, 0, 0)),
            whole(params.shape),
        ],
        out_specs=[
            whole((n, d)),
            pl.BlockSpec((1, n, d), lambda j: (jnp.maximum(j - 1, 0), 0, 0)),
        ],
        out_shape=[
            jax.ShapeDtypeStruct((n, d), BF),
            jax.ShapeDtypeStruct((2, n, d), BF),
        ],
        compiler_params=params_of(("arbitrary",)),
        cost_estimate=pl.CostEstimate(flops=6 * n * d * d, bytes_accessed=6 * d * d + 8 * n * d, transcendentals=0),
    )(x, w4, params)


def half_masks(n):
    lane = lax.broadcasted_iota(jnp.int32, (n, 2 * HD), 1)
    return lane < HD


def attend_pair(q, kvs, biases):
    n = q.shape[0]
    low = half_masks(n)
    q = q * jnp.asarray(HD**-0.5, BF)
    outs = []
    logs = []
    for side in range(2):
        qm = jnp.where(low if side == 0 else ~low, q, jnp.zeros_like(q))
        scores = []
        for t, (key, _) in enumerate(kvs):
            s = mm_nt(qm, key)
            if biases is not None:
                s = s + biases[t]
            scores.append(s)
        top = scores[0].max(axis=-1, keepdims=True)
        for s in scores[1:]:
            top = jnp.maximum(top, s.max(axis=-1, keepdims=True))
        total = jnp.zeros((n, 1), F32)
        numer = jnp.zeros((n, 2 * HD), F32)
        for t, (_, value) in enumerate(kvs):
            weight = jnp.exp(scores[t] - top)
            total = total + weight.sum(axis=-1, keepdims=True)
            numer = numer + mm(weight.astype(BF), value)
        outs.append(numer / total)
        logs.append(top + jnp.log(total))
    return jnp.where(low, outs[0], outs[1]).astype(BF), jnp.where(low, logs[0], logs[1])


def attend_kernel(pieces, masked, *refs):
    q_ref = refs[0]
    kv_refs = refs[1 : 1 + pieces]
    refs = refs[1 + pieces :]
    biases = None
    if masked:
        biases, refs = [refs[0][t] for t in range(pieces)], refs[1:]
    att_ref, lse_ref = refs
    att_ref[...], lse_ref[...] = attend_pair(q_ref[...], [(r[0], r[1]) for r in kv_refs], biases)


def attend(q, kvs, biases):
    n, d = q.shape
    pieces = len(kvs)
    masked = biases is not None
    pair = 2 * HD
    col = pl.BlockSpec((n, pair), lambda j: (0, j))
    kv_spec = pl.BlockSpec((2, n, pair), lambda j: (0, 0, j))
    extra = (biases,) if masked else ()
    return pl.pallas_call(
        partial(attend_kernel, pieces, masked),
        name="attend",
        grid=(d // pair,),
        in_specs=[col] + [kv_spec] * pieces + [whole(b.shape) for b in extra],
        out_specs=[col, col],
        out_shape=[jax.ShapeDtypeStruct((n, d), BF), jax.ShapeDtypeStruct((n, d), F32)],
        compiler_params=params_of(("arbitrary",)),
        cost_estimate=pl.CostEstimate(
            flops=4 * n * n * pieces * d, bytes_accessed=(8 + 4 * pieces) * n * d, transcendentals=n * n * pieces * H
        ),
    )(q, *kvs, *extra)


def attend_back_kernel(pieces, masked, *refs):
    q_ref, do_ref, att_ref, lse_ref = refs[:4]
    kv_refs = refs[4 : 4 + pieces]
    refs = refs[4 + pieces :]
    bias_ref = None
    if masked:
        bias_ref, refs = refs[0], refs[1:]
    dq_ref = refs[0]
    dkv_refs = refs[1:]
    n = q_ref.shape[0]
    scale = HD**-0.5
    low = half_masks(n)
    q = q_ref[...] * jnp.asarray(scale, BF)
    do = do_ref[...]
    prod = do.astype(F32) * att_ref[...].astype(F32)
    dq = jnp.zeros((n, 2 * HD), F32)
    qms, doms, deltas, lses = [], [], [], []
    for side in range(2):
        mask = low if side == 0 else ~low
        qms.append(jnp.where(mask, q, jnp.zeros_like(q)))
        doms.append(jnp.where(mask, do, jnp.zeros_like(do)))
        deltas.append(jnp.sum(jnp.where(mask, prod, 0.0), axis=-1, keepdims=True))
        lses.append(lse_ref[:, side * HD : side * HD + 1])
    dqs = [jnp.zeros((n, 2 * HD), F32) for _ in range(2)]
    for t in range(pieces):
        k = kv_refs[t][0]
        v = kv_refs[t][1]
        dk = jnp.zeros((n, 2 * HD), F32)
        dv = jnp.zeros((n, 2 * HD), F32)
        for side in range(2):
            s = mm_nt(qms[side], k)
            if masked:
                s = s + bias_ref[t]
            p = jnp.exp(s - lses[side])
            dp = mm_nt(doms[side], v)
            ds = (p * (dp - deltas[side])).astype(BF)
            dv = dv + mm_tn(p.astype(BF), doms[side])
            dk = dk + mm_tn(ds, qms[side])
            dqs[side] = dqs[side] + mm(ds, k)
        dkv_refs[t][0] = dk.astype(BF)
        dkv_refs[t][1] = dv.astype(BF)
    dq_ref[...] = (jnp.where(low, dqs[0], dqs[1]) * scale).astype(BF)


def attend_back(q, do, att, lse, kvs, biases):
    n, d = q.shape
    pieces = len(kvs)
    masked = biases is not None
    pair = 2 * HD
    col = pl.BlockSpec((n, pair), lambda j: (0, j))
    kv_spec = pl.BlockSpec((2, n, pair), lambda j: (0, 0, j))
    extra = (biases,) if masked else ()
    out = pl.pallas_call(
        partial(attend_back_kernel, pieces, masked),
        name="attend_back",
        grid=(d // pair,),
        in_specs=[col] * 4 + [kv_spec] * pieces + [whole(b.shape) for b in extra],
        out_specs=[col] + [kv_spec] * pieces,
        out_shape=[jax.ShapeDtypeStruct((n, d), BF)] + [jax.ShapeDtypeStruct((2, n, d), BF)] * pieces,
        compiler_params=params_of(("arbitrary",)),
        cost_estimate=pl.CostEstimate(
            flops=10 * n * n * pieces * d, bytes_accessed=(12 + 8 * pieces) * n * d, transcendentals=n * n * pieces * H
        ),
    )(q, do, att, lse, *kvs, *extra)
    return out[0], out[1:]


def normed(value):
    mean = jnp.mean(value, axis=-1, keepdims=True)
    centred = value - mean
    spread = jnp.mean(centred * centred, axis=-1, keepdims=True)
    scale = lax.rsqrt(spread + EPS)
    return centred * scale, scale


def norm_back(grad, xhat, scale):
    mean_grad = jnp.mean(grad, axis=-1, keepdims=True)
    mean_dot = jnp.mean(grad * xhat, axis=-1, keepdims=True)
    return scale * (grad - mean_grad - xhat * mean_dot)


def gelu_pair(value):
    cdf = 0.5 + 0.5 * lax.erf(value * (0.5**0.5))
    pdf = jnp.exp(-0.5 * value * value) * ((2.0 * math.pi) ** -0.5)
    return value * cdf, cdf + value * pdf


def post_kernel(
    x_ref, att_ref, w_ref, e_ref, eb_ref, r_ref, p_ref,
    out_ref, xhat1_ref, scale1_ref, act_ref, slope_ref, xhat2_ref, scale2_ref,
    hidden_ref, low_ref, total_ref,
):
    j = pl.program_id(0)
    lanes = scale1_ref.shape

    @pl.when(j == 0)
    def _():
        summed = x_ref[...].astype(F32) + mm(att_ref[...], w_ref[0]) + p_ref[2:3, :]
        xhat, scale = normed(summed)
        xhat1_ref[...] = xhat
        scale1_ref[...] = jnp.broadcast_to(scale, lanes)
        hidden = xhat * p_ref[3:4, :] + p_ref[4:5, :]
        hidden_ref[...] = hidden
        low_ref[...] = hidden.astype(BF)
        total_ref[...] = jnp.zeros_like(total_ref)

    inner = mm(low_ref[...], e_ref[...]) + eb_ref[...]
    active, slope = gelu_pair(inner)
    active = active.astype(BF)
    act_ref[...] = active
    slope_ref[...] = slope.astype(BF)
    total_ref[...] += mm(active, r_ref[...])

    @pl.when(j == pl.num_programs(0) - 1)
    def _():
        pre = hidden_ref[...] + total_ref[...] + p_ref[5:6, :]
        xhat, scale = normed(pre)
        xhat2_ref[...] = xhat
        scale2_ref[...] = jnp.broadcast_to(scale, lanes)
        out_ref[...] = (xhat * p_ref[6:7, :] + p_ref[7:8, :]).astype(BF)


def post(x, att, w4, e, eb, r, params):
    n, d = x.shape
    ff = e.shape[1]
    fc = min(ff, 512)
    full = whole((n, d))
    thin = whole((n, 128))
    tall = pl.BlockSpec((n, fc), lambda j: (0, j))
    return pl.pallas_call(
        post_kernel,
        name="post",
        grid=(ff // fc,),
        in_specs=[
            full, full,
            pl.BlockSpec((1, d, d), lambda j: (3, 0, 0)),
            pl.BlockSpec((d, fc), lambda j: (0, j)),
            pl.BlockSpec((1, fc), lambda j: (0, j)),
            pl.BlockSpec((fc, d), lambda j: (j, 0)),
            whole(params.shape),
        ],
        out_specs=[full, full, thin, tall, tall, full, thin],
        out_shape=[
            jax.ShapeDtypeStruct((n, d), BF),
            jax.ShapeDtypeStruct((n, d), F32),
            jax.ShapeDtypeStruct((n, 128), F32),
            jax.ShapeDtypeStruct((n, ff), BF),
            jax.ShapeDtypeStruct((n, ff), BF),
            jax.ShapeDtypeStruct((n, d), F32),
            jax.ShapeDtypeStruct((n, 128), F32),
        ],
        scratch_shapes=[pltpu.VMEM((n, d), F32), pltpu.VMEM((n, d), BF), pltpu.VMEM((n, d), F32)],
        compiler_params=params_of(("arbitrary",)),
        cost_estimate=pl.CostEstimate(
            flops=2 * n * d * (d + 2 * ff), bytes_accessed=2 * d * (d + 2 * ff) + 4 * n * ff + 16 * n * d, transcendentals=2 * n * ff
        ),
    )(x, att, w4, e, eb, r, params)


def rows_sum(value):
    return jnp.sum(value, axis=0, keepdims=True)


def ffn_back_kernel(
    g_ref, xhat2_ref, scale2_ref, p_ref, act_ref, slope_ref, r_ref, e_ref, xhat1_ref, scale1_ref, att_ref, w_ref,
    gr_ref, ge_ref, geb_ref, dsum_ref, go_ref, datt_ref, small_ref,
    outer_ref, low_ref, total_ref,
):
    j = pl.program_id(0)

    @pl.when(j == 0)
    def _():
        g = g_ref[...].astype(F32)
        xhat = xhat2_ref[...]
        d_pre = norm_back(g * p_ref[6:7, :], xhat, scale2_ref[:, 0:1])
        outer = d_pre.astype(BF)
        outer_ref[...] = outer
        total_ref[...] = d_pre
        small_ref[0:1, :] = jnp.zeros_like(small_ref[0:1, :])
        small_ref[1:2, :] = jnp.zeros_like(small_ref[1:2, :])
        small_ref[5:6, :] = rows_sum(outer.astype(F32))
        small_ref[6:7, :] = rows_sum(g * xhat)
        small_ref[7:8, :] = rows_sum(g)
        low_ref[...] = (xhat1_ref[...] * p_ref[3:4, :] + p_ref[4:5, :]).astype(BF)

    outer = outer_ref[...]
    d_active = mm_nt(outer, r_ref[...])
    d_inner_full = d_active * slope_ref[...].astype(F32)
    d_inner = d_inner_full.astype(BF)
    gr_ref[...] = mm_tn(act_ref[...], outer).astype(BF)
    ge_ref[...] = mm_tn(low_ref[...], d_inner).astype(BF)
    geb_ref[...] = rows_sum(d_inner.astype(F32))
    total_ref[...] += mm_nt(d_inner, e_ref[...])

    @pl.when(j == pl.num_programs(0) - 1)
    def _():
        d_hidden = total_ref[...]
        xhat = xhat1_ref[...]
        d_summed = norm_back(d_hidden * p_ref[3:4, :], xhat, scale1_ref[:, 0:1])
        dsum_ref[...] = d_summed
        branch = d_summed.astype(BF)
        small_ref[2:3, :] = rows_sum(branch.astype(F32))
        small_ref[3:4, :] = rows_sum(d_hidden * xhat)
        small_ref[4:5, :] = rows_sum(d_hidden)
        go_ref[...] = mm_tn(att_ref[...], branch).astype(BF)
        datt_ref[...] = mm_nt(branch, w_ref[0]).astype(BF)


def ffn_back(g, saved, w4, e, r, params):
    x, att, xhat1, scale1, act, slope, xhat2, scale2 = saved
    n, d = x.shape
    ff = e.shape[1]
    fc = min(ff, 512)
    full = whole((n, d))
    thin = whole((n, 128))
    tall = pl.BlockSpec((n, fc), lambda j: (0, j))
    e_spec = pl.BlockSpec((d, fc), lambda j: (0, j))
    r_spec = pl.BlockSpec((fc, d), lambda j: (j, 0))
    return pl.pallas_call(
        ffn_back_kernel,
        name="ffn_back",
        grid=(ff // fc,),
        in_specs=[
            full, full, thin, whole(params.shape), tall, tall, r_spec, e_spec, full, thin, full,
            pl.BlockSpec((1, d, d), lambda j: (3, 0, 0)),
        ],
        out_specs=[
            r_spec, e_spec, pl.BlockSpec((1, fc), lambda j: (0, j)), full, whole((d, d)), full, whole((8, d)),
        ],
        out_shape=[
            jax.ShapeDtypeStruct((ff, d), BF),
            jax.ShapeDtypeStruct((d, ff), BF),
            jax.ShapeDtypeStruct((1, ff), F32),
            jax.ShapeDtypeStruct((n, d), F32),
            jax.ShapeDtypeStruct((d, d), BF),
            jax.ShapeDtypeStruct((n, d), BF),
            jax.ShapeDtypeStruct((8, d), F32),
        ],
        scratch_shapes=[pltpu.VMEM((n, d), BF), pltpu.VMEM((n, d), BF), pltpu.VMEM((n, d), F32)],
        compiler_params=params_of(("arbitrary",)),
        cost_estimate=pl.CostEstimate(
            flops=4 * n * d * (d + 2 * ff), bytes_accessed=4 * d * (d + 2 * ff) + 4 * n * ff + 24 * n * d, transcendentals=0
        ),
    )(g, xhat2, scale2, params, act, slope, r, e, xhat1, scale1, att, w4)


def input_back_kernel(others, x_ref, dq_ref, own_ref, *refs):
    other_refs = refs[:others]
    w_ref, dsum_ref, g3_ref, dx_ref, small_ref = refs[others:]
    j = pl.program_id(0)

    def step(grad, row):
        g3_ref[0] = mm_tn(x_ref[...], grad).astype(BF)
        if row is not None:
            small_ref[row : row + 1, :] = rows_sum(grad.astype(F32))
        return mm_nt(grad, w_ref[0])

    def joined(index):
        value = own_ref[index].astype(F32)
        for ref in other_refs:
            value = value + ref[index].astype(F32)
        return value.astype(BF)

    @pl.when(j == 0)
    def _():
        small_ref[...] = jnp.zeros_like(small_ref)
        dx_ref[...] = dsum_ref[...] + step(dq_ref[...], 0)

    @pl.when(j == 1)
    def _():
        dx_ref[...] += step(joined(0), None)

    @pl.when(j == 2)
    def _():
        dx_ref[...] += step(joined(1), 1)


def input_back(x, dq, own, others, w4, dsum):
    n, d = x.shape
    full = whole((n, d))
    return pl.pallas_call(
        partial(input_back_kernel, len(others)),
        name="input_back",
        grid=(3,),
        in_specs=[full, full, whole((2, n, d))]
        + [whole((2, n, d))] * len(others)
        + [pl.BlockSpec((1, d, d), lambda j: (j, 0, 0)), full],
        out_specs=[pl.BlockSpec((1, d, d), lambda j: (j, 0, 0)), full, whole((8, d))],
        out_shape=[
            jax.ShapeDtypeStruct((3, d, d), BF),
            jax.ShapeDtypeStruct((n, d), F32),
            jax.ShapeDtypeStruct((8, d), F32),
        ],
        compiler_params=params_of(("arbitrary",)),
        cost_estimate=pl.CostEstimate(flops=12 * n * d * d, bytes_accessed=12 * d * d + 16 * n * d, transcendentals=0),
    )(x, dq, own, *others, w4, dsum)


class Grid:
    def __init__(self, dp, seq):
        self.ny = max(seq // 2, 1)
        self.nc = seq // self.ny
        self.nx = self.ny if dp % self.ny == 0 else 1
        self.nz = dp // self.nx
        self.sizes = {"z": self.nz, "x": self.nx, "y": self.ny, "c": self.nc}

    def here(self):
        d = lax.axis_index("dp")
        s = lax.axis_index("seq")
        return {"z": d // self.nx, "x": lax.rem(d, self.nx), "y": s // self.nc, "c": lax.rem(s, self.nc)}

    def device(self, at):
        return (at["z"] * self.nx + at["x"], at["y"] * self.nc + at["c"])

    def shifted(self, me, axis, step):
        other = dict(me)
        other[axis] = lax.rem(me[axis] + step, self.sizes[axis])
        return other

    def shape(self):
        return (self.nz, self.nx, self.ny, self.nc)

    def peers(self):
        return [(axis, step) for axis in "zxyc" for step in range(1, self.sizes[axis])]

    def barrier(self, me):
        sem = pltpu.get_barrier_semaphore()
        for axis, step in self.peers():
            pl.semaphore_signal(
                sem, inc=1, device_id=self.device(self.shifted(me, axis, step)), device_id_type=MESH
            )
        pl.semaphore_wait(sem, len(self.peers()))


def picked(place, axes):
    return tuple(slice(None) if axis in axes else place[axis] for axis in "zxyc")


def cuts_of(shapes):
    groups = []
    for number, shape in enumerate(shapes):
        rows, columns = shape[-2:]
        lead = shape[0] if len(shape) == 3 else None
        if columns % 256:
            groups.append([(number, None, (0, rows), (0, columns))])
            continue
        if lead is not None and lead % 2 == 0:
            pieces = [(number, (k, k + 1), (0, rows), (0, columns)) for k in range(lead)]
        elif lead == 3:
            left, right = (0, columns // 2), (columns // 2, columns // 2)
            pieces = [(number, (0, 1), (0, rows), (0, columns)), (number, (1, 2), (0, rows), (0, columns))]
            pieces += [(number, (2, 3), (0, rows), left), (number, (2, 3), (0, rows), right)]
        elif columns % 1024 == 0:
            pieces = [(number, None, (0, rows), (k * columns // 4, columns // 4)) for k in range(4)]
        elif rows % 32 == 0:
            pieces = [(number, None, (k * rows // 4, rows // 4), (0, columns)) for k in range(4)]
        elif columns % 256 == 0:
            pieces = [(number, None, (0, rows), (k * columns // 2, columns // 2)) for k in range(2)]
        else:
            groups.append([(number, None, (0, rows), (0, columns))])
            continue
        groups += [pieces[k : k + 2] for k in range(0, len(pieces), 2)]
    return groups


def region(ref, shape, cut, index):
    _, lead, rows, columns = cut
    head = ()
    if len(shape) == 3:
        head = (slice(None) if lead is None else slice(*lead),)
    return ref.at[head + tuple(index) + (slice(rows[0], sum(rows)), slice(columns[0], sum(columns)))]


ORDERS = (("z", "x", "y", "c"), ("z", "y", "x", "c"))


class Sender:
    def __init__(self, grid, me, send_sem, recv_sem):
        self.grid, self.me, self.send_sem, self.recv_sem = grid, me, send_sem, recv_sem
        self.started = []

    def send(self, src, dst, axis, step):
        return self.send_to(src, dst, self.grid.device(self.grid.shifted(self.me, axis, step)))

    def send_to(self, src, dst, device):
        k = len(self.started)
        copy = pltpu.make_async_remote_copy(
            src_ref=src, dst_ref=dst, send_sem=self.send_sem.at[k], recv_sem=self.recv_sem.at[k],
            device_id=device, device_id_type=MESH,
        )
        copy.start()
        self.started.append(copy)
        return copy

    def finish(self):
        for copy in self.started:
            copy.wait_send()


def gather_turns(sender, shapes, srcs, dsts, own_sem):
    grid, me = sender.grid, sender.me
    groups = cuts_of(shapes)
    own = []
    first = []
    for group in groups:
        copies = []
        for cut in group:
            shape = shapes[cut[0]]
            src = region(srcs[cut[0]], shape, cut, ())
            dst = region(dsts[cut[0]], shape, cut, picked(me, ""))
            copies.append([sender.send(src, dst, "z", step) for step in range(1, grid.nz)])
        first.append(copies)
    for k in range(len(shapes)):
        head = (slice(None),) if len(shapes[k]) == 3 else ()
        copy = pltpu.make_async_copy(srcs[k], dsts[k].at[head + picked(me, "")], own_sem.at[k])
        copy.start()
        own.append(copy)
    for copy in own:
        copy.wait()
    yield
    stages = {0: first}
    total = len(groups)
    depth = len(ORDERS[0])
    for turn in range(total + depth - 1):
        for stage in range(1, depth):
            g = turn - (stage - 1)
            if not 0 <= g < total:
                continue
            copies = []
            for side, cut in enumerate(groups[g]):
                order = ORDERS[side % 2]
                for copy in stages[stage - 1][g][side]:
                    copy.wait_recv()
                block = region(dsts[cut[0]], shapes[cut[0]], cut, picked(me, order[:stage]))
                copies.append(
                    [sender.send(block, block, order[stage], step) for step in range(1, grid.sizes[order[stage]])]
                )
            stages.setdefault(stage, {})[g] = copies
        g = turn - (depth - 1)
        if 0 <= g < total:
            for copies in stages[depth - 1][g]:
                for copy in copies:
                    copy.wait_recv()
        yield


def gather_kernel(grid, shapes, *refs):
    count = len(shapes)
    me = grid.here()
    grid.barrier(me)
    sender = Sender(grid, me, *refs[2 * count : 2 * count + 2])
    for _ in gather_turns(sender, shapes, refs[:count], refs[count : 2 * count], refs[-1]):
        pass
    sender.finish()


def copies_in(grid, shapes):
    return sum(len(group) for group in cuts_of(shapes)) * len(grid.peers())


def gather(grid, arrays, name, collective_id):
    shapes = [a.shape for a in arrays]
    outs = [a.shape[:-2] + grid.shape() + a.shape[-2:] for a in arrays]
    count = copies_in(grid, shapes)
    got = pl.pallas_call(
        partial(gather_kernel, grid, shapes),
        name=name,
        in_specs=[pl.BlockSpec(memory_space=pltpu.VMEM)] * len(arrays),
        out_specs=[pl.BlockSpec(memory_space=pl.ANY)] * len(arrays),
        out_shape=[jax.ShapeDtypeStruct(s, a.dtype) for s, a in zip(outs, arrays)],
        scratch_shapes=[
            pltpu.SemaphoreType.DMA((count,)),
            pltpu.SemaphoreType.DMA((count,)),
            pltpu.SemaphoreType.DMA((len(arrays),)),
        ],
        compiler_params=pltpu.CompilerParams(
            collective_id=collective_id, has_side_effects=True, vmem_limit_bytes=VMEM_LIMIT
        ),
    )(*arrays)
    blocks = math.prod(grid.shape())
    return [o.reshape(a.shape[:-2] + (blocks * a.shape[-2], a.shape[-1])) for o, a in zip(got, arrays)]


def spread_small(table_ref, thin_refs, wide_refs, rows, blocks):
    lines = table_ref.shape[-2]
    table = table_ref[...].reshape(blocks * lines, 128)

    def picker(per, width):
        column = lax.broadcasted_iota(jnp.int32, (128, width), 1)
        scale = -(-(1 << 20) // per)
        rest = column - lax.shift_right_logical(column * scale, 20) * per
        hot = (lax.broadcasted_iota(jnp.int32, (128, width), 0) == rest).astype(F32).astype(BF)
        place = lax.broadcasted_iota(jnp.int32, (blocks, lines, width), 2)
        owner = lax.broadcasted_iota(jnp.int32, (blocks, lines, width), 0)
        return hot, lax.shift_right_logical(place * scale, 20) == owner

    thin_width = thin_refs[0].shape[-1]
    hot, keep = picker(rows, thin_width)
    wide = mm(table, hot).reshape(blocks, lines, thin_width)
    vectors = jnp.sum(jnp.where(keep, wide, 0.0), axis=0)
    for layer, ref in enumerate(thin_refs):
        ref[...] = vectors[layer * 16 : layer * 16 + ROWS]
    step = 1024
    for first in range(0, wide_refs[0].shape[-1], step):
        scale = -(-(1 << 20) // (4 * rows))
        column = lax.broadcasted_iota(jnp.int32, (128, step), 1) + first
        rest = column - lax.shift_right_logical(column * scale, 20) * (4 * rows)
        hot = (lax.broadcasted_iota(jnp.int32, (128, step), 0) == rest).astype(F32).astype(BF)
        place = lax.broadcasted_iota(jnp.int32, (blocks, lines, step), 2) + first
        owner = lax.broadcasted_iota(jnp.int32, (blocks, lines, step), 0)
        full = mm(table, hot).reshape(blocks, lines, step)
        part = jnp.sum(jnp.where(lax.shift_right_logical(place * scale, 20) == owner, full, 0.0), axis=0)
        for layer, ref in enumerate(wide_refs):
            ref[:, first : first + step] = part[layer * 16 + 8 : layer * 16 + 9]


def front_kernel(grid, shapes, *refs):
    count = len(shapes)
    srcs, refs = refs[:count], refs[count:]
    x_ref, refs = refs[0], refs[1:]
    fulls, refs = refs[: count - 1], refs[count - 1 :]
    p1_ref, p2_ref, eb1_ref, eb2_ref, q_ref, kv_ref, far_ref, att_ref, lse_ref = refs[:9]
    out_ref, xhat1_ref, scale1_ref, act_ref, slope_ref, xhat2_ref, scale2_ref = refs[9:16]
    table_ref, w4_ref, r_ref, e_ref, hidden_ref, low_ref, total_ref = refs[16:23]
    send_sem, recv_sem, own_sem, load_sem = refs[23:]
    n, d = x_ref.shape
    ff = e_ref.shape[-1]
    me = grid.here()
    grid.barrier(me)
    sender = Sender(grid, me, send_sem, recv_sem)
    turns = gather_turns(sender, shapes, srcs, (table_ref,) + tuple(fulls), own_sem)
    left = [len(cuts_of(shapes)) + 4]

    def advance(steps=1):
        for _ in range(min(steps, left[0])):
            next(turns)
            left[0] -= 1

    def load(source, target, k):
        copy = pltpu.make_async_copy(source, target, load_sem.at[k])
        copy.start()
        return copy

    def joined(blocks):
        return blocks.astype(F32).reshape(-1, blocks.shape[-1]).astype(BF)

    advance(5)
    blocks = math.prod(grid.shape())
    spread_small(table_ref, (p1_ref, p2_ref), (eb1_ref, eb2_ref), shapes[1][-2], blocks)
    advance(2)
    load(fulls[0], w4_ref, 0).wait()
    x = x_ref[...]
    kv_ref[0] = mm(x, joined(w4_ref[1])).astype(BF)
    kv_ref[1] = (mm(x, joined(w4_ref[2])) + p1_ref[1:2, :]).astype(BF)
    swapped = sender.send(kv_ref, far_ref, "c", 1)
    q_ref[...] = (mm(x, joined(w4_ref[0])) + p1_ref[0:1, :]).astype(BF)
    advance(1)
    swapped.wait_recv()
    for pair in range(d // (2 * HD)):
        lanes = slice(pair * 2 * HD, (pair + 1) * 2 * HD)
        kvs = [(r[0, :, lanes], r[1, :, lanes]) for r in (kv_ref, far_ref)]
        att_ref[:, lanes], lse_ref[:, lanes] = attend_pair(q_ref[:, lanes], kvs, None)
        if pair % 2:
            advance(1)
        if pair == 1:
            loads = [load(fulls[1], r_ref, 1)]
    loads.append(load(fulls[2], e_ref, 2))
    summed = x.astype(F32) + mm(att_ref[...], joined(w4_ref[3])) + p1_ref[2:3, :]
    xhat, scale = normed(summed)
    xhat1_ref[...] = xhat
    scale1_ref[...] = jnp.broadcast_to(scale, scale1_ref.shape)
    hidden = xhat * p1_ref[3:4, :] + p1_ref[4:5, :]
    hidden_ref[...] = hidden
    low_ref[...] = hidden.astype(BF)
    for copy in loads:
        copy.wait()
    step = 512
    for first in range(0, ff, step):
        part = slice(first, first + step)
        active, slope = gelu_pair(mm(low_ref[...], joined(e_ref[..., part])) + eb1_ref[:, part])
        active = active.astype(BF)
        act_ref[:, part] = active
        slope_ref[:, part] = slope.astype(BF)
        more = mm(active, r_ref[...].reshape(ff, d)[part, :])
        total_ref[...] = more if first == 0 else total_ref[...] + more
        if first // step % 2:
            advance(1)
    pre = hidden_ref[...] + total_ref[...] + p1_ref[5:6, :]
    xhat, scale = normed(pre)
    xhat2_ref[...] = xhat
    scale2_ref[...] = jnp.broadcast_to(scale, scale2_ref.shape)
    out_ref[...] = (xhat * p1_ref[6:7, :] + p1_ref[7:8, :]).astype(BF)
    advance(left[0])
    sender.finish()


def front(grid, arrays, x, name, collective_id):
    shapes = [a.shape for a in arrays]
    n, d = x.shape
    ff = arrays[3].shape[1]
    count = copies_in(grid, shapes) + 1
    vmem = pl.BlockSpec(memory_space=pltpu.VMEM)
    hbm = pl.BlockSpec(memory_space=pl.ANY)
    fulls = [jax.ShapeDtypeStruct(a.shape[:-2] + grid.shape() + a.shape[-2:], BF) for a in arrays[1:]]
    local = [
        ((ROWS, d), F32), ((ROWS, d), F32), ((1, ff), F32), ((1, ff), F32),
        ((n, d), BF), ((2, n, d), BF), ((2, n, d), BF), ((n, d), BF), ((n, d), F32),
        ((n, d), BF), ((n, d), F32), ((n, 128), F32), ((n, ff), BF), ((n, ff), BF), ((n, d), F32), ((n, 128), F32),
    ]
    got = pl.pallas_call(
        partial(front_kernel, grid, shapes),
        name=name,
        in_specs=[vmem] * (len(arrays) + 1),
        out_specs=[hbm] * len(fulls) + [vmem] * len(local),
        out_shape=fulls + [jax.ShapeDtypeStruct(*s) for s in local],
        scratch_shapes=[
            pltpu.VMEM(grid.shape() + arrays[0].shape, BF),
            pltpu.VMEM(fulls[0].shape, BF),
            pltpu.VMEM(fulls[1].shape, BF),
            pltpu.VMEM(fulls[2].shape, BF),
            pltpu.VMEM((n, d), F32),
            pltpu.VMEM((n, d), BF),
            pltpu.VMEM((n, d), F32),
            pltpu.SemaphoreType.DMA((count,)),
            pltpu.SemaphoreType.DMA((count,)),
            pltpu.SemaphoreType.DMA((len(arrays),)),
            pltpu.SemaphoreType.DMA((3,)),
        ],
        compiler_params=pltpu.CompilerParams(
            collective_id=collective_id, has_side_effects=True, vmem_limit_bytes=VMEM_LIMIT
        ),
    )(*arrays, x)
    blocks = math.prod(grid.shape())
    weights = [
        o.reshape(a.shape[:-2] + (blocks * a.shape[-2], a.shape[-1])) for o, a in zip(got, arrays[1:])
    ]
    return weights, got[len(fulls) :]


BACK_ORDERS = (("c", "x", "y", "z"), ("c", "y", "x", "z"))


def left_axes(order, stage):
    return [axis for axis in "zxyc" if axis not in order[:stage]]


def scatter_kernel(grid, shapes, layouts, *refs):
    count = len(shapes)
    srcs, outs = refs[:count], refs[count : 2 * count]
    held = refs[2 * count : 2 * count + sum(len(stages) for stages in layouts)]
    send_sem, recv_sem, own_sem = refs[-3:]
    me = grid.here()
    grid.barrier(me)
    groups = cuts_of(shapes)
    number = [0]
    waits = []
    buffers = {}
    position = 0
    piece = 0
    for g, group in enumerate(groups):
        for side in range(len(group)):
            for stage in range(len(layouts[piece])):
                buffers[g, side, stage] = held[position]
                position += 1
            piece += 1

    def send(src, dst, axis, step):
        k = number[0]
        number[0] += 1
        copy = pltpu.make_async_remote_copy(
            src_ref=src, dst_ref=dst, send_sem=send_sem.at[k], recv_sem=recv_sem.at[k],
            device_id=grid.device(grid.shifted(me, axis, step)), device_id_type=MESH,
        )
        copy.start()
        waits.append(copy)
        return copy

    def part(cut, ref):
        return region(ref, shapes[cut[0]], cut, ())

    owns = {}
    flights = {}
    own_number = 0
    for g, group in enumerate(groups):
        for side, cut in enumerate(group):
            shape = shapes[cut[0]]
            order = BACK_ORDERS[side % 2]
            axis = order[0]
            buf = buffers[g, side, 0]
            mine = dict(me)
            copy = pltpu.make_async_copy(
                region(srcs[cut[0]], shape, cut, picked(mine, "zxy")), buf.at[0], own_sem.at[own_number]
            )
            copy.start()
            owns[g, side] = copy
            own_number += 1
            flights[g, side, 0] = [
                send(
                    region(srcs[cut[0]], shape, cut, picked(grid.shifted(me, axis, step), "zxy")),
                    buf.at[step], axis, step,
                )
                for step in range(1, grid.sizes[axis])
            ]
    depth = 4

    def lead_of(cut):
        return len(shapes[cut[0]]) == 3

    def add_into(buf, cut, stage, order):
        slots = buf.shape[0]
        lead = buf.shape[1] if lead_of(cut) else 1
        spread = buf.shape[2 if lead_of(cut) else 1 : -2]
        blocks = lead * math.prod(spread)
        flat = buf.shape[1:-2]

        def body(i, carry):
            index = []
            rest = i
            for size in reversed(flat):
                index.append(lax.rem(rest, size))
                rest = rest // size
            index = tuple(reversed(index))
            value = buf[(0,) + index].astype(F32)
            for slot in range(1, slots):
                value = value + buf[(slot,) + index].astype(F32)
            buf[(0,) + index] = value.astype(buf.dtype)
            return carry

        lax.fori_loop(0, blocks, body, 0)

    for turn in range(len(groups) + depth - 1):
        for stage in range(depth):
            g = turn - stage
            if not 0 <= g < len(groups):
                continue
            for side, cut in enumerate(groups[g]):
                order = BACK_ORDERS[side % 2]
                buf = buffers[g, side, stage]
                for copy in flights[g, side, stage]:
                    copy.wait_recv()
                if stage == 0:
                    owns[g, side].wait()
                if stage == depth - 1:
                    out = part(cut, outs[cut[0]])
                    value = buffers[g, side, stage - 1]
                    rest = left_axes(order, stage)
                    head = (slice(None),) if lead_of(cut) else ()
                    total = value[(0,) + head + tuple(me[a] for a in rest)].astype(F32)
                    for slot in range(buf.shape[0]):
                        total = total + buf[slot].astype(F32)
                    out[...] = total
                    continue
                if stage == 0:
                    add_into(buf, cut, stage, order)
                    source = buf
                else:
                    source = buffers[g, side, stage - 1]
                    merge(source, buf, me, left_axes(order, stage), order[stage], lead_of(cut), grid)
                    source = buf
                rest = left_axes(order, stage + 1)
                axis = order[stage + 1]
                nxt = buffers[g, side, stage + 1]
                head = (slice(None),) if lead_of(cut) else ()
                flights[g, side, stage + 1] = []
                base = 0 if stage + 1 == depth - 1 else 1
                for step in range(1, grid.sizes[axis]):
                    there = grid.shifted(me, axis, step)
                    index = tuple(there[a] if a == axis else slice(None) for a in rest)
                    flights[g, side, stage + 1].append(
                        send(source.at[(0,) + head + index], nxt.at[step - 1 + base], axis, step)
                    )
    for copy in waits:
        copy.wait_send()


def merge(source, buf, me, axes, axis, lead, grid):
    flat = buf.shape[1:-2]
    blocks = math.prod(flat) if flat else 1
    where = axes.index(axis) + (1 if lead else 0)

    def body(i, carry):
        index = []
        rest = i
        for size in reversed(flat):
            index.append(lax.rem(rest, size))
            rest = rest // size
        index = tuple(reversed(index))
        wide = index[:where] + (me[axis],) + index[where:]
        value = source[(0,) + wide].astype(F32)
        for slot in range(1, buf.shape[0]):
            value = value + buf[(slot,) + index].astype(F32)
        buf[(0,) + index] = value.astype(buf.dtype)
        return carry

    lax.fori_loop(0, blocks, body, 0)


def scatter(grid, arrays, name, collective_id):
    blocks = math.prod(grid.shape())
    shapes = [a.shape[:-2] + (a.shape[-2] // blocks, a.shape[-1]) for a in arrays]
    views = [a.reshape(s[:-2] + grid.shape() + s[-2:]) for a, s in zip(arrays, shapes)]
    layouts = []
    scratch = []
    pieces = 0
    for group in cuts_of(shapes):
        for side, cut in enumerate(group):
            shape = shapes[cut[0]]
            order = BACK_ORDERS[side % 2]
            head = ()
            if len(shape) == 3:
                head = (shape[0] if cut[1] is None else cut[1][1] - cut[1][0],)
            stages = []
            for stage in range(4):
                rest = left_axes(order, stage + 1)
                slots = grid.sizes[order[stage]] - (1 if stage == 3 else 0)
                stages.append((slots,) + head + tuple(grid.sizes[a] for a in rest) + (cut[2][1], cut[3][1]))
            layouts.append(stages)
            scratch += [pltpu.VMEM(s, arrays[cut[0]].dtype) for s in stages]
            pieces += 1
    count = copies_in(grid, shapes)
    return pl.pallas_call(
        partial(scatter_kernel, grid, shapes, layouts),
        name=name,
        in_specs=[pl.BlockSpec(memory_space=pl.ANY)] * len(arrays),
        out_specs=[pl.BlockSpec(memory_space=pltpu.VMEM)] * len(arrays),
        out_shape=[jax.ShapeDtypeStruct(s, F32) for s in shapes],
        scratch_shapes=scratch
        + [
            pltpu.SemaphoreType.DMA((count,)),
            pltpu.SemaphoreType.DMA((count,)),
            pltpu.SemaphoreType.DMA((pieces,)),
        ],
        compiler_params=pltpu.CompilerParams(
            collective_id=collective_id, has_side_effects=True, vmem_limit_bytes=VMEM_LIMIT
        ),
    )(*views)


ROWS = 8
ROW_AT = (1, 4, 6, 7, 8, 12, 13, 14)


def pack_small(layers):
    parts = []
    for params in layers:
        parts += [params[k] for k in ROW_AT] + [params[10]]
    flat = jnp.concatenate(parts)
    size = 1024 * -(-flat.shape[0] // 1024)
    return jnp.pad(flat, (0, size - flat.shape[0])).reshape(size // 128, 128)


def small_table(layers):
    lines = []
    for params in layers:
        for k in ROW_AT + (10,):
            lines.append(jnp.pad(params[k], (0, 128 - params[k].shape[0])))
        lines += [jnp.zeros((128,), BF)] * 7
    return jnp.stack(lines)


def unpack_small(full, blocks, rows, layers):
    per = full.shape[0] // blocks * full.shape[1]
    flat = full.reshape(blocks, per)
    out = []
    width = (ROWS + 4) * rows
    for layer in range(layers):
        part = flat[:, layer * width : (layer + 1) * width].astype(F32)
        thin = part[:, : ROWS * rows].reshape(blocks, ROWS, rows).transpose(1, 0, 2).reshape(ROWS, blocks * rows)
        out.append((thin, part[:, ROWS * rows :].reshape(1, blocks * 4 * rows)))
    return out


def pack_grads(grads, blocks, rows):
    parts = []
    for thin, wide in grads:
        parts.append(thin.reshape(ROWS, blocks, rows).transpose(1, 0, 2).reshape(blocks, ROWS * rows))
        parts.append(wide.reshape(blocks, 4 * rows))
    flat = jnp.concatenate(parts, axis=1)
    size = 1024 * -(-flat.shape[1] // 1024)
    return jnp.pad(flat, ((0, 0), (0, size - flat.shape[1]))).reshape(blocks * (size // 128), 128)


def on_device(grid, tokens, early, cot_backbone, cot_head, lengths, cls_pos, *weights):
    layers = (weights[:15], weights[15:])
    members = lax.axis_size("seq")
    blocks = math.prod(grid.shape())
    seqs, rows, width = tokens.shape
    half = members // seqs
    spot = lax.axis_index("seq")
    mine = spot // half
    swap = [(i, (i + half) % members) for i in range(members)]
    far = lax.rem(spot + half, members)
    masked = rows * members > MIN_LEN

    def spread(value):
        kept = lax.dynamic_index_in_dim(value, mine, 0, keepdims=False)
        sent = lax.dynamic_index_in_dim(value, 1 - mine, 0, keepdims=False)
        return jnp.concatenate([kept, lax.ppermute(sent, "seq", swap)], axis=0)

    def collect(value):
        kept = value[:rows]
        got = lax.ppermute(value[rows:], "seq", swap)
        return jnp.where(mine == 0, jnp.stack([kept, got]), jnp.stack([got, kept]))

    def around(value, step):
        pairs = [(i, i // half * half + (i % half + step) % half) for i in range(members)]
        return lax.ppermute(value, "seq", pairs)

    length = lax.dynamic_index_in_dim(lengths, mine, 0, keepdims=False)
    cls = lax.dynamic_index_in_dim(cls_pos, mine, 0, keepdims=False)
    line = jnp.arange(rows, dtype=jnp.int32)
    positions = jnp.concatenate([spot * rows + line, far * rows + line])
    is_cls = (positions == cls)[:, None]
    valid = (positions < length)[:, None]
    biases = None
    if masked:
        steps = []
        for step in range(half):
            member = mine * half + lax.rem(lax.rem(spot, half) - step + half, half)
            other = lax.rem(member + half, members)
            place = jnp.concatenate([member * rows + line, other * rows + line])
            steps.append(jnp.where(place < length, 0.0, NEG)[None, :])
        biases = jnp.stack(steps)

    x_back = spread(tokens)
    x_early = spread(early)
    g_back = spread(cot_backbone)
    g_head = spread(cot_head)
    if masked:
        g_back = jnp.where(valid, g_back, jnp.zeros_like(g_back))
        g_head = jnp.where(valid, g_head, jnp.zeros_like(g_head))

    shard = layers[0][0].shape[0]
    stacked = [jnp.stack([p[0], p[2], p[3], p[5]]) for p in layers]
    fused = shard % 8 == 0 and half == 2 and not masked
    if fused:
        travel = [small_table(layers)]
        for k in range(2):
            travel += [stacked[k], layers[k][11], layers[k][9]]
        (w4_back, r_back, e_back, w4_head, r_head, e_head), kept = front(grid, travel, x_back, "front", 0)
        p_back, p_head, eb_back, eb_head, q, kv, far_kv, att, lse, back_low = kept[:10]
        back_kept = (q, [kv, far_kv], lse, (x_back, att) + tuple(kept[10:]))
    else:
        small = pack_small(layers)
        w4_back, e_back, r_back, small_full = gather(
            grid, [stacked[0], layers[0][9], layers[0][11], small], "gather_back", 0
        )
        w4_head, e_head, r_head = gather(grid, [stacked[1], layers[1][9], layers[1][11]], "gather_head", 1)
        (p_back, eb_back), (p_head, eb_head) = unpack_small(small_full, blocks, shard, 2)

    def forward(x, w4, e, r, params, eb):
        q, kv = qkv(x, w4, params)
        kvs = [kv] + [around(kv, step) for step in range(1, half)]
        att, lse = attend(q, kvs, biases)
        out, xhat1, scale1, act, slope, xhat2, scale2 = post(x, att, w4, e, eb, r, params)
        return out, (q, kvs, lse, (x, att, xhat1, scale1, act, slope, xhat2, scale2))

    def backward(g, kept, w4, e, r, params):
        q, kvs, lse, saved = kept
        x, att = saved[:2]
        gr, ge, geb, dsum, go, datt, small_a = ffn_back(g, saved, w4, e, r, params)
        dq, dkvs = attend_back(q, datt, att, lse, kvs, biases)
        others = [around(dkvs[step], half - step) for step in range(1, half)]
        g3, dx, small_b = input_back(x, dq, dkvs[0], others, w4, dsum)
        return dx, (g3, go[None], ge, gr), (small_a + small_b, geb)

    if not fused:
        back_low, back_kept = forward(x_back, w4_back, e_back, r_back, p_back, eb_back)
    head_in = jnp.where(is_cls, back_low, x_early)
    head_low, head_kept = forward(head_in, w4_head, e_head, r_head, p_head, eb_head)
    dx_head, big_head, small_head = backward(g_head, head_kept, w4_head, e_head, r_head, p_head)
    s3h, soh, seh, srh = scatter(grid, list(big_head), "scatter_head", 2)
    g_mixed = g_back.astype(F32) + jnp.where(is_cls, dx_head, 0.0)
    dx_back, big_back, small_back = backward(g_mixed, back_kept, w4_back, e_back, r_back, p_back)
    packed = pack_grads([small_back, small_head], blocks, shard)
    s3b, sob, seb, srb, small_sum = scatter(grid, list(big_back) + [packed], "scatter_back", 3)

    flat = small_sum.reshape(-1)

    def layer_grads(layer, s3, so, se, sr):
        base = layer * (ROWS + 4) * shard
        thin = [flat[base + k * shard : base + (k + 1) * shard] for k in range(ROWS)]
        wide = flat[base + ROWS * shard : base + (ROWS + 4) * shard]
        return (
            s3[0], thin[0], s3[1], s3[2], thin[1], so[0], thin[2], thin[3], thin[4],
            se, wide, sr, thin[5], thin[6], thin[7],
        )

    return (
        collect(back_low),
        collect(head_low),
        collect(dx_back.astype(BF)),
        collect(jnp.where(is_cls, 0.0, dx_head).astype(BF)),
    ) + layer_grads(0, s3b, sob, seb, srb) + layer_grads(1, s3h, soh, seh, srh)


def solution(mesh):
    rows = P("dp", "seq", None)
    wide = P(("dp", "seq"), None)
    thin = P(("dp", "seq"))
    layer = tuple(thin if k in (1, 4, 6, 7, 8, 10, 12, 13, 14) else wide for k in range(15))
    grid = Grid(mesh.shape["dp"], mesh.shape["seq"])
    return jax.shard_map(
        partial(on_device, grid),
        mesh=mesh,
        in_specs=(rows,) * 4 + (P("dp"),) * 2 + layer + layer,
        out_specs=(rows,) * 4 + layer + layer,
        check_vma=False,
    )
```

```python
from functools import partial
import math

import jax
import jax.numpy as jnp
from jax import lax
from jax.experimental import pallas as pl
from jax.experimental.pallas import tpu as pltpu
from jax.sharding import PartitionSpec as P

H = 12
HD = 64
EPS = 1e-12
NEG = -1e30
MIN_LEN = 1024
BF = jnp.bfloat16
F32 = jnp.float32
MESH = pl.DeviceIdType.MESH
VMEM_LIMIT = 60 * 1024 * 1024


def mm(left, right):
    return lax.dot_general(left, right, (((1,), (0,)), ((), ())), preferred_element_type=F32)


def mm_nt(left, right):
    return lax.dot_general(left, right, (((1,), (1,)), ((), ())), preferred_element_type=F32)


def mm_tn(left, right):
    return lax.dot_general(left, right, (((0,), (0,)), ((), ())), preferred_element_type=F32)


def whole(shape):
    return pl.BlockSpec(shape, lambda *_: (0,) * len(shape))


def params_of(semantics):
    return pltpu.CompilerParams(dimension_semantics=semantics, vmem_limit_bytes=VMEM_LIMIT)


def qkv_kernel(x_ref, w_ref, p_ref, q_ref, kv_ref):
    j = pl.program_id(0)
    out = mm(x_ref[...], w_ref[0])

    @pl.when(j == 0)
    def _():
        q_ref[...] = (out + p_ref[0:1, :]).astype(BF)

    @pl.when(j == 1)
    def _():
        kv_ref[0] = out.astype(BF)

    @pl.when(j == 2)
    def _():
        kv_ref[0] = (out + p_ref[1:2, :]).astype(BF)


def qkv(x, w4, params):
    n, d = x.shape
    return pl.pallas_call(
        qkv_kernel,
        name="qkv",
        grid=(3,),
        in_specs=[
            whole((n, d)),
            pl.BlockSpec((1, d, d), lambda j: (j, 0, 0)),
            whole(params.shape),
        ],
        out_specs=[
            whole((n, d)),
            pl.BlockSpec((1, n, d), lambda j: (jnp.maximum(j - 1, 0), 0, 0)),
        ],
        out_shape=[
            jax.ShapeDtypeStruct((n, d), BF),
            jax.ShapeDtypeStruct((2, n, d), BF),
        ],
        compiler_params=params_of(("arbitrary",)),
        cost_estimate=pl.CostEstimate(flops=6 * n * d * d, bytes_accessed=6 * d * d + 8 * n * d, transcendentals=0),
    )(x, w4, params)


def half_masks(n):
    lane = lax.broadcasted_iota(jnp.int32, (n, 2 * HD), 1)
    return lane < HD


def attend_pair(q, kvs, biases):
    n = q.shape[0]
    low = half_masks(n)
    q = q * jnp.asarray(HD**-0.5, BF)
    outs = []
    logs = []
    for side in range(2):
        qm = jnp.where(low if side == 0 else ~low, q, jnp.zeros_like(q))
        scores = []
        for t, (key, _) in enumerate(kvs):
            s = mm_nt(qm, key)
            if biases is not None:
                s = s + biases[t]
            scores.append(s)
        top = scores[0].max(axis=-1, keepdims=True)
        for s in scores[1:]:
            top = jnp.maximum(top, s.max(axis=-1, keepdims=True))
        total = jnp.zeros((n, 1), F32)
        numer = jnp.zeros((n, 2 * HD), F32)
        for t, (_, value) in enumerate(kvs):
            weight = jnp.exp(scores[t] - top)
            total = total + weight.sum(axis=-1, keepdims=True)
            numer = numer + mm(weight.astype(BF), value)
        outs.append(numer / total)
        logs.append(top + jnp.log(total))
    return jnp.where(low, outs[0], outs[1]).astype(BF), jnp.where(low, logs[0], logs[1])


def attend_kernel(pieces, masked, *refs):
    q_ref = refs[0]
    kv_refs = refs[1 : 1 + pieces]
    refs = refs[1 + pieces :]
    biases = None
    if masked:
        biases, refs = [refs[0][t] for t in range(pieces)], refs[1:]
    att_ref, lse_ref = refs
    att_ref[...], lse_ref[...] = attend_pair(q_ref[...], [(r[0], r[1]) for r in kv_refs], biases)


def attend(q, kvs, biases):
    n, d = q.shape
    pieces = len(kvs)
    masked = biases is not None
    pair = 2 * HD
    col = pl.BlockSpec((n, pair), lambda j: (0, j))
    kv_spec = pl.BlockSpec((2, n, pair), lambda j: (0, 0, j))
    extra = (biases,) if masked else ()
    return pl.pallas_call(
        partial(attend_kernel, pieces, masked),
        name="attend",
        grid=(d // pair,),
        in_specs=[col] + [kv_spec] * pieces + [whole(b.shape) for b in extra],
        out_specs=[col, col],
        out_shape=[jax.ShapeDtypeStruct((n, d), BF), jax.ShapeDtypeStruct((n, d), F32)],
        compiler_params=params_of(("arbitrary",)),
        cost_estimate=pl.CostEstimate(
            flops=4 * n * n * pieces * d, bytes_accessed=(8 + 4 * pieces) * n * d, transcendentals=n * n * pieces * H
        ),
    )(q, *kvs, *extra)


def attend_back_kernel(pieces, masked, *refs):
    q_ref, do_ref, att_ref, lse_ref = refs[:4]
    kv_refs = refs[4 : 4 + pieces]
    refs = refs[4 + pieces :]
    bias_ref = None
    if masked:
        bias_ref, refs = refs[0], refs[1:]
    dq_ref = refs[0]
    dkv_refs = refs[1:]
    n = q_ref.shape[0]
    scale = HD**-0.5
    low = half_masks(n)
    q = q_ref[...] * jnp.asarray(scale, BF)
    do = do_ref[...]
    prod = do.astype(F32) * att_ref[...].astype(F32)
    dq = jnp.zeros((n, 2 * HD), F32)
    qms, doms, deltas, lses = [], [], [], []
    for side in range(2):
        mask = low if side == 0 else ~low
        qms.append(jnp.where(mask, q, jnp.zeros_like(q)))
        doms.append(jnp.where(mask, do, jnp.zeros_like(do)))
        deltas.append(jnp.sum(jnp.where(mask, prod, 0.0), axis=-1, keepdims=True))
        lses.append(lse_ref[:, side * HD : side * HD + 1])
    dqs = [jnp.zeros((n, 2 * HD), F32) for _ in range(2)]
    for t in range(pieces):
        k = kv_refs[t][0]
        v = kv_refs[t][1]
        dk = jnp.zeros((n, 2 * HD), F32)
        dv = jnp.zeros((n, 2 * HD), F32)
        for side in range(2):
            s = mm_nt(qms[side], k)
            if masked:
                s = s + bias_ref[t]
            p = jnp.exp(s - lses[side])
            dp = mm_nt(doms[side], v)
            ds = (p * (dp - deltas[side])).astype(BF)
            dv = dv + mm_tn(p.astype(BF), doms[side])
            dk = dk + mm_tn(ds, qms[side])
            dqs[side] = dqs[side] + mm(ds, k)
        dkv_refs[t][0] = dk.astype(BF)
        dkv_refs[t][1] = dv.astype(BF)
    dq_ref[...] = (jnp.where(low, dqs[0], dqs[1]) * scale).astype(BF)


def attend_back(q, do, att, lse, kvs, biases, ride=None):
    n, d = q.shape
    pieces = len(kvs)
    masked = biases is not None
    pair = 2 * HD
    col = pl.BlockSpec((n, pair), lambda j: (0, j))
    kv_spec = pl.BlockSpec((2, n, pair), lambda j: (0, 0, j))
    extra = (biases,) if masked else ()
    out, sums = stepped(
        partial(attend_back_kernel, pieces, masked),
        ride,
        "attend_back",
        d // pair,
        (q, do, att, lse, *kvs, *extra),
        [col] * 4 + [kv_spec] * pieces + [whole(b.shape) for b in extra],
        [col] + [kv_spec] * pieces,
        [jax.ShapeDtypeStruct((n, d), BF)] + [jax.ShapeDtypeStruct((2, n, d), BF)] * pieces,
        [],
        pl.CostEstimate(
            flops=10 * n * n * pieces * d, bytes_accessed=(12 + 8 * pieces) * n * d, transcendentals=n * n * pieces * H
        ),
    )
    return out[0], out[1:], sums


def normed(value):
    mean = jnp.mean(value, axis=-1, keepdims=True)
    centred = value - mean
    spread = jnp.mean(centred * centred, axis=-1, keepdims=True)
    scale = lax.rsqrt(spread + EPS)
    return centred * scale, scale


def norm_back(grad, xhat, scale):
    mean_grad = jnp.mean(grad, axis=-1, keepdims=True)
    mean_dot = jnp.mean(grad * xhat, axis=-1, keepdims=True)
    return scale * (grad - mean_grad - xhat * mean_dot)


def gelu_pair(value):
    cdf = 0.5 + 0.5 * lax.erf(value * (0.5**0.5))
    pdf = jnp.exp(-0.5 * value * value) * ((2.0 * math.pi) ** -0.5)
    return value * cdf, cdf + value * pdf


def post_kernel(
    x_ref, att_ref, w_ref, e_ref, eb_ref, r_ref, p_ref,
    out_ref, xhat1_ref, scale1_ref, act_ref, slope_ref, xhat2_ref, scale2_ref,
    hidden_ref, low_ref, total_ref,
):
    j = pl.program_id(0)
    lanes = scale1_ref.shape

    @pl.when(j == 0)
    def _():
        summed = x_ref[...].astype(F32) + mm(att_ref[...], w_ref[0]) + p_ref[2:3, :]
        xhat, scale = normed(summed)
        xhat1_ref[...] = xhat
        scale1_ref[...] = jnp.broadcast_to(scale, lanes)
        hidden = xhat * p_ref[3:4, :] + p_ref[4:5, :]
        hidden_ref[...] = hidden
        low_ref[...] = hidden.astype(BF)
        total_ref[...] = jnp.zeros_like(total_ref)

    inner = mm(low_ref[...], e_ref[...]) + eb_ref[...]
    active, slope = gelu_pair(inner)
    active = active.astype(BF)
    act_ref[...] = active
    slope_ref[...] = slope.astype(BF)
    total_ref[...] += mm(active, r_ref[...])

    @pl.when(j == pl.num_programs(0) - 1)
    def _():
        pre = hidden_ref[...] + total_ref[...] + p_ref[5:6, :]
        xhat, scale = normed(pre)
        xhat2_ref[...] = xhat
        scale2_ref[...] = jnp.broadcast_to(scale, lanes)
        out_ref[...] = (xhat * p_ref[6:7, :] + p_ref[7:8, :]).astype(BF)


def post(x, att, w4, e, eb, r, params):
    n, d = x.shape
    ff = e.shape[1]
    fc = min(ff, 512)
    full = whole((n, d))
    thin = whole((n, 128))
    tall = pl.BlockSpec((n, fc), lambda j: (0, j))
    return pl.pallas_call(
        post_kernel,
        name="post",
        grid=(ff // fc,),
        in_specs=[
            full, full,
            pl.BlockSpec((1, d, d), lambda j: (3, 0, 0)),
            pl.BlockSpec((d, fc), lambda j: (0, j)),
            pl.BlockSpec((1, fc), lambda j: (0, j)),
            pl.BlockSpec((fc, d), lambda j: (j, 0)),
            whole(params.shape),
        ],
        out_specs=[full, full, thin, tall, tall, full, thin],
        out_shape=[
            jax.ShapeDtypeStruct((n, d), BF),
            jax.ShapeDtypeStruct((n, d), F32),
            jax.ShapeDtypeStruct((n, 128), F32),
            jax.ShapeDtypeStruct((n, ff), BF),
            jax.ShapeDtypeStruct((n, ff), BF),
            jax.ShapeDtypeStruct((n, d), F32),
            jax.ShapeDtypeStruct((n, 128), F32),
        ],
        scratch_shapes=[pltpu.VMEM((n, d), F32), pltpu.VMEM((n, d), BF), pltpu.VMEM((n, d), F32)],
        compiler_params=params_of(("arbitrary",)),
        cost_estimate=pl.CostEstimate(
            flops=2 * n * d * (d + 2 * ff), bytes_accessed=2 * d * (d + 2 * ff) + 4 * n * ff + 16 * n * d, transcendentals=2 * n * ff
        ),
    )(x, att, w4, e, eb, r, params)


def rows_sum(value):
    return jnp.sum(value, axis=0, keepdims=True)


def ffn_back_kernel(
    g_ref, xhat2_ref, scale2_ref, p_ref, act_ref, slope_ref, r_ref, e_ref, xhat1_ref, scale1_ref, att_ref, w_ref,
    gr_ref, ge_ref, geb_ref, dsum_ref, go_ref, datt_ref, small_ref,
    outer_ref, low_ref, total_ref,
):
    j = pl.program_id(0)

    @pl.when(j == 0)
    def _():
        g = g_ref[...].astype(F32)
        xhat = xhat2_ref[...]
        d_pre = norm_back(g * p_ref[6:7, :], xhat, scale2_ref[:, 0:1])
        outer = d_pre.astype(BF)
        outer_ref[...] = outer
        total_ref[...] = d_pre
        small_ref[0:1, :] = jnp.zeros_like(small_ref[0:1, :])
        small_ref[1:2, :] = jnp.zeros_like(small_ref[1:2, :])
        small_ref[5:6, :] = rows_sum(outer.astype(F32))
        small_ref[6:7, :] = rows_sum(g * xhat)
        small_ref[7:8, :] = rows_sum(g)
        low_ref[...] = (xhat1_ref[...] * p_ref[3:4, :] + p_ref[4:5, :]).astype(BF)

    outer = outer_ref[...]
    d_active = mm_nt(outer, r_ref[...])
    d_inner_full = d_active * slope_ref[...].astype(F32)
    d_inner = d_inner_full.astype(BF)
    gr_ref[...] = mm_tn(act_ref[...], outer).astype(BF)
    ge_ref[...] = mm_tn(low_ref[...], d_inner).astype(BF)
    geb_ref[...] = rows_sum(d_inner.astype(F32))
    total_ref[...] += mm_nt(d_inner, e_ref[...])

    @pl.when(j == pl.num_programs(0) - 1)
    def _():
        d_hidden = total_ref[...]
        xhat = xhat1_ref[...]
        d_summed = norm_back(d_hidden * p_ref[3:4, :], xhat, scale1_ref[:, 0:1])
        dsum_ref[...] = d_summed
        branch = d_summed.astype(BF)
        small_ref[2:3, :] = rows_sum(branch.astype(F32))
        small_ref[3:4, :] = rows_sum(d_hidden * xhat)
        small_ref[4:5, :] = rows_sum(d_hidden)
        go_ref[...] = mm_tn(att_ref[...], branch).astype(BF)
        datt_ref[...] = mm_nt(branch, w_ref[0]).astype(BF)


def ffn_back(g, saved, w4, e, r, params, ride=None):
    x, att, xhat1, scale1, act, slope, xhat2, scale2 = saved
    n, d = x.shape
    ff = e.shape[1]
    fc = min(ff, 512)
    full = whole((n, d))
    thin = whole((n, 128))
    tall = pl.BlockSpec((n, fc), lambda j: (0, j))
    e_spec = pl.BlockSpec((d, fc), lambda j: (0, j))
    r_spec = pl.BlockSpec((fc, d), lambda j: (j, 0))
    return stepped(
        ffn_back_kernel,
        ride,
        "ffn_back",
        ff // fc,
        (g, xhat2, scale2, params, act, slope, r, e, xhat1, scale1, att, w4),
        [
            full, full, thin, whole(params.shape), tall, tall, r_spec, e_spec, full, thin, full,
            pl.BlockSpec((1, d, d), lambda j: (3, 0, 0)),
        ],
        [
            r_spec, e_spec, pl.BlockSpec((1, fc), lambda j: (0, j)), full, whole((d, d)), full, whole((8, d)),
        ],
        [
            jax.ShapeDtypeStruct((ff, d), BF),
            jax.ShapeDtypeStruct((d, ff), BF),
            jax.ShapeDtypeStruct((1, ff), F32),
            jax.ShapeDtypeStruct((n, d), F32),
            jax.ShapeDtypeStruct((d, d), BF),
            jax.ShapeDtypeStruct((n, d), BF),
            jax.ShapeDtypeStruct((8, d), F32),
        ],
        [pltpu.VMEM((n, d), BF), pltpu.VMEM((n, d), BF), pltpu.VMEM((n, d), F32)],
        pl.CostEstimate(
            flops=4 * n * d * (d + 2 * ff), bytes_accessed=4 * d * (d + 2 * ff) + 4 * n * ff + 24 * n * d, transcendentals=0
        ),
    )


def input_back_kernel(others, x_ref, dq_ref, own_ref, *refs):
    other_refs = refs[:others]
    w_ref, dsum_ref, g3_ref, dx_ref, small_ref = refs[others:]
    j = pl.program_id(0)

    def step(grad, row):
        g3_ref[0] = mm_tn(x_ref[...], grad).astype(BF)
        if row is not None:
            small_ref[row : row + 1, :] = rows_sum(grad.astype(F32))
        return mm_nt(grad, w_ref[0])

    def joined(index):
        value = own_ref[index].astype(F32)
        for ref in other_refs:
            value = value + ref[index].astype(F32)
        return value.astype(BF)

    @pl.when(j == 0)
    def _():
        small_ref[...] = jnp.zeros_like(small_ref)
        dx_ref[...] = dsum_ref[...] + step(dq_ref[...], 0)

    @pl.when(j == 1)
    def _():
        dx_ref[...] += step(joined(0), None)

    @pl.when(j == 2)
    def _():
        dx_ref[...] += step(joined(1), 1)


def input_back(x, dq, own, others, w4, dsum):
    n, d = x.shape
    full = whole((n, d))
    return pl.pallas_call(
        partial(input_back_kernel, len(others)),
        name="input_back",
        grid=(3,),
        in_specs=[full, full, whole((2, n, d))]
        + [whole((2, n, d))] * len(others)
        + [pl.BlockSpec((1, d, d), lambda j: (j, 0, 0)), full],
        out_specs=[pl.BlockSpec((1, d, d), lambda j: (j, 0, 0)), full, whole((8, d))],
        out_shape=[
            jax.ShapeDtypeStruct((3, d, d), BF),
            jax.ShapeDtypeStruct((n, d), F32),
            jax.ShapeDtypeStruct((8, d), F32),
        ],
        compiler_params=params_of(("arbitrary",)),
        cost_estimate=pl.CostEstimate(flops=12 * n * d * d, bytes_accessed=12 * d * d + 16 * n * d, transcendentals=0),
    )(x, dq, own, *others, w4, dsum)


class Grid:
    def __init__(self, dp, seq):
        self.ny = max(seq // 2, 1)
        self.nc = seq // self.ny
        self.nx = self.ny if dp % self.ny == 0 else 1
        self.nz = dp // self.nx
        self.sizes = {"z": self.nz, "x": self.nx, "y": self.ny, "c": self.nc}

    def here(self):
        d = lax.axis_index("dp")
        s = lax.axis_index("seq")
        return {"z": d // self.nx, "x": lax.rem(d, self.nx), "y": s // self.nc, "c": lax.rem(s, self.nc)}

    def device(self, at):
        return (at["z"] * self.nx + at["x"], at["y"] * self.nc + at["c"])

    def shifted(self, me, axis, step):
        other = dict(me)
        other[axis] = lax.rem(me[axis] + step, self.sizes[axis])
        return other

    def shape(self):
        return (self.nz, self.nx, self.ny, self.nc)

    def peers(self):
        return [(axis, step) for axis in "zxyc" for step in range(1, self.sizes[axis])]

    def barrier(self, me):
        sem = pltpu.get_barrier_semaphore()
        for axis, step in self.peers():
            pl.semaphore_signal(
                sem, inc=1, device_id=self.device(self.shifted(me, axis, step)), device_id_type=MESH
            )
        pl.semaphore_wait(sem, len(self.peers()))


def picked(place, axes):
    return tuple(slice(None) if axis in axes else place[axis] for axis in "zxyc")


def cuts_of(shapes):
    groups = []
    for number, shape in enumerate(shapes):
        rows, columns = shape[-2:]
        lead = shape[0] if len(shape) == 3 else None
        if columns % 256:
            groups.append([(number, None, (0, rows), (0, columns))])
            continue
        if lead is not None and lead % 2 == 0:
            pieces = [(number, (k, k + 1), (0, rows), (0, columns)) for k in range(lead)]
        elif lead == 3:
            left, right = (0, columns // 2), (columns // 2, columns // 2)
            pieces = [(number, (0, 1), (0, rows), (0, columns)), (number, (1, 2), (0, rows), (0, columns))]
            pieces += [(number, (2, 3), (0, rows), left), (number, (2, 3), (0, rows), right)]
        elif columns % 1024 == 0:
            pieces = [(number, None, (0, rows), (k * columns // 4, columns // 4)) for k in range(4)]
        elif rows % 32 == 0:
            pieces = [(number, None, (k * rows // 4, rows // 4), (0, columns)) for k in range(4)]
        elif columns % 256 == 0:
            pieces = [(number, None, (0, rows), (k * columns // 2, columns // 2)) for k in range(2)]
        else:
            groups.append([(number, None, (0, rows), (0, columns))])
            continue
        groups += [pieces[k : k + 2] for k in range(0, len(pieces), 2)]
    return groups


def region(ref, shape, cut, index):
    _, lead, rows, columns = cut
    head = ()
    if len(shape) == 3:
        head = (slice(None) if lead is None else slice(*lead),)
    return ref.at[head + tuple(index) + (slice(rows[0], sum(rows)), slice(columns[0], sum(columns)))]


ORDERS = (("z", "x", "y", "c"), ("z", "y", "x", "c"))


class Sender:
    def __init__(self, grid, me, send_sem, recv_sem):
        self.grid, self.me, self.send_sem, self.recv_sem = grid, me, send_sem, recv_sem
        self.started = []

    def send(self, src, dst, axis, step):
        return self.send_to(src, dst, self.grid.device(self.grid.shifted(self.me, axis, step)))

    def send_to(self, src, dst, device):
        k = len(self.started)
        copy = pltpu.make_async_remote_copy(
            src_ref=src, dst_ref=dst, send_sem=self.send_sem.at[k], recv_sem=self.recv_sem.at[k],
            device_id=device, device_id_type=MESH,
        )
        copy.start()
        self.started.append(copy)
        return copy

    def finish(self):
        for copy in self.started:
            copy.wait_send()


def gather_turns(sender, shapes, srcs, dsts, own_sem):
    grid, me = sender.grid, sender.me
    groups = cuts_of(shapes)
    own = []
    first = []
    for group in groups:
        copies = []
        for cut in group:
            shape = shapes[cut[0]]
            src = region(srcs[cut[0]], shape, cut, ())
            dst = region(dsts[cut[0]], shape, cut, picked(me, ""))
            copies.append([sender.send(src, dst, "z", step) for step in range(1, grid.nz)])
        first.append(copies)
    for k in range(len(shapes)):
        head = (slice(None),) if len(shapes[k]) == 3 else ()
        copy = pltpu.make_async_copy(srcs[k], dsts[k].at[head + picked(me, "")], own_sem.at[k])
        copy.start()
        own.append(copy)
    for copy in own:
        copy.wait()
    yield
    stages = {0: first}
    total = len(groups)
    depth = len(ORDERS[0])
    for turn in range(total + depth - 1):
        for stage in range(1, depth):
            g = turn - (stage - 1)
            if not 0 <= g < total:
                continue
            copies = []
            for side, cut in enumerate(groups[g]):
                order = ORDERS[side % 2]
                for copy in stages[stage - 1][g][side]:
                    copy.wait_recv()
                block = region(dsts[cut[0]], shapes[cut[0]], cut, picked(me, order[:stage]))
                copies.append(
                    [sender.send(block, block, order[stage], step) for step in range(1, grid.sizes[order[stage]])]
                )
            stages.setdefault(stage, {})[g] = copies
        g = turn - (depth - 1)
        if 0 <= g < total:
            for copies in stages[depth - 1][g]:
                for copy in copies:
                    copy.wait_recv()
        yield


def gather_kernel(grid, shapes, *refs):
    count = len(shapes)
    me = grid.here()
    grid.barrier(me)
    sender = Sender(grid, me, *refs[2 * count : 2 * count + 2])
    for _ in gather_turns(sender, shapes, refs[:count], refs[count : 2 * count], refs[-1]):
        pass
    sender.finish()


def copies_in(grid, shapes):
    return sum(len(group) for group in cuts_of(shapes)) * len(grid.peers())


def gather(grid, arrays, name, collective_id):
    shapes = [a.shape for a in arrays]
    outs = [a.shape[:-2] + grid.shape() + a.shape[-2:] for a in arrays]
    count = copies_in(grid, shapes)
    got = pl.pallas_call(
        partial(gather_kernel, grid, shapes),
        name=name,
        in_specs=[pl.BlockSpec(memory_space=pltpu.VMEM)] * len(arrays),
        out_specs=[pl.BlockSpec(memory_space=pl.ANY)] * len(arrays),
        out_shape=[jax.ShapeDtypeStruct(s, a.dtype) for s, a in zip(outs, arrays)],
        scratch_shapes=[
            pltpu.SemaphoreType.DMA((count,)),
            pltpu.SemaphoreType.DMA((count,)),
            pltpu.SemaphoreType.DMA((len(arrays),)),
        ],
        compiler_params=pltpu.CompilerParams(
            collective_id=collective_id, has_side_effects=True, vmem_limit_bytes=VMEM_LIMIT
        ),
    )(*arrays)
    blocks = math.prod(grid.shape())
    return [o.reshape(a.shape[:-2] + (blocks * a.shape[-2], a.shape[-1])) for o, a in zip(got, arrays)]


def spread_small(table_ref, thin_refs, wide_refs, rows, blocks):
    lines = table_ref.shape[-2]
    table = table_ref[...].reshape(blocks * lines, 128)

    def picker(per, width):
        column = lax.broadcasted_iota(jnp.int32, (128, width), 1)
        scale = -(-(1 << 20) // per)
        rest = column - lax.shift_right_logical(column * scale, 20) * per
        hot = (lax.broadcasted_iota(jnp.int32, (128, width), 0) == rest).astype(F32).astype(BF)
        place = lax.broadcasted_iota(jnp.int32, (blocks, lines, width), 2)
        owner = lax.broadcasted_iota(jnp.int32, (blocks, lines, width), 0)
        return hot, lax.shift_right_logical(place * scale, 20) == owner

    thin_width = thin_refs[0].shape[-1]
    hot, keep = picker(rows, thin_width)
    wide = mm(table, hot).reshape(blocks, lines, thin_width)
    vectors = jnp.sum(jnp.where(keep, wide, 0.0), axis=0)
    for layer, ref in enumerate(thin_refs):
        ref[...] = vectors[layer * 16 : layer * 16 + ROWS]
    step = 1024
    for first in range(0, wide_refs[0].shape[-1], step):
        scale = -(-(1 << 20) // (4 * rows))
        column = lax.broadcasted_iota(jnp.int32, (128, step), 1) + first
        rest = column - lax.shift_right_logical(column * scale, 20) * (4 * rows)
        hot = (lax.broadcasted_iota(jnp.int32, (128, step), 0) == rest).astype(F32).astype(BF)
        place = lax.broadcasted_iota(jnp.int32, (blocks, lines, step), 2) + first
        owner = lax.broadcasted_iota(jnp.int32, (blocks, lines, step), 0)
        full = mm(table, hot).reshape(blocks, lines, step)
        part = jnp.sum(jnp.where(lax.shift_right_logical(place * scale, 20) == owner, full, 0.0), axis=0)
        for layer, ref in enumerate(wide_refs):
            ref[:, first : first + step] = part[layer * 16 + 8 : layer * 16 + 9]


def front_kernel(grid, shapes, *refs):
    count = len(shapes)
    srcs, refs = refs[:count], refs[count:]
    x_ref, refs = refs[0], refs[1:]
    fulls, refs = refs[: count - 1], refs[count - 1 :]
    p1_ref, p2_ref, eb1_ref, eb2_ref, q_ref, kv_ref, far_ref, att_ref, lse_ref = refs[:9]
    out_ref, xhat1_ref, scale1_ref, act_ref, slope_ref, xhat2_ref, scale2_ref = refs[9:16]
    table_ref, w4_ref, r_ref, e_ref, hidden_ref, low_ref, total_ref = refs[16:23]
    send_sem, recv_sem, own_sem, load_sem = refs[23:]
    n, d = x_ref.shape
    ff = e_ref.shape[-1]
    me = grid.here()
    grid.barrier(me)
    sender = Sender(grid, me, send_sem, recv_sem)
    turns = gather_turns(sender, shapes, srcs, (table_ref,) + tuple(fulls), own_sem)
    left = [len(cuts_of(shapes)) + 4]

    def advance(steps=1):
        for _ in range(min(steps, left[0])):
            next(turns)
            left[0] -= 1

    def load(source, target, k):
        copy = pltpu.make_async_copy(source, target, load_sem.at[k])
        copy.start()
        return copy

    def joined(blocks):
        return blocks.astype(F32).reshape(-1, blocks.shape[-1]).astype(BF)

    advance(5)
    blocks = math.prod(grid.shape())
    spread_small(table_ref, (p1_ref, p2_ref), (eb1_ref, eb2_ref), shapes[1][-2], blocks)
    advance(2)
    load(fulls[0], w4_ref, 0).wait()
    x = x_ref[...]
    kv_ref[0] = mm(x, joined(w4_ref[1])).astype(BF)
    kv_ref[1] = (mm(x, joined(w4_ref[2])) + p1_ref[1:2, :]).astype(BF)
    swapped = sender.send(kv_ref, far_ref, "c", 1)
    q_ref[...] = (mm(x, joined(w4_ref[0])) + p1_ref[0:1, :]).astype(BF)
    advance(1)
    swapped.wait_recv()
    for pair in range(d // (2 * HD)):
        lanes = slice(pair * 2 * HD, (pair + 1) * 2 * HD)
        kvs = [(r[0, :, lanes], r[1, :, lanes]) for r in (kv_ref, far_ref)]
        att_ref[:, lanes], lse_ref[:, lanes] = attend_pair(q_ref[:, lanes], kvs, None)
        if pair % 2:
            advance(1)
        if pair == 1:
            loads = [load(fulls[1], r_ref, 1)]
    loads.append(load(fulls[2], e_ref, 2))
    summed = x.astype(F32) + mm(att_ref[...], joined(w4_ref[3])) + p1_ref[2:3, :]
    xhat, scale = normed(summed)
    xhat1_ref[...] = xhat
    scale1_ref[...] = jnp.broadcast_to(scale, scale1_ref.shape)
    hidden = xhat * p1_ref[3:4, :] + p1_ref[4:5, :]
    hidden_ref[...] = hidden
    low_ref[...] = hidden.astype(BF)
    for copy in loads:
        copy.wait()
    step = 512
    for first in range(0, ff, step):
        part = slice(first, first + step)
        active, slope = gelu_pair(mm(low_ref[...], joined(e_ref[..., part])) + eb1_ref[:, part])
        active = active.astype(BF)
        act_ref[:, part] = active
        slope_ref[:, part] = slope.astype(BF)
        more = mm(active, r_ref[...].reshape(ff, d)[part, :])
        total_ref[...] = more if first == 0 else total_ref[...] + more
        if first // step % 2:
            advance(1)
    pre = hidden_ref[...] + total_ref[...] + p1_ref[5:6, :]
    xhat, scale = normed(pre)
    xhat2_ref[...] = xhat
    scale2_ref[...] = jnp.broadcast_to(scale, scale2_ref.shape)
    out_ref[...] = (xhat * p1_ref[6:7, :] + p1_ref[7:8, :]).astype(BF)
    advance(left[0])
    sender.finish()


def front(grid, arrays, x, name, collective_id):
    shapes = [a.shape for a in arrays]
    n, d = x.shape
    ff = arrays[3].shape[1]
    count = copies_in(grid, shapes) + 1
    vmem = pl.BlockSpec(memory_space=pltpu.VMEM)
    hbm = pl.BlockSpec(memory_space=pl.ANY)
    fulls = [jax.ShapeDtypeStruct(a.shape[:-2] + grid.shape() + a.shape[-2:], BF) for a in arrays[1:]]
    local = [
        ((ROWS, d), F32), ((ROWS, d), F32), ((1, ff), F32), ((1, ff), F32),
        ((n, d), BF), ((2, n, d), BF), ((2, n, d), BF), ((n, d), BF), ((n, d), F32),
        ((n, d), BF), ((n, d), F32), ((n, 128), F32), ((n, ff), BF), ((n, ff), BF), ((n, d), F32), ((n, 128), F32),
    ]
    got = pl.pallas_call(
        partial(front_kernel, grid, shapes),
        name=name,
        in_specs=[vmem] * (len(arrays) + 1),
        out_specs=[hbm] * len(fulls) + [vmem] * len(local),
        out_shape=fulls + [jax.ShapeDtypeStruct(*s) for s in local],
        scratch_shapes=[
            pltpu.VMEM(grid.shape() + arrays[0].shape, BF),
            pltpu.VMEM(fulls[0].shape, BF),
            pltpu.VMEM(fulls[1].shape, BF),
            pltpu.VMEM(fulls[2].shape, BF),
            pltpu.VMEM((n, d), F32),
            pltpu.VMEM((n, d), BF),
            pltpu.VMEM((n, d), F32),
            pltpu.SemaphoreType.DMA((count,)),
            pltpu.SemaphoreType.DMA((count,)),
            pltpu.SemaphoreType.DMA((len(arrays),)),
            pltpu.SemaphoreType.DMA((3,)),
        ],
        compiler_params=pltpu.CompilerParams(
            collective_id=collective_id, has_side_effects=True, vmem_limit_bytes=VMEM_LIMIT
        ),
    )(*arrays, x)
    blocks = math.prod(grid.shape())
    weights = [
        o.reshape(a.shape[:-2] + (blocks * a.shape[-2], a.shape[-1])) for o, a in zip(got, arrays[1:])
    ]
    return weights, got[len(fulls) :]


BACK_ORDERS = (("c", "x", "y", "z"), ("c", "y", "x", "z"))


def left_axes(order, stage):
    return [axis for axis in "zxyc" if axis not in order[:stage]]


class Scatter:
    def __init__(self, grid, plan, refs):
        shapes, layouts = plan.shapes, plan.layouts
        count = len(shapes)
        self.grid, self.shapes = grid, shapes
        self.me = grid.here()
        self.srcs, self.outs = refs[:count], refs[count : 2 * count]
        held = refs[2 * count : -3]
        send_sem, recv_sem, own_sem = refs[-3:]
        self.groups = cuts_of(shapes)
        self.near = {peer: grid.shifted(self.me, *peer) for peer in grid.peers()}
        devices = {peer: grid.device(at) for peer, at in self.near.items()}
        self.buffers, self.own, self.flights = {}, {}, {}
        position = piece = number = 0
        for g, group in enumerate(self.groups):
            for side, cut in enumerate(group):
                order = BACK_ORDERS[side % 2]
                head = (slice(None),) if self.lead_of(cut) else ()
                for stage in range(len(layouts[piece])):
                    buf = held[position]
                    position += 1
                    self.buffers[g, side, stage] = buf
                    axis = order[stage]
                    copies = []
                    for step in range(1, grid.sizes[axis]):
                        there = self.near[axis, step]
                        if stage == 0:
                            src = region(self.srcs[cut[0]], shapes[cut[0]], cut, picked(there, "zxy"))
                        else:
                            index = tuple(
                                there[a] if a == axis else slice(None) for a in left_axes(order, stage)
                            )
                            src = self.buffers[g, side, stage - 1].at[(0,) + head + index]
                        slot = step - 1 if stage == len(layouts[piece]) - 1 else step
                        copies.append(
                            pltpu.make_async_remote_copy(
                                src_ref=src, dst_ref=buf.at[slot],
                                send_sem=send_sem.at[number], recv_sem=recv_sem.at[number],
                                device_id=devices[axis, step], device_id_type=MESH,
                            )
                        )
                        number += 1
                    self.flights[g, side, stage] = copies
                src = region(self.srcs[cut[0]], shapes[cut[0]], cut, picked(self.me, "zxy"))
                self.own[g, side] = pltpu.make_async_copy(src, self.buffers[g, side, 0].at[0], own_sem.at[piece])
                piece += 1

    def lead_of(self, cut):
        return len(self.shapes[cut[0]]) == 3

    def start(self):
        self.grid.barrier(self.me)
        for g, group in enumerate(self.groups):
            for side in range(len(group)):
                self.own[g, side].start()
                for copy in self.flights[g, side, 0]:
                    copy.start()

    def turn(self, number):
        depth = 4
        for stage in range(depth):
            g = number - stage
            if not 0 <= g < len(self.groups):
                continue
            for side, cut in enumerate(self.groups[g]):
                order = BACK_ORDERS[side % 2]
                buf = self.buffers[g, side, stage]
                for copy in self.flights[g, side, stage]:
                    copy.wait_recv()
                if stage == 0:
                    self.own[g, side].wait()
                    add_into(buf)
                else:
                    source = self.buffers[g, side, stage - 1]
                    rest = left_axes(order, stage)
                    if stage == depth - 1:
                        head = (slice(None),) if self.lead_of(cut) else ()
                        total = source[(0,) + head + tuple(self.me[a] for a in rest)].astype(F32)
                        for slot in range(buf.shape[0]):
                            total = total + buf[slot].astype(F32)
                        region(self.outs[cut[0]], self.shapes[cut[0]], cut, ())[...] = total
                        continue
                    merge(source, buf, self.me, rest, order[stage], self.lead_of(cut))
                for copy in self.flights[g, side, stage + 1]:
                    copy.start()

    def finish(self):
        for copies in self.flights.values():
            for copy in copies:
                copy.wait_send()

    def turns(self):
        steps = [partial(self.turn, k) for k in range(len(self.groups) + 3)]
        return [self.start] + steps + [self.finish]


def unflat(number, sizes):
    index = []
    for size in reversed(sizes):
        index.append(lax.rem(number, size))
        number = number // size
    return tuple(reversed(index))


def add_into(buf):
    flat = buf.shape[1:-2]

    def body(i, carry):
        index = unflat(i, flat)
        value = buf[(0,) + index].astype(F32)
        for slot in range(1, buf.shape[0]):
            value = value + buf[(slot,) + index].astype(F32)
        buf[(0,) + index] = value.astype(buf.dtype)
        return carry

    lax.fori_loop(0, math.prod(flat), body, 0)


def merge(source, buf, me, axes, axis, lead):
    flat = buf.shape[1:-2]
    where = axes.index(axis) + (1 if lead else 0)

    def body(i, carry):
        index = unflat(i, flat)
        wide = index[:where] + (me[axis],) + index[where:]
        value = source[(0,) + wide].astype(F32)
        for slot in range(1, buf.shape[0]):
            value = value + buf[(slot,) + index].astype(F32)
        buf[(0,) + index] = value.astype(buf.dtype)
        return carry

    lax.fori_loop(0, math.prod(flat), body, 0)


class ScatterPlan:
    def __init__(self, grid, arrays):
        blocks = math.prod(grid.shape())
        self.shapes = [a.shape[:-2] + (a.shape[-2] // blocks, a.shape[-1]) for a in arrays]
        self.views = [a.reshape(s[:-2] + grid.shape() + s[-2:]) for a, s in zip(arrays, self.shapes)]
        self.layouts = []
        self.scratch = []
        for group in cuts_of(self.shapes):
            for side, cut in enumerate(group):
                shape = self.shapes[cut[0]]
                order = BACK_ORDERS[side % 2]
                head = ()
                if len(shape) == 3:
                    head = (shape[0] if cut[1] is None else cut[1][1] - cut[1][0],)
                stages = []
                for stage in range(4):
                    rest = left_axes(order, stage + 1)
                    slots = grid.sizes[order[stage]] - (1 if stage == 3 else 0)
                    stages.append((slots,) + head + tuple(grid.sizes[a] for a in rest) + (cut[2][1], cut[3][1]))
                self.layouts.append(stages)
                self.scratch += [pltpu.VMEM(s, arrays[cut[0]].dtype) for s in stages]
        count = copies_in(grid, self.shapes)
        self.scratch += [
            pltpu.SemaphoreType.DMA((count,)),
            pltpu.SemaphoreType.DMA((count,)),
            pltpu.SemaphoreType.DMA((len(self.layouts),)),
        ]
        self.outs = [jax.ShapeDtypeStruct(s, F32) for s in self.shapes]


def scatter(grid, arrays, name, collective_id):
    plan = ScatterPlan(grid, arrays)

    def kernel(*refs):
        for step in Scatter(grid, plan, refs).turns():
            step()

    return pl.pallas_call(
        kernel,
        name=name,
        in_specs=[pl.BlockSpec(memory_space=pl.ANY)] * len(arrays),
        out_specs=[pl.BlockSpec(memory_space=pltpu.VMEM)] * len(arrays),
        out_shape=plan.outs,
        scratch_shapes=plan.scratch,
        compiler_params=pltpu.CompilerParams(
            collective_id=collective_id, has_side_effects=True, vmem_limit_bytes=VMEM_LIMIT
        ),
    )(*plan.views)


def stepped(body, ride, name, steps, args, in_specs, out_specs, out_shape, scratch, cost):
    if ride is None:
        out = pl.pallas_call(
            body, name=name, grid=(steps,), in_specs=in_specs, out_specs=out_specs, out_shape=out_shape,
            scratch_shapes=scratch, compiler_params=params_of(("arbitrary",)), cost_estimate=cost,
        )(*args)
        return out, ()
    grid, arrays, collective_id = ride
    plan = ScatterPlan(grid, arrays)
    count, riders = len(args), len(arrays)
    results, locals_ = len(out_shape), len(scratch)

    def kernel(*refs):
        ins, refs = refs[:count], refs[count:]
        views, refs = refs[:riders], refs[riders:]
        outs, refs = refs[:results], refs[results:]
        sums, refs = refs[:riders], refs[riders:]
        own, refs = refs[:locals_], refs[locals_:]
        turns = Scatter(grid, plan, views + sums + refs).turns()
        j = pl.program_id(0)
        for k, turn in enumerate(turns[:steps]):
            pl.when(j == k)(turn)
        body(*ins, *outs, *own)

        @pl.when(j == steps - 1)
        def _():
            for turn in turns[steps:]:
                turn()

    out = pl.pallas_call(
        kernel,
        name=name,
        grid=(steps,),
        in_specs=in_specs + [pl.BlockSpec(memory_space=pl.ANY)] * riders,
        out_specs=out_specs + [whole(s.shape) for s in plan.outs],
        out_shape=out_shape + plan.outs,
        scratch_shapes=scratch + plan.scratch,
        compiler_params=pltpu.CompilerParams(
            dimension_semantics=("arbitrary",), collective_id=collective_id, has_side_effects=True,
            vmem_limit_bytes=VMEM_LIMIT,
        ),
        cost_estimate=cost,
    )(*args, *plan.views)
    return out[:results], out[results:]


ROWS = 8
ROW_AT = (1, 4, 6, 7, 8, 12, 13, 14)


def pack_small(layers):
    parts = []
    for params in layers:
        parts += [params[k] for k in ROW_AT] + [params[10]]
    flat = jnp.concatenate(parts)
    size = 1024 * -(-flat.shape[0] // 1024)
    return jnp.pad(flat, (0, size - flat.shape[0])).reshape(size // 128, 128)


def small_table(layers):
    lines = []
    for params in layers:
        for k in ROW_AT + (10,):
            lines.append(jnp.pad(params[k], (0, 128 - params[k].shape[0])))
        lines += [jnp.zeros((128,), BF)] * 7
    return jnp.stack(lines)


def unpack_small(full, blocks, rows, layers):
    per = full.shape[0] // blocks * full.shape[1]
    flat = full.reshape(blocks, per)
    out = []
    width = (ROWS + 4) * rows
    for layer in range(layers):
        part = flat[:, layer * width : (layer + 1) * width].astype(F32)
        thin = part[:, : ROWS * rows].reshape(blocks, ROWS, rows).transpose(1, 0, 2).reshape(ROWS, blocks * rows)
        out.append((thin, part[:, ROWS * rows :].reshape(1, blocks * 4 * rows)))
    return out


def pack_grads(grads, blocks, rows):
    parts = []
    for thin, wide in grads:
        parts.append(thin.reshape(ROWS, blocks, rows).transpose(1, 0, 2).reshape(blocks, ROWS * rows))
        parts.append(wide.reshape(blocks, 4 * rows))
    flat = jnp.concatenate(parts, axis=1)
    size = 1024 * -(-flat.shape[1] // 1024)
    return jnp.pad(flat, ((0, 0), (0, size - flat.shape[1]))).reshape(blocks * (size // 128), 128)


def on_device(grid, tokens, early, cot_backbone, cot_head, lengths, cls_pos, *weights):
    layers = (weights[:15], weights[15:])
    members = lax.axis_size("seq")
    blocks = math.prod(grid.shape())
    seqs, rows, width = tokens.shape
    half = members // seqs
    spot = lax.axis_index("seq")
    mine = spot // half
    swap = [(i, (i + half) % members) for i in range(members)]
    far = lax.rem(spot + half, members)
    masked = rows * members > MIN_LEN

    def spread(value):
        kept = lax.dynamic_index_in_dim(value, mine, 0, keepdims=False)
        sent = lax.dynamic_index_in_dim(value, 1 - mine, 0, keepdims=False)
        return jnp.concatenate([kept, lax.ppermute(sent, "seq", swap)], axis=0)

    def collect(value):
        kept = value[:rows]
        got = lax.ppermute(value[rows:], "seq", swap)
        return jnp.where(mine == 0, jnp.stack([kept, got]), jnp.stack([got, kept]))

    def around(value, step):
        pairs = [(i, i // half * half + (i % half + step) % half) for i in range(members)]
        return lax.ppermute(value, "seq", pairs)

    length = lax.dynamic_index_in_dim(lengths, mine, 0, keepdims=False)
    cls = lax.dynamic_index_in_dim(cls_pos, mine, 0, keepdims=False)
    line = jnp.arange(rows, dtype=jnp.int32)
    positions = jnp.concatenate([spot * rows + line, far * rows + line])
    is_cls = (positions == cls)[:, None]
    valid = (positions < length)[:, None]
    biases = None
    if masked:
        steps = []
        for step in range(half):
            member = mine * half + lax.rem(lax.rem(spot, half) - step + half, half)
            other = lax.rem(member + half, members)
            place = jnp.concatenate([member * rows + line, other * rows + line])
            steps.append(jnp.where(place < length, 0.0, NEG)[None, :])
        biases = jnp.stack(steps)

    x_back = spread(tokens)
    x_early = spread(early)
    g_back = spread(cot_backbone)
    g_head = spread(cot_head)
    if masked:
        g_back = jnp.where(valid, g_back, jnp.zeros_like(g_back))
        g_head = jnp.where(valid, g_head, jnp.zeros_like(g_head))

    shard = layers[0][0].shape[0]
    stacked = [jnp.stack([p[0], p[2], p[3], p[5]]) for p in layers]
    fused = shard % 8 == 0 and half == 2 and not masked
    if fused:
        travel = [small_table(layers)]
        for k in range(2):
            travel += [stacked[k], layers[k][11], layers[k][9]]
        (w4_back, r_back, e_back, w4_head, r_head, e_head), kept = front(grid, travel, x_back, "front", 0)
        p_back, p_head, eb_back, eb_head, q, kv, far_kv, att, lse, back_low = kept[:10]
        back_kept = (q, [kv, far_kv], lse, (x_back, att) + tuple(kept[10:]))
    else:
        small = pack_small(layers)
        w4_back, e_back, r_back, small_full = gather(
            grid, [stacked[0], layers[0][9], layers[0][11], small], "gather_back", 0
        )
        w4_head, e_head, r_head = gather(grid, [stacked[1], layers[1][9], layers[1][11]], "gather_head", 1)
        (p_back, eb_back), (p_head, eb_head) = unpack_small(small_full, blocks, shard, 2)

    def forward(x, w4, e, r, params, eb):
        q, kv = qkv(x, w4, params)
        kvs = [kv] + [around(kv, step) for step in range(1, half)]
        att, lse = attend(q, kvs, biases)
        out, xhat1, scale1, act, slope, xhat2, scale2 = post(x, att, w4, e, eb, r, params)
        return out, (q, kvs, lse, (x, att, xhat1, scale1, act, slope, xhat2, scale2))

    def backward(g, kept, w4, e, r, params, before, number):
        q, kvs, lse, saved = kept
        x, att = saved[:2]
        ride = None if before is None else (grid, before, number)
        (gr, ge, geb, dsum, go, datt, small_a), sums = ffn_back(g, saved, w4, e, r, params, ride)
        dq, dkvs, wide = attend_back(q, datt, att, lse, kvs, biases, (grid, [ge, gr], number + 1))
        others = [around(dkvs[step], half - step) for step in range(1, half)]
        g3, dx, small_b = input_back(x, dq, dkvs[0], others, w4, dsum)
        return dx, [g3, go[None]], (small_a + small_b, geb), wide, sums

    if not fused:
        back_low, back_kept = forward(x_back, w4_back, e_back, r_back, p_back, eb_back)
    head_in = jnp.where(is_cls, back_low, x_early)
    head_low, head_kept = forward(head_in, w4_head, e_head, r_head, p_head, eb_head)
    dx_head, narrow_head, small_head, (seh, srh), _ = backward(
        g_head, head_kept, w4_head, e_head, r_head, p_head, None, 2
    )
    g_mixed = g_back.astype(F32) + jnp.where(is_cls, dx_head, 0.0)
    dx_back, narrow_back, small_back, (seb, srb), (s3h, soh) = backward(
        g_mixed, back_kept, w4_back, e_back, r_back, p_back, narrow_head, 4
    )
    packed = pack_grads([small_back, small_head], blocks, shard)
    s3b, sob, small_sum = scatter(grid, narrow_back + [packed], "scatter_back", 6)

    flat = small_sum.reshape(-1)

    def layer_grads(layer, s3, so, se, sr):
        base = layer * (ROWS + 4) * shard
        thin = [flat[base + k * shard : base + (k + 1) * shard] for k in range(ROWS)]
        wide = flat[base + ROWS * shard : base + (ROWS + 4) * shard]
        return (
            s3[0], thin[0], s3[1], s3[2], thin[1], so[0], thin[2], thin[3], thin[4],
            se, wide, sr, thin[5], thin[6], thin[7],
        )

    return (
        collect(back_low),
        collect(head_low),
        collect(dx_back.astype(BF)),
        collect(jnp.where(is_cls, 0.0, dx_head).astype(BF)),
    ) + layer_grads(0, s3b, sob, seb, srb) + layer_grads(1, s3h, soh, seh, srh)


def solution(mesh):
    rows = P("dp", "seq", None)
    wide = P(("dp", "seq"), None)
    thin = P(("dp", "seq"))
    layer = tuple(thin if k in (1, 4, 6, 7, 8, 10, 12, 13, 14) else wide for k in range(15))
    grid = Grid(mesh.shape["dp"], mesh.shape["seq"])
    return jax.shard_map(
        partial(on_device, grid),
        mesh=mesh,
        in_specs=(rows,) * 4 + (P("dp"),) * 2 + layer + layer,
        out_specs=(rows,) * 4 + layer + layer,
        check_vma=False,
    )
```

```python
from functools import partial
import math

import jax
import jax.numpy as jnp
from jax import lax
from jax.experimental import pallas as pl
from jax.experimental.pallas import tpu as pltpu
from jax.sharding import PartitionSpec as P

H = 12
HD = 64
EPS = 1e-12
NEG = -1e30
MIN_LEN = 1024
BF = jnp.bfloat16
F32 = jnp.float32
MESH = pl.DeviceIdType.MESH
VMEM_LIMIT = 60 * 1024 * 1024


def mm(left, right):
    return lax.dot_general(left, right, (((1,), (0,)), ((), ())), preferred_element_type=F32)


def mm_nt(left, right):
    return lax.dot_general(left, right, (((1,), (1,)), ((), ())), preferred_element_type=F32)


def mm_tn(left, right):
    return lax.dot_general(left, right, (((0,), (0,)), ((), ())), preferred_element_type=F32)


def whole(shape):
    return pl.BlockSpec(shape, lambda *_: (0,) * len(shape))


def params_of(semantics):
    return pltpu.CompilerParams(dimension_semantics=semantics, vmem_limit_bytes=VMEM_LIMIT)


def qkv_kernel(x_ref, w_ref, p_ref, q_ref, kv_ref):
    j = pl.program_id(0)
    out = mm(x_ref[...], w_ref[0])

    @pl.when(j == 0)
    def _():
        q_ref[...] = (out + p_ref[0:1, :]).astype(BF)

    @pl.when(j == 1)
    def _():
        kv_ref[0] = out.astype(BF)

    @pl.when(j == 2)
    def _():
        kv_ref[0] = (out + p_ref[1:2, :]).astype(BF)


def qkv(x, w4, params):
    n, d = x.shape
    return pl.pallas_call(
        qkv_kernel,
        name="qkv",
        grid=(3,),
        in_specs=[
            whole((n, d)),
            pl.BlockSpec((1, d, d), lambda j: (j, 0, 0)),
            whole(params.shape),
        ],
        out_specs=[
            whole((n, d)),
            pl.BlockSpec((1, n, d), lambda j: (jnp.maximum(j - 1, 0), 0, 0)),
        ],
        out_shape=[
            jax.ShapeDtypeStruct((n, d), BF),
            jax.ShapeDtypeStruct((2, n, d), BF),
        ],
        compiler_params=params_of(("arbitrary",)),
        cost_estimate=pl.CostEstimate(flops=6 * n * d * d, bytes_accessed=6 * d * d + 8 * n * d, transcendentals=0),
    )(x, w4, params)


def half_masks(n):
    lane = lax.broadcasted_iota(jnp.int32, (n, 2 * HD), 1)
    return lane < HD


def attend_pair(q, kvs, biases):
    n = q.shape[0]
    low = half_masks(n)
    q = q * jnp.asarray(HD**-0.5, BF)
    outs = []
    logs = []
    for side in range(2):
        qm = jnp.where(low if side == 0 else ~low, q, jnp.zeros_like(q))
        scores = []
        for t, (key, _) in enumerate(kvs):
            s = mm_nt(qm, key)
            if biases is not None:
                s = s + biases[t]
            scores.append(s)
        top = scores[0].max(axis=-1, keepdims=True)
        for s in scores[1:]:
            top = jnp.maximum(top, s.max(axis=-1, keepdims=True))
        total = jnp.zeros((n, 1), F32)
        numer = jnp.zeros((n, 2 * HD), F32)
        for t, (_, value) in enumerate(kvs):
            weight = jnp.exp(scores[t] - top)
            total = total + weight.sum(axis=-1, keepdims=True)
            numer = numer + mm(weight.astype(BF), value)
        outs.append(numer / total)
        logs.append(top + jnp.log(total))
    return jnp.where(low, outs[0], outs[1]).astype(BF), jnp.where(low, logs[0], logs[1])


def attend_kernel(pieces, masked, *refs):
    q_ref = refs[0]
    kv_refs = refs[1 : 1 + pieces]
    refs = refs[1 + pieces :]
    biases = None
    if masked:
        biases, refs = [refs[0][t] for t in range(pieces)], refs[1:]
    att_ref, lse_ref = refs
    att_ref[...], lse_ref[...] = attend_pair(q_ref[...], [(r[0], r[1]) for r in kv_refs], biases)


def attend(q, kvs, biases):
    n, d = q.shape
    pieces = len(kvs)
    masked = biases is not None
    pair = 2 * HD
    col = pl.BlockSpec((n, pair), lambda j: (0, j))
    kv_spec = pl.BlockSpec((2, n, pair), lambda j: (0, 0, j))
    extra = (biases,) if masked else ()
    return pl.pallas_call(
        partial(attend_kernel, pieces, masked),
        name="attend",
        grid=(d // pair,),
        in_specs=[col] + [kv_spec] * pieces + [whole(b.shape) for b in extra],
        out_specs=[col, col],
        out_shape=[jax.ShapeDtypeStruct((n, d), BF), jax.ShapeDtypeStruct((n, d), F32)],
        compiler_params=params_of(("arbitrary",)),
        cost_estimate=pl.CostEstimate(
            flops=4 * n * n * pieces * d, bytes_accessed=(8 + 4 * pieces) * n * d, transcendentals=n * n * pieces * H
        ),
    )(q, *kvs, *extra)


def attend_back_kernel(pieces, masked, *refs):
    q_ref, do_ref, att_ref, lse_ref = refs[:4]
    kv_refs = refs[4 : 4 + pieces]
    refs = refs[4 + pieces :]
    bias_ref = None
    if masked:
        bias_ref, refs = refs[0], refs[1:]
    dq_ref = refs[0]
    dkv_refs = refs[1:]
    n = q_ref.shape[0]
    scale = HD**-0.5
    low = half_masks(n)
    q = q_ref[...] * jnp.asarray(scale, BF)
    do = do_ref[...]
    prod = do.astype(F32) * att_ref[...].astype(F32)
    dq = jnp.zeros((n, 2 * HD), F32)
    qms, doms, deltas, lses = [], [], [], []
    for side in range(2):
        mask = low if side == 0 else ~low
        qms.append(jnp.where(mask, q, jnp.zeros_like(q)))
        doms.append(jnp.where(mask, do, jnp.zeros_like(do)))
        deltas.append(jnp.sum(jnp.where(mask, prod, 0.0), axis=-1, keepdims=True))
        lses.append(lse_ref[:, side * HD : side * HD + 1])
    dqs = [jnp.zeros((n, 2 * HD), F32) for _ in range(2)]
    for t in range(pieces):
        k = kv_refs[t][0]
        v = kv_refs[t][1]
        dk = jnp.zeros((n, 2 * HD), F32)
        dv = jnp.zeros((n, 2 * HD), F32)
        for side in range(2):
            s = mm_nt(qms[side], k)
            if masked:
                s = s + bias_ref[t]
            p = jnp.exp(s - lses[side])
            dp = mm_nt(doms[side], v)
            ds = (p * (dp - deltas[side])).astype(BF)
            dv = dv + mm_tn(p.astype(BF), doms[side])
            dk = dk + mm_tn(ds, qms[side])
            dqs[side] = dqs[side] + mm(ds, k)
        dkv_refs[t][0] = dk.astype(BF)
        dkv_refs[t][1] = dv.astype(BF)
    dq_ref[...] = (jnp.where(low, dqs[0], dqs[1]) * scale).astype(BF)


def attend_back(q, do, att, lse, kvs, biases, ride=None):
    n, d = q.shape
    pieces = len(kvs)
    masked = biases is not None
    pair = 2 * HD
    col = pl.BlockSpec((n, pair), lambda j: (0, j))
    kv_spec = pl.BlockSpec((2, n, pair), lambda j: (0, 0, j))
    extra = (biases,) if masked else ()
    out, sums = stepped(
        partial(attend_back_kernel, pieces, masked),
        ride,
        "attend_back",
        d // pair,
        (q, do, att, lse, *kvs, *extra),
        [col] * 4 + [kv_spec] * pieces + [whole(b.shape) for b in extra],
        [col] + [kv_spec] * pieces,
        [jax.ShapeDtypeStruct((n, d), BF)] + [jax.ShapeDtypeStruct((2, n, d), BF)] * pieces,
        [],
        pl.CostEstimate(
            flops=10 * n * n * pieces * d, bytes_accessed=(12 + 8 * pieces) * n * d, transcendentals=n * n * pieces * H
        ),
    )
    return out[0], out[1:], sums


def normed(value):
    mean = jnp.mean(value, axis=-1, keepdims=True)
    centred = value - mean
    spread = jnp.mean(centred * centred, axis=-1, keepdims=True)
    scale = lax.rsqrt(spread + EPS)
    return centred * scale, scale


def norm_back(grad, xhat, scale):
    mean_grad = jnp.mean(grad, axis=-1, keepdims=True)
    mean_dot = jnp.mean(grad * xhat, axis=-1, keepdims=True)
    return scale * (grad - mean_grad - xhat * mean_dot)


def gelu_pair(value):
    cdf = 0.5 + 0.5 * lax.erf(value * (0.5**0.5))
    pdf = jnp.exp(-0.5 * value * value) * ((2.0 * math.pi) ** -0.5)
    return value * cdf, cdf + value * pdf


def post_kernel(
    x_ref, att_ref, w_ref, e_ref, eb_ref, r_ref, p_ref,
    out_ref, xhat1_ref, scale1_ref, act_ref, slope_ref, xhat2_ref, scale2_ref,
    hidden_ref, low_ref, total_ref,
):
    j = pl.program_id(0)
    lanes = scale1_ref.shape

    @pl.when(j == 0)
    def _():
        summed = x_ref[...].astype(F32) + mm(att_ref[...], w_ref[0]) + p_ref[2:3, :]
        xhat, scale = normed(summed)
        xhat1_ref[...] = xhat
        scale1_ref[...] = jnp.broadcast_to(scale, lanes)
        hidden = xhat * p_ref[3:4, :] + p_ref[4:5, :]
        hidden_ref[...] = hidden
        low_ref[...] = hidden.astype(BF)
        total_ref[...] = jnp.zeros_like(total_ref)

    inner = mm(low_ref[...], e_ref[...]) + eb_ref[...]
    active, slope = gelu_pair(inner)
    active = active.astype(BF)
    act_ref[...] = active
    slope_ref[...] = slope.astype(BF)
    total_ref[...] += mm(active, r_ref[...])

    @pl.when(j == pl.num_programs(0) - 1)
    def _():
        pre = hidden_ref[...] + total_ref[...] + p_ref[5:6, :]
        xhat, scale = normed(pre)
        xhat2_ref[...] = xhat
        scale2_ref[...] = jnp.broadcast_to(scale, lanes)
        out_ref[...] = (xhat * p_ref[6:7, :] + p_ref[7:8, :]).astype(BF)


def post(x, att, w4, e, eb, r, params):
    n, d = x.shape
    ff = e.shape[1]
    fc = min(ff, 512)
    full = whole((n, d))
    thin = whole((n, 128))
    tall = pl.BlockSpec((n, fc), lambda j: (0, j))
    return pl.pallas_call(
        post_kernel,
        name="post",
        grid=(ff // fc,),
        in_specs=[
            full, full,
            pl.BlockSpec((1, d, d), lambda j: (3, 0, 0)),
            pl.BlockSpec((d, fc), lambda j: (0, j)),
            pl.BlockSpec((1, fc), lambda j: (0, j)),
            pl.BlockSpec((fc, d), lambda j: (j, 0)),
            whole(params.shape),
        ],
        out_specs=[full, full, thin, tall, tall, full, thin],
        out_shape=[
            jax.ShapeDtypeStruct((n, d), BF),
            jax.ShapeDtypeStruct((n, d), F32),
            jax.ShapeDtypeStruct((n, 128), F32),
            jax.ShapeDtypeStruct((n, ff), BF),
            jax.ShapeDtypeStruct((n, ff), BF),
            jax.ShapeDtypeStruct((n, d), F32),
            jax.ShapeDtypeStruct((n, 128), F32),
        ],
        scratch_shapes=[pltpu.VMEM((n, d), F32), pltpu.VMEM((n, d), BF), pltpu.VMEM((n, d), F32)],
        compiler_params=params_of(("arbitrary",)),
        cost_estimate=pl.CostEstimate(
            flops=2 * n * d * (d + 2 * ff), bytes_accessed=2 * d * (d + 2 * ff) + 4 * n * ff + 16 * n * d, transcendentals=2 * n * ff
        ),
    )(x, att, w4, e, eb, r, params)


def rows_sum(value):
    return jnp.sum(value, axis=0, keepdims=True)


def ffn_back_kernel(
    g_ref, xhat2_ref, scale2_ref, p_ref, act_ref, slope_ref, r_ref, e_ref, xhat1_ref, scale1_ref, att_ref, w_ref,
    gr_ref, ge_ref, geb_ref, dsum_ref, go_ref, datt_ref, small_ref,
    outer_ref, low_ref, total_ref,
):
    j = pl.program_id(0)

    @pl.when(j == 0)
    def _():
        g = g_ref[...].astype(F32)
        xhat = xhat2_ref[...]
        d_pre = norm_back(g * p_ref[6:7, :], xhat, scale2_ref[:, 0:1])
        outer = d_pre.astype(BF)
        outer_ref[...] = outer
        total_ref[...] = d_pre
        small_ref[0:1, :] = jnp.zeros_like(small_ref[0:1, :])
        small_ref[1:2, :] = jnp.zeros_like(small_ref[1:2, :])
        small_ref[5:6, :] = rows_sum(outer.astype(F32))
        small_ref[6:7, :] = rows_sum(g * xhat)
        small_ref[7:8, :] = rows_sum(g)
        low_ref[...] = (xhat1_ref[...] * p_ref[3:4, :] + p_ref[4:5, :]).astype(BF)

    outer = outer_ref[...]
    d_active = mm_nt(outer, r_ref[...])
    d_inner_full = d_active * slope_ref[...].astype(F32)
    d_inner = d_inner_full.astype(BF)
    gr_ref[...] = mm_tn(act_ref[...], outer).astype(BF)
    ge_ref[...] = mm_tn(low_ref[...], d_inner).astype(BF)
    geb_ref[...] = rows_sum(d_inner.astype(F32))
    total_ref[...] += mm_nt(d_inner, e_ref[...])

    @pl.when(j == pl.num_programs(0) - 1)
    def _():
        d_hidden = total_ref[...]
        xhat = xhat1_ref[...]
        d_summed = norm_back(d_hidden * p_ref[3:4, :], xhat, scale1_ref[:, 0:1])
        dsum_ref[...] = d_summed
        branch = d_summed.astype(BF)
        small_ref[2:3, :] = rows_sum(branch.astype(F32))
        small_ref[3:4, :] = rows_sum(d_hidden * xhat)
        small_ref[4:5, :] = rows_sum(d_hidden)
        go_ref[...] = mm_tn(att_ref[...], branch).astype(BF)
        datt_ref[...] = mm_nt(branch, w_ref[0]).astype(BF)


def ffn_back(g, saved, w4, e, r, params, ride=None):
    x, att, xhat1, scale1, act, slope, xhat2, scale2 = saved
    n, d = x.shape
    ff = e.shape[1]
    fc = min(ff, 512)
    full = whole((n, d))
    thin = whole((n, 128))
    tall = pl.BlockSpec((n, fc), lambda j: (0, j))
    e_spec = pl.BlockSpec((d, fc), lambda j: (0, j))
    r_spec = pl.BlockSpec((fc, d), lambda j: (j, 0))
    return stepped(
        ffn_back_kernel,
        ride,
        "ffn_back",
        ff // fc,
        (g, xhat2, scale2, params, act, slope, r, e, xhat1, scale1, att, w4),
        [
            full, full, thin, whole(params.shape), tall, tall, r_spec, e_spec, full, thin, full,
            pl.BlockSpec((1, d, d), lambda j: (3, 0, 0)),
        ],
        [
            r_spec, e_spec, pl.BlockSpec((1, fc), lambda j: (0, j)), full, whole((d, d)), full, whole((8, d)),
        ],
        [
            jax.ShapeDtypeStruct((ff, d), BF),
            jax.ShapeDtypeStruct((d, ff), BF),
            jax.ShapeDtypeStruct((1, ff), F32),
            jax.ShapeDtypeStruct((n, d), F32),
            jax.ShapeDtypeStruct((d, d), BF),
            jax.ShapeDtypeStruct((n, d), BF),
            jax.ShapeDtypeStruct((8, d), F32),
        ],
        [pltpu.VMEM((n, d), BF), pltpu.VMEM((n, d), BF), pltpu.VMEM((n, d), F32)],
        pl.CostEstimate(
            flops=4 * n * d * (d + 2 * ff), bytes_accessed=4 * d * (d + 2 * ff) + 4 * n * ff + 24 * n * d, transcendentals=0
        ),
    )


def input_back_kernel(others, x_ref, dq_ref, own_ref, *refs):
    other_refs = refs[:others]
    w_ref, dsum_ref, g3_ref, dx_ref, small_ref = refs[others:]
    j = pl.program_id(0)

    def step(grad, row):
        g3_ref[0] = mm_tn(x_ref[...], grad).astype(BF)
        if row is not None:
            small_ref[row : row + 1, :] = rows_sum(grad.astype(F32))
        return mm_nt(grad, w_ref[0])

    def joined(index):
        value = own_ref[index].astype(F32)
        for ref in other_refs:
            value = value + ref[index].astype(F32)
        return value.astype(BF)

    @pl.when(j == 0)
    def _():
        small_ref[...] = jnp.zeros_like(small_ref)
        dx_ref[...] = dsum_ref[...] + step(dq_ref[...], 0)

    @pl.when(j == 1)
    def _():
        dx_ref[...] += step(joined(0), None)

    @pl.when(j == 2)
    def _():
        dx_ref[...] += step(joined(1), 1)


def input_back(x, dq, own, others, w4, dsum):
    n, d = x.shape
    full = whole((n, d))
    return pl.pallas_call(
        partial(input_back_kernel, len(others)),
        name="input_back",
        grid=(3,),
        in_specs=[full, full, whole((2, n, d))]
        + [whole((2, n, d))] * len(others)
        + [pl.BlockSpec((1, d, d), lambda j: (j, 0, 0)), full],
        out_specs=[pl.BlockSpec((1, d, d), lambda j: (j, 0, 0)), full, whole((8, d))],
        out_shape=[
            jax.ShapeDtypeStruct((3, d, d), BF),
            jax.ShapeDtypeStruct((n, d), F32),
            jax.ShapeDtypeStruct((8, d), F32),
        ],
        compiler_params=params_of(("arbitrary",)),
        cost_estimate=pl.CostEstimate(flops=12 * n * d * d, bytes_accessed=12 * d * d + 16 * n * d, transcendentals=0),
    )(x, dq, own, *others, w4, dsum)


class Grid:
    def __init__(self, dp, seq):
        self.ny = max(seq // 2, 1)
        self.nc = seq // self.ny
        self.nx = self.ny if dp % self.ny == 0 else 1
        self.nz = dp // self.nx
        self.sizes = {"z": self.nz, "x": self.nx, "y": self.ny, "c": self.nc}

    def here(self):
        d = lax.axis_index("dp")
        s = lax.axis_index("seq")
        return {"z": d // self.nx, "x": lax.rem(d, self.nx), "y": s // self.nc, "c": lax.rem(s, self.nc)}

    def device(self, at):
        return (at["z"] * self.nx + at["x"], at["y"] * self.nc + at["c"])

    def shifted(self, me, axis, step):
        other = dict(me)
        other[axis] = lax.rem(me[axis] + step, self.sizes[axis])
        return other

    def shape(self):
        return (self.nz, self.nx, self.ny, self.nc)

    def peers(self):
        return [(axis, step) for axis in "zxyc" for step in range(1, self.sizes[axis])]

    def barrier(self, me):
        sem = pltpu.get_barrier_semaphore()
        for axis, step in self.peers():
            pl.semaphore_signal(
                sem, inc=1, device_id=self.device(self.shifted(me, axis, step)), device_id_type=MESH
            )
        pl.semaphore_wait(sem, len(self.peers()))


def picked(place, axes):
    return tuple(slice(None) if axis in axes else place[axis] for axis in "zxyc")


def fine_cuts_of(shapes):
    groups = []
    for group in cuts_of(shapes):
        if any(cut[3][1] % 256 for cut in group):
            groups.append(group)
            continue
        for part in range(2):
            groups.append(
                [
                    (number, lead, rows, (first + part * count // 2, count // 2))
                    for number, lead, rows, (first, count) in group
                ]
            )
    return groups


def cuts_of(shapes):
    groups = []
    for number, shape in enumerate(shapes):
        rows, columns = shape[-2:]
        lead = shape[0] if len(shape) == 3 else None
        if columns % 256:
            groups.append([(number, None, (0, rows), (0, columns))])
            continue
        if lead is not None and lead % 2 == 0:
            pieces = [(number, (k, k + 1), (0, rows), (0, columns)) for k in range(lead)]
        elif lead == 3:
            left, right = (0, columns // 2), (columns // 2, columns // 2)
            pieces = [(number, (0, 1), (0, rows), (0, columns)), (number, (1, 2), (0, rows), (0, columns))]
            pieces += [(number, (2, 3), (0, rows), left), (number, (2, 3), (0, rows), right)]
        elif columns % 1024 == 0:
            pieces = [(number, None, (0, rows), (k * columns // 4, columns // 4)) for k in range(4)]
        elif rows % 32 == 0:
            pieces = [(number, None, (k * rows // 4, rows // 4), (0, columns)) for k in range(4)]
        elif columns % 256 == 0:
            pieces = [(number, None, (0, rows), (k * columns // 2, columns // 2)) for k in range(2)]
        else:
            groups.append([(number, None, (0, rows), (0, columns))])
            continue
        groups += [pieces[k : k + 2] for k in range(0, len(pieces), 2)]
    return groups


def region(ref, shape, cut, index):
    _, lead, rows, columns = cut
    head = ()
    if len(shape) == 3:
        head = (slice(None) if lead is None else slice(*lead),)
    return ref.at[head + tuple(index) + (slice(rows[0], sum(rows)), slice(columns[0], sum(columns)))]


ORDERS = (("z", "x", "y", "c"), ("z", "y", "x", "c"))


class Sender:
    def __init__(self, grid, me, send_sem, recv_sem):
        self.grid, self.me, self.send_sem, self.recv_sem = grid, me, send_sem, recv_sem
        self.started = []

    def send(self, src, dst, axis, step):
        return self.send_to(src, dst, self.grid.device(self.grid.shifted(self.me, axis, step)))

    def send_to(self, src, dst, device):
        k = len(self.started)
        copy = pltpu.make_async_remote_copy(
            src_ref=src, dst_ref=dst, send_sem=self.send_sem.at[k], recv_sem=self.recv_sem.at[k],
            device_id=device, device_id_type=MESH,
        )
        copy.start()
        self.started.append(copy)
        return copy

    def finish(self):
        for copy in self.started:
            copy.wait_send()


def gather_turns(sender, shapes, srcs, dsts, own_sem):
    grid, me = sender.grid, sender.me
    groups = cuts_of(shapes)
    own = []
    first = []
    for group in groups:
        copies = []
        for cut in group:
            shape = shapes[cut[0]]
            src = region(srcs[cut[0]], shape, cut, ())
            dst = region(dsts[cut[0]], shape, cut, picked(me, ""))
            copies.append([sender.send(src, dst, "z", step) for step in range(1, grid.nz)])
        first.append(copies)
    for k in range(len(shapes)):
        head = (slice(None),) if len(shapes[k]) == 3 else ()
        copy = pltpu.make_async_copy(srcs[k], dsts[k].at[head + picked(me, "")], own_sem.at[k])
        copy.start()
        own.append(copy)
    for copy in own:
        copy.wait()
    yield
    stages = {0: first}
    total = len(groups)
    depth = len(ORDERS[0])
    for turn in range(total + depth - 1):
        for stage in range(1, depth):
            g = turn - (stage - 1)
            if not 0 <= g < total:
                continue
            copies = []
            for side, cut in enumerate(groups[g]):
                order = ORDERS[side % 2]
                for copy in stages[stage - 1][g][side]:
                    copy.wait_recv()
                block = region(dsts[cut[0]], shapes[cut[0]], cut, picked(me, order[:stage]))
                copies.append(
                    [sender.send(block, block, order[stage], step) for step in range(1, grid.sizes[order[stage]])]
                )
            stages.setdefault(stage, {})[g] = copies
        g = turn - (depth - 1)
        if 0 <= g < total:
            for copies in stages[depth - 1][g]:
                for copy in copies:
                    copy.wait_recv()
        yield


def gather_kernel(grid, shapes, *refs):
    count = len(shapes)
    me = grid.here()
    grid.barrier(me)
    sender = Sender(grid, me, *refs[2 * count : 2 * count + 2])
    for _ in gather_turns(sender, shapes, refs[:count], refs[count : 2 * count], refs[-1]):
        pass
    sender.finish()


def copies_in(grid, shapes):
    return sum(len(group) for group in cuts_of(shapes)) * len(grid.peers())


def gather(grid, arrays, name, collective_id):
    shapes = [a.shape for a in arrays]
    outs = [a.shape[:-2] + grid.shape() + a.shape[-2:] for a in arrays]
    count = copies_in(grid, shapes)
    got = pl.pallas_call(
        partial(gather_kernel, grid, shapes),
        name=name,
        in_specs=[pl.BlockSpec(memory_space=pltpu.VMEM)] * len(arrays),
        out_specs=[pl.BlockSpec(memory_space=pl.ANY)] * len(arrays),
        out_shape=[jax.ShapeDtypeStruct(s, a.dtype) for s, a in zip(outs, arrays)],
        scratch_shapes=[
            pltpu.SemaphoreType.DMA((count,)),
            pltpu.SemaphoreType.DMA((count,)),
            pltpu.SemaphoreType.DMA((len(arrays),)),
        ],
        compiler_params=pltpu.CompilerParams(
            collective_id=collective_id, has_side_effects=True, vmem_limit_bytes=VMEM_LIMIT
        ),
    )(*arrays)
    blocks = math.prod(grid.shape())
    return [o.reshape(a.shape[:-2] + (blocks * a.shape[-2], a.shape[-1])) for o, a in zip(got, arrays)]


def spread_small(table_ref, thin_refs, wide_refs, rows, blocks):
    lines = table_ref.shape[-2]
    table = table_ref[...].reshape(blocks * lines, 128)

    def picker(per, width):
        column = lax.broadcasted_iota(jnp.int32, (128, width), 1)
        scale = -(-(1 << 20) // per)
        rest = column - lax.shift_right_logical(column * scale, 20) * per
        hot = (lax.broadcasted_iota(jnp.int32, (128, width), 0) == rest).astype(F32).astype(BF)
        place = lax.broadcasted_iota(jnp.int32, (blocks, lines, width), 2)
        owner = lax.broadcasted_iota(jnp.int32, (blocks, lines, width), 0)
        return hot, lax.shift_right_logical(place * scale, 20) == owner

    thin_width = thin_refs[0].shape[-1]
    hot, keep = picker(rows, thin_width)
    wide = mm(table, hot).reshape(blocks, lines, thin_width)
    vectors = jnp.sum(jnp.where(keep, wide, 0.0), axis=0)
    for layer, ref in enumerate(thin_refs):
        ref[...] = vectors[layer * 16 : layer * 16 + ROWS]
    step = 1024
    for first in range(0, wide_refs[0].shape[-1], step):
        scale = -(-(1 << 20) // (4 * rows))
        column = lax.broadcasted_iota(jnp.int32, (128, step), 1) + first
        rest = column - lax.shift_right_logical(column * scale, 20) * (4 * rows)
        hot = (lax.broadcasted_iota(jnp.int32, (128, step), 0) == rest).astype(F32).astype(BF)
        place = lax.broadcasted_iota(jnp.int32, (blocks, lines, step), 2) + first
        owner = lax.broadcasted_iota(jnp.int32, (blocks, lines, step), 0)
        full = mm(table, hot).reshape(blocks, lines, step)
        part = jnp.sum(jnp.where(lax.shift_right_logical(place * scale, 20) == owner, full, 0.0), axis=0)
        for layer, ref in enumerate(wide_refs):
            ref[:, first : first + step] = part[layer * 16 + 8 : layer * 16 + 9]


def front_kernel(grid, shapes, *refs):
    count = len(shapes)
    srcs, refs = refs[:count], refs[count:]
    tokens_ref, refs = refs[0], refs[1:]
    fulls, refs = refs[: count - 1], refs[count - 1 :]
    x_ref, refs = refs[0], refs[1:]
    p1_ref, p2_ref, eb1_ref, eb2_ref, q_ref, kv_ref, far_ref, att_ref, lse_ref = refs[:9]
    out_ref, xhat1_ref, scale1_ref, act_ref, slope_ref, xhat2_ref, scale2_ref = refs[9:16]
    table_ref, w4_ref, r_ref, e_ref, hidden_ref, low_ref, total_ref = refs[16:23]
    send_sem, recv_sem, own_sem, load_sem = refs[23:]
    n, d = x_ref.shape
    ff = e_ref.shape[-1]
    me = grid.here()
    grid.barrier(me)
    sender = Sender(grid, me, send_sem, recv_sem)
    turns = gather_turns(sender, shapes, srcs, (table_ref,) + tuple(fulls), own_sem)
    left = [len(cuts_of(shapes)) + 4]

    def advance(steps=1):
        for _ in range(min(steps, left[0])):
            next(turns)
            left[0] -= 1

    def load(source, target, k):
        copy = pltpu.make_async_copy(source, target, load_sem.at[k])
        copy.start()
        return copy

    def joined(blocks):
        return blocks.astype(F32).reshape(-1, blocks.shape[-1]).astype(BF)

    advance(1)
    rows = tokens_ref.shape[1]
    crossed = sender.send(tokens_ref.at[1 - me["y"]], x_ref.at[pl.ds(rows, rows)], "y", 1)
    x_ref[pl.ds(0, rows), :] = tokens_ref[me["y"]]
    advance(4)
    blocks = math.prod(grid.shape())
    spread_small(table_ref, (p1_ref, p2_ref), (eb1_ref, eb2_ref), shapes[1][-2], blocks)
    advance(2)
    load(fulls[0], w4_ref, 0).wait()
    crossed.wait_recv()
    x = x_ref[...]
    kv_ref[0] = mm(x, joined(w4_ref[1])).astype(BF)
    kv_ref[1] = (mm(x, joined(w4_ref[2])) + p1_ref[1:2, :]).astype(BF)
    swapped = sender.send(kv_ref, far_ref, "c", 1)
    q_ref[...] = (mm(x, joined(w4_ref[0])) + p1_ref[0:1, :]).astype(BF)
    advance(1)
    swapped.wait_recv()
    for pair in range(d // (2 * HD)):
        lanes = slice(pair * 2 * HD, (pair + 1) * 2 * HD)
        kvs = [(r[0, :, lanes], r[1, :, lanes]) for r in (kv_ref, far_ref)]
        att_ref[:, lanes], lse_ref[:, lanes] = attend_pair(q_ref[:, lanes], kvs, None)
        if pair % 2:
            advance(1)
        if pair == 1:
            loads = [load(fulls[1], r_ref, 1)]
    loads.append(load(fulls[2], e_ref, 2))
    summed = x.astype(F32) + mm(att_ref[...], joined(w4_ref[3])) + p1_ref[2:3, :]
    xhat, scale = normed(summed)
    xhat1_ref[...] = xhat
    scale1_ref[...] = jnp.broadcast_to(scale, scale1_ref.shape)
    hidden = xhat * p1_ref[3:4, :] + p1_ref[4:5, :]
    hidden_ref[...] = hidden
    low_ref[...] = hidden.astype(BF)
    for copy in loads:
        copy.wait()
    step = 512
    for first in range(0, ff, step):
        part = slice(first, first + step)
        active, slope = gelu_pair(mm(low_ref[...], joined(e_ref[..., part])) + eb1_ref[:, part])
        active = active.astype(BF)
        act_ref[:, part] = active
        slope_ref[:, part] = slope.astype(BF)
        more = mm(active, r_ref[...].reshape(ff, d)[part, :])
        total_ref[...] = more if first == 0 else total_ref[...] + more
        if first // step % 2:
            advance(1)
    pre = hidden_ref[...] + total_ref[...] + p1_ref[5:6, :]
    xhat, scale = normed(pre)
    xhat2_ref[...] = xhat
    scale2_ref[...] = jnp.broadcast_to(scale, scale2_ref.shape)
    out_ref[...] = (xhat * p1_ref[6:7, :] + p1_ref[7:8, :]).astype(BF)
    advance(left[0])
    sender.finish()


def front(grid, arrays, tokens, name, collective_id):
    shapes = [a.shape for a in arrays]
    n, d = tokens.shape[0] * tokens.shape[1], tokens.shape[2]
    ff = arrays[3].shape[1]
    count = copies_in(grid, shapes) + 2
    vmem = pl.BlockSpec(memory_space=pltpu.VMEM)
    hbm = pl.BlockSpec(memory_space=pl.ANY)
    fulls = [jax.ShapeDtypeStruct(a.shape[:-2] + grid.shape() + a.shape[-2:], BF) for a in arrays[1:]]
    local = [
        ((n, d), BF),
        ((ROWS, d), F32), ((ROWS, d), F32), ((1, ff), F32), ((1, ff), F32),
        ((n, d), BF), ((2, n, d), BF), ((2, n, d), BF), ((n, d), BF), ((n, d), F32),
        ((n, d), BF), ((n, d), F32), ((n, 128), F32), ((n, ff), BF), ((n, ff), BF), ((n, d), F32), ((n, 128), F32),
    ]
    got = pl.pallas_call(
        partial(front_kernel, grid, shapes),
        name=name,
        in_specs=[vmem] * (len(arrays) + 1),
        out_specs=[hbm] * len(fulls) + [vmem] * len(local),
        out_shape=fulls + [jax.ShapeDtypeStruct(*s) for s in local],
        scratch_shapes=[
            pltpu.VMEM(grid.shape() + arrays[0].shape, BF),
            pltpu.VMEM(fulls[0].shape, BF),
            pltpu.VMEM(fulls[1].shape, BF),
            pltpu.VMEM(fulls[2].shape, BF),
            pltpu.VMEM((n, d), F32),
            pltpu.VMEM((n, d), BF),
            pltpu.VMEM((n, d), F32),
            pltpu.SemaphoreType.DMA((count,)),
            pltpu.SemaphoreType.DMA((count,)),
            pltpu.SemaphoreType.DMA((len(arrays),)),
            pltpu.SemaphoreType.DMA((3,)),
        ],
        compiler_params=pltpu.CompilerParams(
            collective_id=collective_id, has_side_effects=True, vmem_limit_bytes=VMEM_LIMIT
        ),
    )(*arrays, tokens)
    blocks = math.prod(grid.shape())
    weights = [
        o.reshape(a.shape[:-2] + (blocks * a.shape[-2], a.shape[-1])) for o, a in zip(got, arrays[1:])
    ]
    return weights, got[len(fulls) :]


BACK_ORDERS = (("c", "x", "y", "z"), ("c", "y", "x", "z"))


def left_axes(order, stage):
    return [axis for axis in "zxyc" if axis not in order[:stage]]


class Scatter:
    def __init__(self, grid, plan, refs):
        shapes, layouts = plan.shapes, plan.layouts
        count = len(shapes)
        self.grid, self.shapes = grid, shapes
        self.me = grid.here()
        self.srcs, self.outs = refs[:count], refs[count : 2 * count]
        held = refs[2 * count : -3]
        send_sem, recv_sem, own_sem = refs[-3:]
        self.groups = fine_cuts_of(shapes)
        self.near = {peer: grid.shifted(self.me, *peer) for peer in grid.peers()}
        devices = {peer: grid.device(at) for peer, at in self.near.items()}
        self.buffers, self.own, self.flights = {}, {}, {}
        position = piece = number = 0
        for g, group in enumerate(self.groups):
            for side, cut in enumerate(group):
                order = BACK_ORDERS[side % 2]
                head = (slice(None),) if self.lead_of(cut) else ()
                for stage in range(len(layouts[piece])):
                    buf = held[position]
                    position += 1
                    self.buffers[g, side, stage] = buf
                    axis = order[stage]
                    copies = []
                    for step in range(1, grid.sizes[axis]):
                        there = self.near[axis, step]
                        if stage == 0:
                            src = region(self.srcs[cut[0]], shapes[cut[0]], cut, picked(there, "zxy"))
                        else:
                            index = tuple(
                                there[a] if a == axis else slice(None) for a in left_axes(order, stage)
                            )
                            src = self.buffers[g, side, stage - 1].at[(0,) + head + index]
                        slot = step - 1 if stage == len(layouts[piece]) - 1 else step
                        copies.append(
                            pltpu.make_async_remote_copy(
                                src_ref=src, dst_ref=buf.at[slot],
                                send_sem=send_sem.at[number], recv_sem=recv_sem.at[number],
                                device_id=devices[axis, step], device_id_type=MESH,
                            )
                        )
                        number += 1
                    self.flights[g, side, stage] = copies
                src = region(self.srcs[cut[0]], shapes[cut[0]], cut, picked(self.me, "zxy"))
                self.own[g, side] = pltpu.make_async_copy(src, self.buffers[g, side, 0].at[0], own_sem.at[piece])
                piece += 1

    def lead_of(self, cut):
        return len(self.shapes[cut[0]]) == 3

    def start(self):
        self.grid.barrier(self.me)
        for g, group in enumerate(self.groups):
            for side in range(len(group)):
                self.own[g, side].start()
                for copy in self.flights[g, side, 0]:
                    copy.start()

    def turn(self, number):
        depth = 4
        for stage in range(depth):
            g = number - stage
            if not 0 <= g < len(self.groups):
                continue
            for side, cut in enumerate(self.groups[g]):
                order = BACK_ORDERS[side % 2]
                buf = self.buffers[g, side, stage]
                for copy in self.flights[g, side, stage]:
                    copy.wait_recv()
                if stage == 0:
                    self.own[g, side].wait()
                    add_into(buf)
                else:
                    source = self.buffers[g, side, stage - 1]
                    rest = left_axes(order, stage)
                    if stage == depth - 1:
                        head = (slice(None),) if self.lead_of(cut) else ()
                        total = source[(0,) + head + tuple(self.me[a] for a in rest)].astype(F32)
                        for slot in range(buf.shape[0]):
                            total = total + buf[slot].astype(F32)
                        region(self.outs[cut[0]], self.shapes[cut[0]], cut, ())[...] = total
                        continue
                    merge(source, buf, self.me, rest, order[stage], self.lead_of(cut))
                for copy in self.flights[g, side, stage + 1]:
                    copy.start()

    def finish(self):
        for copies in self.flights.values():
            for copy in copies:
                copy.wait_send()

    def turns(self):
        steps = [partial(self.turn, k) for k in range(len(self.groups) + 3)]
        return [self.start] + steps + [self.finish]


def unflat(number, sizes):
    index = []
    for size in reversed(sizes):
        index.append(lax.rem(number, size))
        number = number // size
    return tuple(reversed(index))


def add_into(buf):
    flat = buf.shape[1:-2]

    def body(i, carry):
        index = unflat(i, flat)
        value = buf[(0,) + index].astype(F32)
        for slot in range(1, buf.shape[0]):
            value = value + buf[(slot,) + index].astype(F32)
        buf[(0,) + index] = value.astype(buf.dtype)
        return carry

    lax.fori_loop(0, math.prod(flat), body, 0)


def merge(source, buf, me, axes, axis, lead):
    flat = buf.shape[1:-2]
    where = axes.index(axis) + (1 if lead else 0)

    def body(i, carry):
        index = unflat(i, flat)
        wide = index[:where] + (me[axis],) + index[where:]
        value = source[(0,) + wide].astype(F32)
        for slot in range(1, buf.shape[0]):
            value = value + buf[(slot,) + index].astype(F32)
        buf[(0,) + index] = value.astype(buf.dtype)
        return carry

    lax.fori_loop(0, math.prod(flat), body, 0)


class ScatterPlan:
    def __init__(self, grid, arrays):
        blocks = math.prod(grid.shape())
        self.shapes = [a.shape[:-2] + (a.shape[-2] // blocks, a.shape[-1]) for a in arrays]
        self.views = [a.reshape(s[:-2] + grid.shape() + s[-2:]) for a, s in zip(arrays, self.shapes)]
        self.layouts = []
        self.scratch = []
        for group in fine_cuts_of(self.shapes):
            for side, cut in enumerate(group):
                shape = self.shapes[cut[0]]
                order = BACK_ORDERS[side % 2]
                head = ()
                if len(shape) == 3:
                    head = (shape[0] if cut[1] is None else cut[1][1] - cut[1][0],)
                stages = []
                for stage in range(4):
                    rest = left_axes(order, stage + 1)
                    slots = grid.sizes[order[stage]] - (1 if stage == 3 else 0)
                    stages.append((slots,) + head + tuple(grid.sizes[a] for a in rest) + (cut[2][1], cut[3][1]))
                self.layouts.append(stages)
                self.scratch += [pltpu.VMEM(s, arrays[cut[0]].dtype) for s in stages]
        count = len(self.layouts) * len(grid.peers())
        self.scratch += [
            pltpu.SemaphoreType.DMA((count,)),
            pltpu.SemaphoreType.DMA((count,)),
            pltpu.SemaphoreType.DMA((len(self.layouts),)),
        ]
        self.outs = [jax.ShapeDtypeStruct(s, F32) for s in self.shapes]


def scatter(grid, arrays, name, collective_id):
    plan = ScatterPlan(grid, arrays)

    def kernel(*refs):
        for step in Scatter(grid, plan, refs).turns():
            step()

    return pl.pallas_call(
        kernel,
        name=name,
        in_specs=[pl.BlockSpec(memory_space=pl.ANY)] * len(arrays),
        out_specs=[pl.BlockSpec(memory_space=pltpu.VMEM)] * len(arrays),
        out_shape=plan.outs,
        scratch_shapes=plan.scratch,
        compiler_params=pltpu.CompilerParams(
            collective_id=collective_id, has_side_effects=True, vmem_limit_bytes=VMEM_LIMIT
        ),
    )(*plan.views)


def stepped(body, ride, name, steps, args, in_specs, out_specs, out_shape, scratch, cost):
    if ride is None:
        out = pl.pallas_call(
            body, name=name, grid=(steps,), in_specs=in_specs, out_specs=out_specs, out_shape=out_shape,
            scratch_shapes=scratch, compiler_params=params_of(("arbitrary",)), cost_estimate=cost,
        )(*args)
        return out, ()
    grid, arrays, collective_id = ride
    plan = ScatterPlan(grid, arrays)
    count, riders = len(args), len(arrays)
    results, locals_ = len(out_shape), len(scratch)

    def kernel(*refs):
        ins, refs = refs[:count], refs[count:]
        views, refs = refs[:riders], refs[riders:]
        outs, refs = refs[:results], refs[results:]
        sums, refs = refs[:riders], refs[riders:]
        own, refs = refs[:locals_], refs[locals_:]
        turns = Scatter(grid, plan, views + sums + refs).turns()
        j = pl.program_id(0)
        for k, turn in enumerate(turns[:steps]):
            pl.when(j == k)(turn)
        body(*ins, *outs, *own)

        @pl.when(j == steps - 1)
        def _():
            for turn in turns[steps:]:
                turn()

    out = pl.pallas_call(
        kernel,
        name=name,
        grid=(steps,),
        in_specs=in_specs + [pl.BlockSpec(memory_space=pl.ANY)] * riders,
        out_specs=out_specs + [whole(s.shape) for s in plan.outs],
        out_shape=out_shape + plan.outs,
        scratch_shapes=scratch + plan.scratch,
        compiler_params=pltpu.CompilerParams(
            dimension_semantics=("arbitrary",), collective_id=collective_id, has_side_effects=True,
            vmem_limit_bytes=VMEM_LIMIT,
        ),
        cost_estimate=cost,
    )(*args, *plan.views)
    return out[:results], out[results:]


ROWS = 8
ROW_AT = (1, 4, 6, 7, 8, 12, 13, 14)


def pack_small(layers):
    parts = []
    for params in layers:
        parts += [params[k] for k in ROW_AT] + [params[10]]
    flat = jnp.concatenate(parts)
    size = 1024 * -(-flat.shape[0] // 1024)
    return jnp.pad(flat, (0, size - flat.shape[0])).reshape(size // 128, 128)


def small_table(layers):
    lines = []
    for params in layers:
        for k in ROW_AT + (10,):
            lines.append(jnp.pad(params[k], (0, 128 - params[k].shape[0])))
        lines += [jnp.zeros((128,), BF)] * 7
    return jnp.stack(lines)


def unpack_small(full, blocks, rows, layers):
    per = full.shape[0] // blocks * full.shape[1]
    flat = full.reshape(blocks, per)
    out = []
    width = (ROWS + 4) * rows
    for layer in range(layers):
        part = flat[:, layer * width : (layer + 1) * width].astype(F32)
        thin = part[:, : ROWS * rows].reshape(blocks, ROWS, rows).transpose(1, 0, 2).reshape(ROWS, blocks * rows)
        out.append((thin, part[:, ROWS * rows :].reshape(1, blocks * 4 * rows)))
    return out


def pack_grads(grads, blocks, rows):
    parts = []
    for thin, wide in grads:
        parts.append(thin.reshape(ROWS, blocks, rows).transpose(1, 0, 2).reshape(blocks, ROWS * rows))
        parts.append(wide.reshape(blocks, 4 * rows))
    flat = jnp.concatenate(parts, axis=1)
    size = 1024 * -(-flat.shape[1] // 1024)
    return jnp.pad(flat, ((0, 0), (0, size - flat.shape[1]))).reshape(blocks * (size // 128), 128)


def on_device(grid, tokens, early, cot_backbone, cot_head, lengths, cls_pos, *weights):
    layers = (weights[:15], weights[15:])
    members = lax.axis_size("seq")
    blocks = math.prod(grid.shape())
    seqs, rows, width = tokens.shape
    half = members // seqs
    spot = lax.axis_index("seq")
    mine = spot // half
    swap = [(i, (i + half) % members) for i in range(members)]
    far = lax.rem(spot + half, members)
    masked = rows * members > MIN_LEN

    def spread(value):
        kept = lax.dynamic_index_in_dim(value, mine, 0, keepdims=False)
        sent = lax.dynamic_index_in_dim(value, 1 - mine, 0, keepdims=False)
        return jnp.concatenate([kept, lax.ppermute(sent, "seq", swap)], axis=0)

    def cross(value):
        return lax.ppermute(value[rows:], "seq", swap)

    def collect(value, got):
        kept = value[:rows]
        return jnp.where(mine == 0, jnp.stack([kept, got]), jnp.stack([got, kept]))

    def around(value, step):
        pairs = [(i, i // half * half + (i % half + step) % half) for i in range(members)]
        return lax.ppermute(value, "seq", pairs)

    length = lax.dynamic_index_in_dim(lengths, mine, 0, keepdims=False)
    cls = lax.dynamic_index_in_dim(cls_pos, mine, 0, keepdims=False)
    line = jnp.arange(rows, dtype=jnp.int32)
    positions = jnp.concatenate([spot * rows + line, far * rows + line])
    is_cls = (positions == cls)[:, None]
    valid = (positions < length)[:, None]
    biases = None
    if masked:
        steps = []
        for step in range(half):
            member = mine * half + lax.rem(lax.rem(spot, half) - step + half, half)
            other = lax.rem(member + half, members)
            place = jnp.concatenate([member * rows + line, other * rows + line])
            steps.append(jnp.where(place < length, 0.0, NEG)[None, :])
        biases = jnp.stack(steps)

    x_early = spread(early)
    g_back = spread(cot_backbone)
    g_head = spread(cot_head)
    if masked:
        g_back = jnp.where(valid, g_back, jnp.zeros_like(g_back))
        g_head = jnp.where(valid, g_head, jnp.zeros_like(g_head))

    shard = layers[0][0].shape[0]
    stacked = [jnp.stack([p[0], p[2], p[3], p[5]]) for p in layers]
    fused = shard % 8 == 0 and half == 2 and not masked
    if fused:
        travel = [small_table(layers)]
        for k in range(2):
            travel += [stacked[k], layers[k][11], layers[k][9]]
        (w4_back, r_back, e_back, w4_head, r_head, e_head), kept = front(grid, travel, tokens, "front", 0)
        x_back, kept = kept[0], kept[1:]
        p_back, p_head, eb_back, eb_head, q, kv, far_kv, att, lse, back_low = kept[:10]
        back_kept = (q, [kv, far_kv], lse, (x_back, att) + tuple(kept[10:]))
    else:
        x_back = spread(tokens)
        small = pack_small(layers)
        w4_back, e_back, r_back, small_full = gather(
            grid, [stacked[0], layers[0][9], layers[0][11], small], "gather_back", 0
        )
        w4_head, e_head, r_head = gather(grid, [stacked[1], layers[1][9], layers[1][11]], "gather_head", 1)
        (p_back, eb_back), (p_head, eb_head) = unpack_small(small_full, blocks, shard, 2)

    def forward(x, w4, e, r, params, eb, held=None):
        q, kv = qkv(x, w4, params)
        kvs = [kv] + [around(kv, step) for step in range(1, half)]
        att, lse = attend(q, kvs, biases)
        if held is not None:
            att, held = lax.optimization_barrier((att, held))
        out, xhat1, scale1, act, slope, xhat2, scale2 = post(x, att, w4, e, eb, r, params)
        return out, (q, kvs, lse, (x, att, xhat1, scale1, act, slope, xhat2, scale2)), held

    def backward(g, kept, w4, e, r, params, before, number, held):
        q, kvs, lse, saved = kept
        x, att = saved[:2]
        ride = None if before is None else (grid, before, number)
        (gr, ge, geb, dsum, go, datt, small_a), sums = ffn_back(g, saved, w4, e, r, params, ride)
        datt, held = lax.optimization_barrier((datt, held))
        dq, dkvs, wide = attend_back(q, datt, att, lse, kvs, biases, (grid, [ge, gr], number + 1))
        others = [around(dkvs[step], half - step) for step in range(1, half)]
        g3, dx, small_b = input_back(x, dq, dkvs[0], others, w4, dsum)
        return dx, [g3, go[None]], (small_a + small_b, geb), wide, sums, held

    if not fused:
        back_low, back_kept, _ = forward(x_back, w4_back, e_back, r_back, p_back, eb_back)
    head_in = jnp.where(is_cls, back_low, x_early)
    head_low, head_kept, back_far = forward(head_in, w4_head, e_head, r_head, p_head, eb_head, cross(back_low))
    dx_head, narrow_head, small_head, (seh, srh), _, head_far = backward(
        g_head, head_kept, w4_head, e_head, r_head, p_head, None, 2, cross(head_low)
    )
    early_low = jnp.where(is_cls, 0.0, dx_head).astype(BF)
    g_mixed = g_back.astype(F32) + jnp.where(is_cls, dx_head, 0.0)
    dx_back, narrow_back, small_back, (seb, srb), (s3h, soh), early_far = backward(
        g_mixed, back_kept, w4_back, e_back, r_back, p_back, narrow_head, 4, cross(early_low)
    )
    packed = pack_grads([small_back, small_head], blocks, shard)
    s3b, sob, small_sum = scatter(grid, narrow_back + [packed], "scatter_back", 6)

    back_grad = dx_back.astype(BF)
    flat = small_sum.reshape(-1)

    def layer_grads(layer, s3, so, se, sr):
        base = layer * (ROWS + 4) * shard
        thin = [flat[base + k * shard : base + (k + 1) * shard] for k in range(ROWS)]
        wide = flat[base + ROWS * shard : base + (ROWS + 4) * shard]
        return (
            s3[0], thin[0], s3[1], s3[2], thin[1], so[0], thin[2], thin[3], thin[4],
            se, wide, sr, thin[5], thin[6], thin[7],
        )

    return (
        collect(back_low, back_far),
        collect(head_low, head_far),
        collect(back_grad, cross(back_grad)),
        collect(early_low, early_far),
    ) + layer_grads(0, s3b, sob, seb, srb) + layer_grads(1, s3h, soh, seh, srh)


def solution(mesh):
    rows = P("dp", "seq", None)
    wide = P(("dp", "seq"), None)
    thin = P(("dp", "seq"))
    layer = tuple(thin if k in (1, 4, 6, 7, 8, 10, 12, 13, 14) else wide for k in range(15))
    grid = Grid(mesh.shape["dp"], mesh.shape["seq"])
    return jax.shard_map(
        partial(on_device, grid),
        mesh=mesh,
        in_specs=(rows,) * 4 + (P("dp"),) * 2 + layer + layer,
        out_specs=(rows,) * 4 + layer + layer,
        check_vma=False,
    )
```

```python
from functools import partial
import math

import jax
import jax.numpy as jnp
from jax import lax
from jax.experimental import pallas as pl
from jax.experimental.pallas import tpu as pltpu
from jax.sharding import PartitionSpec as P

H = 12
HD = 64
EPS = 1e-12
NEG = -1e30
MIN_LEN = 1024
BF = jnp.bfloat16
F32 = jnp.float32
MESH = pl.DeviceIdType.MESH
VMEM_LIMIT = 60 * 1024 * 1024


def mm(left, right):
    return lax.dot_general(left, right, (((1,), (0,)), ((), ())), preferred_element_type=F32)


def mm_nt(left, right):
    return lax.dot_general(left, right, (((1,), (1,)), ((), ())), preferred_element_type=F32)


def mm_tn(left, right):
    return lax.dot_general(left, right, (((0,), (0,)), ((), ())), preferred_element_type=F32)


def whole(shape):
    return pl.BlockSpec(shape, lambda *_: (0,) * len(shape))


def params_of(semantics):
    return pltpu.CompilerParams(dimension_semantics=semantics, vmem_limit_bytes=VMEM_LIMIT)


def qkv_kernel(x_ref, w_ref, p_ref, q_ref, kv_ref):
    j = pl.program_id(0)
    out = mm(x_ref[...], w_ref[0])

    @pl.when(j == 0)
    def _():
        q_ref[...] = (out + p_ref[0:1, :]).astype(BF)

    @pl.when(j == 1)
    def _():
        kv_ref[0] = out.astype(BF)

    @pl.when(j == 2)
    def _():
        kv_ref[0] = (out + p_ref[1:2, :]).astype(BF)


def qkv(x, w4, params):
    n, d = x.shape
    return pl.pallas_call(
        qkv_kernel,
        name="qkv",
        grid=(3,),
        in_specs=[
            whole((n, d)),
            pl.BlockSpec((1, d, d), lambda j: (j, 0, 0)),
            whole(params.shape),
        ],
        out_specs=[
            whole((n, d)),
            pl.BlockSpec((1, n, d), lambda j: (jnp.maximum(j - 1, 0), 0, 0)),
        ],
        out_shape=[
            jax.ShapeDtypeStruct((n, d), BF),
            jax.ShapeDtypeStruct((2, n, d), BF),
        ],
        compiler_params=params_of(("arbitrary",)),
        cost_estimate=pl.CostEstimate(flops=6 * n * d * d, bytes_accessed=6 * d * d + 8 * n * d, transcendentals=0),
    )(x, w4, params)


def half_masks(n):
    lane = lax.broadcasted_iota(jnp.int32, (n, 2 * HD), 1)
    return lane < HD


def attend_pair(q, kvs, biases):
    n = q.shape[0]
    low = half_masks(n)
    q = q * jnp.asarray(HD**-0.5, BF)
    outs = []
    logs = []
    for side in range(2):
        qm = jnp.where(low if side == 0 else ~low, q, jnp.zeros_like(q))
        scores = []
        for t, (key, _) in enumerate(kvs):
            s = mm_nt(qm, key)
            if biases is not None:
                s = s + biases[t]
            scores.append(s)
        top = scores[0].max(axis=-1, keepdims=True)
        for s in scores[1:]:
            top = jnp.maximum(top, s.max(axis=-1, keepdims=True))
        total = jnp.zeros((n, 1), F32)
        numer = jnp.zeros((n, 2 * HD), F32)
        for t, (_, value) in enumerate(kvs):
            weight = jnp.exp(scores[t] - top)
            total = total + weight.sum(axis=-1, keepdims=True)
            numer = numer + mm(weight.astype(BF), value)
        outs.append(numer / total)
        logs.append(top + jnp.log(total))
    return jnp.where(low, outs[0], outs[1]).astype(BF), jnp.where(low, logs[0], logs[1])


def attend_kernel(pieces, masked, *refs):
    q_ref = refs[0]
    kv_refs = refs[1 : 1 + pieces]
    refs = refs[1 + pieces :]
    biases = None
    if masked:
        biases, refs = [refs[0][t] for t in range(pieces)], refs[1:]
    att_ref, lse_ref = refs
    att_ref[...], lse_ref[...] = attend_pair(q_ref[...], [(r[0], r[1]) for r in kv_refs], biases)


def attend(q, kvs, biases):
    n, d = q.shape
    pieces = len(kvs)
    masked = biases is not None
    pair = 2 * HD
    col = pl.BlockSpec((n, pair), lambda j: (0, j))
    kv_spec = pl.BlockSpec((2, n, pair), lambda j: (0, 0, j))
    extra = (biases,) if masked else ()
    return pl.pallas_call(
        partial(attend_kernel, pieces, masked),
        name="attend",
        grid=(d // pair,),
        in_specs=[col] + [kv_spec] * pieces + [whole(b.shape) for b in extra],
        out_specs=[col, col],
        out_shape=[jax.ShapeDtypeStruct((n, d), BF), jax.ShapeDtypeStruct((n, d), F32)],
        compiler_params=params_of(("arbitrary",)),
        cost_estimate=pl.CostEstimate(
            flops=4 * n * n * pieces * d, bytes_accessed=(8 + 4 * pieces) * n * d, transcendentals=n * n * pieces * H
        ),
    )(q, *kvs, *extra)


def attend_back_kernel(pieces, masked, *refs):
    q_ref, do_ref, att_ref, lse_ref = refs[:4]
    kv_refs = refs[4 : 4 + pieces]
    refs = refs[4 + pieces :]
    bias_ref = None
    if masked:
        bias_ref, refs = refs[0], refs[1:]
    dq_ref = refs[0]
    dkv_refs = refs[1:]
    n = q_ref.shape[0]
    scale = HD**-0.5
    low = half_masks(n)
    q = q_ref[...] * jnp.asarray(scale, BF)
    do = do_ref[...]
    prod = do.astype(F32) * att_ref[...].astype(F32)
    dq = jnp.zeros((n, 2 * HD), F32)
    qms, doms, deltas, lses = [], [], [], []
    for side in range(2):
        mask = low if side == 0 else ~low
        qms.append(jnp.where(mask, q, jnp.zeros_like(q)))
        doms.append(jnp.where(mask, do, jnp.zeros_like(do)))
        deltas.append(jnp.sum(jnp.where(mask, prod, 0.0), axis=-1, keepdims=True))
        lses.append(lse_ref[:, side * HD : side * HD + 1])
    dqs = [jnp.zeros((n, 2 * HD), F32) for _ in range(2)]
    for t in range(pieces):
        k = kv_refs[t][0]
        v = kv_refs[t][1]
        dk = jnp.zeros((n, 2 * HD), F32)
        dv = jnp.zeros((n, 2 * HD), F32)
        for side in range(2):
            s = mm_nt(qms[side], k)
            if masked:
                s = s + bias_ref[t]
            p = jnp.exp(s - lses[side])
            dp = mm_nt(doms[side], v)
            ds = (p * (dp - deltas[side])).astype(BF)
            dv = dv + mm_tn(p.astype(BF), doms[side])
            dk = dk + mm_tn(ds, qms[side])
            dqs[side] = dqs[side] + mm(ds, k)
        dkv_refs[t][0] = dk.astype(BF)
        dkv_refs[t][1] = dv.astype(BF)
    dq_ref[...] = (jnp.where(low, dqs[0], dqs[1]) * scale).astype(BF)


def attend_back(q, do, att, lse, kvs, biases, ride=None):
    n, d = q.shape
    pieces = len(kvs)
    masked = biases is not None
    pair = 2 * HD
    col = pl.BlockSpec((n, pair), lambda j: (0, j))
    kv_spec = pl.BlockSpec((2, n, pair), lambda j: (0, 0, j))
    extra = (biases,) if masked else ()
    out, sums = stepped(
        partial(attend_back_kernel, pieces, masked),
        ride,
        "attend_back",
        d // pair,
        (q, do, att, lse, *kvs, *extra),
        [col] * 4 + [kv_spec] * pieces + [whole(b.shape) for b in extra],
        [col] + [kv_spec] * pieces,
        [jax.ShapeDtypeStruct((n, d), BF)] + [jax.ShapeDtypeStruct((2, n, d), BF)] * pieces,
        [],
        pl.CostEstimate(
            flops=10 * n * n * pieces * d, bytes_accessed=(12 + 8 * pieces) * n * d, transcendentals=n * n * pieces * H
        ),
    )
    return out[0], out[1:], sums


def normed(value):
    mean = jnp.mean(value, axis=-1, keepdims=True)
    centred = value - mean
    spread = jnp.mean(centred * centred, axis=-1, keepdims=True)
    scale = lax.rsqrt(spread + EPS)
    return centred * scale, scale


def norm_back(grad, xhat, scale):
    mean_grad = jnp.mean(grad, axis=-1, keepdims=True)
    mean_dot = jnp.mean(grad * xhat, axis=-1, keepdims=True)
    return scale * (grad - mean_grad - xhat * mean_dot)


def gelu_pair(value):
    cdf = 0.5 + 0.5 * lax.erf(value * (0.5**0.5))
    pdf = jnp.exp(-0.5 * value * value) * ((2.0 * math.pi) ** -0.5)
    return value * cdf, cdf + value * pdf


def post_kernel(
    x_ref, att_ref, w_ref, e_ref, eb_ref, r_ref, p_ref,
    out_ref, xhat1_ref, scale1_ref, act_ref, slope_ref, xhat2_ref, scale2_ref,
    hidden_ref, low_ref, total_ref,
):
    j = pl.program_id(0)
    lanes = scale1_ref.shape

    @pl.when(j == 0)
    def _():
        summed = x_ref[...].astype(F32) + mm(att_ref[...], w_ref[0]) + p_ref[2:3, :]
        xhat, scale = normed(summed)
        xhat1_ref[...] = xhat
        scale1_ref[...] = jnp.broadcast_to(scale, lanes)
        hidden = xhat * p_ref[3:4, :] + p_ref[4:5, :]
        hidden_ref[...] = hidden
        low_ref[...] = hidden.astype(BF)
        total_ref[...] = jnp.zeros_like(total_ref)

    inner = mm(low_ref[...], e_ref[...]) + eb_ref[...]
    active, slope = gelu_pair(inner)
    active = active.astype(BF)
    act_ref[...] = active
    slope_ref[...] = slope.astype(BF)
    total_ref[...] += mm(active, r_ref[...])

    @pl.when(j == pl.num_programs(0) - 1)
    def _():
        pre = hidden_ref[...] + total_ref[...] + p_ref[5:6, :]
        xhat, scale = normed(pre)
        xhat2_ref[...] = xhat
        scale2_ref[...] = jnp.broadcast_to(scale, lanes)
        out_ref[...] = (xhat * p_ref[6:7, :] + p_ref[7:8, :]).astype(BF)


def post(x, att, w4, e, eb, r, params):
    n, d = x.shape
    ff = e.shape[1]
    fc = min(ff, 512)
    full = whole((n, d))
    thin = whole((n, 128))
    tall = pl.BlockSpec((n, fc), lambda j: (0, j))
    return pl.pallas_call(
        post_kernel,
        name="post",
        grid=(ff // fc,),
        in_specs=[
            full, full,
            pl.BlockSpec((1, d, d), lambda j: (3, 0, 0)),
            pl.BlockSpec((d, fc), lambda j: (0, j)),
            pl.BlockSpec((1, fc), lambda j: (0, j)),
            pl.BlockSpec((fc, d), lambda j: (j, 0)),
            whole(params.shape),
        ],
        out_specs=[full, full, thin, tall, tall, full, thin],
        out_shape=[
            jax.ShapeDtypeStruct((n, d), BF),
            jax.ShapeDtypeStruct((n, d), F32),
            jax.ShapeDtypeStruct((n, 128), F32),
            jax.ShapeDtypeStruct((n, ff), BF),
            jax.ShapeDtypeStruct((n, ff), BF),
            jax.ShapeDtypeStruct((n, d), F32),
            jax.ShapeDtypeStruct((n, 128), F32),
        ],
        scratch_shapes=[pltpu.VMEM((n, d), F32), pltpu.VMEM((n, d), BF), pltpu.VMEM((n, d), F32)],
        compiler_params=params_of(("arbitrary",)),
        cost_estimate=pl.CostEstimate(
            flops=2 * n * d * (d + 2 * ff), bytes_accessed=2 * d * (d + 2 * ff) + 4 * n * ff + 16 * n * d, transcendentals=2 * n * ff
        ),
    )(x, att, w4, e, eb, r, params)


def rows_sum(value):
    return jnp.sum(value, axis=0, keepdims=True)


def ffn_back_kernel(
    g_ref, xhat2_ref, scale2_ref, p_ref, act_ref, slope_ref, r_ref, e_ref, xhat1_ref, scale1_ref, att_ref, w_ref,
    gr_ref, ge_ref, geb_ref, dsum_ref, go_ref, datt_ref, small_ref,
    outer_ref, low_ref, total_ref,
):
    j = pl.program_id(0)

    @pl.when(j == 0)
    def _():
        g = g_ref[...].astype(F32)
        xhat = xhat2_ref[...]
        d_pre = norm_back(g * p_ref[6:7, :], xhat, scale2_ref[:, 0:1])
        outer = d_pre.astype(BF)
        outer_ref[...] = outer
        total_ref[...] = d_pre
        small_ref[0:1, :] = jnp.zeros_like(small_ref[0:1, :])
        small_ref[1:2, :] = jnp.zeros_like(small_ref[1:2, :])
        small_ref[5:6, :] = rows_sum(outer.astype(F32))
        small_ref[6:7, :] = rows_sum(g * xhat)
        small_ref[7:8, :] = rows_sum(g)
        low_ref[...] = (xhat1_ref[...] * p_ref[3:4, :] + p_ref[4:5, :]).astype(BF)

    outer = outer_ref[...]
    d_active = mm_nt(outer, r_ref[...])
    d_inner_full = d_active * slope_ref[...].astype(F32)
    d_inner = d_inner_full.astype(BF)
    gr_ref[...] = mm_tn(act_ref[...], outer).astype(BF)
    ge_ref[...] = mm_tn(low_ref[...], d_inner).astype(BF)
    geb_ref[...] = rows_sum(d_inner.astype(F32))
    total_ref[...] += mm_nt(d_inner, e_ref[...])

    @pl.when(j == pl.num_programs(0) - 1)
    def _():
        d_hidden = total_ref[...]
        xhat = xhat1_ref[...]
        d_summed = norm_back(d_hidden * p_ref[3:4, :], xhat, scale1_ref[:, 0:1])
        dsum_ref[...] = d_summed
        branch = d_summed.astype(BF)
        small_ref[2:3, :] = rows_sum(branch.astype(F32))
        small_ref[3:4, :] = rows_sum(d_hidden * xhat)
        small_ref[4:5, :] = rows_sum(d_hidden)
        go_ref[...] = mm_tn(att_ref[...], branch).astype(BF)
        datt_ref[...] = mm_nt(branch, w_ref[0]).astype(BF)


def ffn_back(g, saved, w4, e, r, params, ride=None):
    x, att, xhat1, scale1, act, slope, xhat2, scale2 = saved
    n, d = x.shape
    ff = e.shape[1]
    fc = min(ff, 512)
    full = whole((n, d))
    thin = whole((n, 128))
    tall = pl.BlockSpec((n, fc), lambda j: (0, j))
    e_spec = pl.BlockSpec((d, fc), lambda j: (0, j))
    r_spec = pl.BlockSpec((fc, d), lambda j: (j, 0))
    return stepped(
        ffn_back_kernel,
        ride,
        "ffn_back",
        ff // fc,
        (g, xhat2, scale2, params, act, slope, r, e, xhat1, scale1, att, w4),
        [
            full, full, thin, whole(params.shape), tall, tall, r_spec, e_spec, full, thin, full,
            pl.BlockSpec((1, d, d), lambda j: (3, 0, 0)),
        ],
        [
            r_spec, e_spec, pl.BlockSpec((1, fc), lambda j: (0, j)), full, whole((d, d)), full, whole((8, d)),
        ],
        [
            jax.ShapeDtypeStruct((ff, d), BF),
            jax.ShapeDtypeStruct((d, ff), BF),
            jax.ShapeDtypeStruct((1, ff), F32),
            jax.ShapeDtypeStruct((n, d), F32),
            jax.ShapeDtypeStruct((d, d), BF),
            jax.ShapeDtypeStruct((n, d), BF),
            jax.ShapeDtypeStruct((8, d), F32),
        ],
        [pltpu.VMEM((n, d), BF), pltpu.VMEM((n, d), BF), pltpu.VMEM((n, d), F32)],
        pl.CostEstimate(
            flops=4 * n * d * (d + 2 * ff), bytes_accessed=4 * d * (d + 2 * ff) + 4 * n * ff + 24 * n * d, transcendentals=0
        ),
    )


def input_back_kernel(others, x_ref, dq_ref, own_ref, *refs):
    other_refs = refs[:others]
    w_ref, dsum_ref, g3_ref, dx_ref, small_ref = refs[others:]
    j = pl.program_id(0)

    def step(grad, row):
        g3_ref[0] = mm_tn(x_ref[...], grad).astype(BF)
        if row is not None:
            small_ref[row : row + 1, :] = rows_sum(grad.astype(F32))
        return mm_nt(grad, w_ref[0])

    def joined(index):
        value = own_ref[index].astype(F32)
        for ref in other_refs:
            value = value + ref[index].astype(F32)
        return value.astype(BF)

    @pl.when(j == 0)
    def _():
        small_ref[...] = jnp.zeros_like(small_ref)
        dx_ref[...] = dsum_ref[...] + step(dq_ref[...], 0)

    @pl.when(j == 1)
    def _():
        dx_ref[...] += step(joined(0), None)

    @pl.when(j == 2)
    def _():
        dx_ref[...] += step(joined(1), 1)


def input_back(x, dq, own, others, w4, dsum):
    n, d = x.shape
    full = whole((n, d))
    return pl.pallas_call(
        partial(input_back_kernel, len(others)),
        name="input_back",
        grid=(3,),
        in_specs=[full, full, whole((2, n, d))]
        + [whole((2, n, d))] * len(others)
        + [pl.BlockSpec((1, d, d), lambda j: (j, 0, 0)), full],
        out_specs=[pl.BlockSpec((1, d, d), lambda j: (j, 0, 0)), full, whole((8, d))],
        out_shape=[
            jax.ShapeDtypeStruct((3, d, d), BF),
            jax.ShapeDtypeStruct((n, d), F32),
            jax.ShapeDtypeStruct((8, d), F32),
        ],
        compiler_params=params_of(("arbitrary",)),
        cost_estimate=pl.CostEstimate(flops=12 * n * d * d, bytes_accessed=12 * d * d + 16 * n * d, transcendentals=0),
    )(x, dq, own, *others, w4, dsum)


class Grid:
    def __init__(self, dp, seq):
        self.ny = max(seq // 2, 1)
        self.nc = seq // self.ny
        self.nx = self.ny if dp % self.ny == 0 else 1
        self.nz = dp // self.nx
        self.sizes = {"z": self.nz, "x": self.nx, "y": self.ny, "c": self.nc}

    def here(self):
        d = lax.axis_index("dp")
        s = lax.axis_index("seq")
        return {"z": d // self.nx, "x": lax.rem(d, self.nx), "y": s // self.nc, "c": lax.rem(s, self.nc)}

    def device(self, at):
        return (at["z"] * self.nx + at["x"], at["y"] * self.nc + at["c"])

    def shifted(self, me, axis, step):
        other = dict(me)
        other[axis] = lax.rem(me[axis] + step, self.sizes[axis])
        return other

    def shape(self):
        return (self.nz, self.nx, self.ny, self.nc)

    def peers(self):
        return [(axis, step) for axis in "zxyc" for step in range(1, self.sizes[axis])]

    def barrier(self, me):
        sem = pltpu.get_barrier_semaphore()
        for axis, step in self.peers():
            pl.semaphore_signal(
                sem, inc=1, device_id=self.device(self.shifted(me, axis, step)), device_id_type=MESH
            )
        pl.semaphore_wait(sem, len(self.peers()))


def picked(place, axes):
    return tuple(slice(None) if axis in axes else place[axis] for axis in "zxyc")


def fine_cuts_of(shapes):
    groups = []
    for group in cuts_of(shapes):
        if any(cut[3][1] % 256 for cut in group):
            groups.append(group)
            continue
        for part in range(2):
            groups.append(
                [
                    (number, lead, rows, (first + part * count // 2, count // 2))
                    for number, lead, rows, (first, count) in group
                ]
            )
    return groups


def cuts_of(shapes):
    groups = []
    for number, shape in enumerate(shapes):
        rows, columns = shape[-2:]
        lead = shape[0] if len(shape) == 3 else None
        if columns % 256:
            groups.append([(number, None, (0, rows), (0, columns))])
            continue
        if lead is not None and lead % 2 == 0:
            pieces = [(number, (k, k + 1), (0, rows), (0, columns)) for k in range(lead)]
        elif lead == 3:
            left, right = (0, columns // 2), (columns // 2, columns // 2)
            pieces = [(number, (0, 1), (0, rows), (0, columns)), (number, (1, 2), (0, rows), (0, columns))]
            pieces += [(number, (2, 3), (0, rows), left), (number, (2, 3), (0, rows), right)]
        elif columns % 1024 == 0:
            pieces = [(number, None, (0, rows), (k * columns // 4, columns // 4)) for k in range(4)]
        elif rows % 32 == 0:
            pieces = [(number, None, (k * rows // 4, rows // 4), (0, columns)) for k in range(4)]
        elif columns % 256 == 0:
            pieces = [(number, None, (0, rows), (k * columns // 2, columns // 2)) for k in range(2)]
        else:
            groups.append([(number, None, (0, rows), (0, columns))])
            continue
        groups += [pieces[k : k + 2] for k in range(0, len(pieces), 2)]
    return groups


def region(ref, shape, cut, index):
    _, lead, rows, columns = cut
    head = ()
    if len(shape) == 3:
        head = (slice(None) if lead is None else slice(*lead),)
    return ref.at[head + tuple(index) + (slice(rows[0], sum(rows)), slice(columns[0], sum(columns)))]


ORDERS = (("z", "x", "y", "c"), ("z", "y", "x", "c"))


class Sender:
    def __init__(self, grid, me, send_sem, recv_sem):
        self.grid, self.me, self.send_sem, self.recv_sem = grid, me, send_sem, recv_sem
        self.started = []

    def send(self, src, dst, axis, step):
        return self.send_to(src, dst, self.grid.device(self.grid.shifted(self.me, axis, step)))

    def send_to(self, src, dst, device):
        k = len(self.started)
        copy = pltpu.make_async_remote_copy(
            src_ref=src, dst_ref=dst, send_sem=self.send_sem.at[k], recv_sem=self.recv_sem.at[k],
            device_id=device, device_id_type=MESH,
        )
        copy.start()
        self.started.append(copy)
        return copy

    def finish(self):
        for copy in self.started:
            copy.wait_send()


def gather_turns(sender, shapes, srcs, dsts, own_sem):
    grid, me = sender.grid, sender.me
    groups = cuts_of(shapes)
    own = []
    first = []
    for group in groups:
        copies = []
        for cut in group:
            shape = shapes[cut[0]]
            src = region(srcs[cut[0]], shape, cut, ())
            dst = region(dsts[cut[0]], shape, cut, picked(me, ""))
            copies.append([sender.send(src, dst, "z", step) for step in range(1, grid.nz)])
        first.append(copies)
    for k in range(len(shapes)):
        head = (slice(None),) if len(shapes[k]) == 3 else ()
        copy = pltpu.make_async_copy(srcs[k], dsts[k].at[head + picked(me, "")], own_sem.at[k])
        copy.start()
        own.append(copy)
    for copy in own:
        copy.wait()
    yield
    stages = {0: first}
    total = len(groups)
    depth = len(ORDERS[0])
    for turn in range(total + depth - 1):
        for stage in range(1, depth):
            g = turn - (stage - 1)
            if not 0 <= g < total:
                continue
            copies = []
            for side, cut in enumerate(groups[g]):
                order = ORDERS[side % 2]
                for copy in stages[stage - 1][g][side]:
                    copy.wait_recv()
                block = region(dsts[cut[0]], shapes[cut[0]], cut, picked(me, order[:stage]))
                copies.append(
                    [sender.send(block, block, order[stage], step) for step in range(1, grid.sizes[order[stage]])]
                )
            stages.setdefault(stage, {})[g] = copies
        g = turn - (depth - 1)
        if 0 <= g < total:
            for copies in stages[depth - 1][g]:
                for copy in copies:
                    copy.wait_recv()
        yield


def gather_kernel(grid, shapes, *refs):
    count = len(shapes)
    me = grid.here()
    grid.barrier(me)
    sender = Sender(grid, me, *refs[2 * count : 2 * count + 2])
    for _ in gather_turns(sender, shapes, refs[:count], refs[count : 2 * count], refs[-1]):
        pass
    sender.finish()


def copies_in(grid, shapes):
    return sum(len(group) for group in cuts_of(shapes)) * len(grid.peers())


def gather(grid, arrays, name, collective_id):
    shapes = [a.shape for a in arrays]
    outs = [a.shape[:-2] + grid.shape() + a.shape[-2:] for a in arrays]
    count = copies_in(grid, shapes)
    got = pl.pallas_call(
        partial(gather_kernel, grid, shapes),
        name=name,
        in_specs=[pl.BlockSpec(memory_space=pltpu.VMEM)] * len(arrays),
        out_specs=[pl.BlockSpec(memory_space=pl.ANY)] * len(arrays),
        out_shape=[jax.ShapeDtypeStruct(s, a.dtype) for s, a in zip(outs, arrays)],
        scratch_shapes=[
            pltpu.SemaphoreType.DMA((count,)),
            pltpu.SemaphoreType.DMA((count,)),
            pltpu.SemaphoreType.DMA((len(arrays),)),
        ],
        compiler_params=pltpu.CompilerParams(
            collective_id=collective_id, has_side_effects=True, vmem_limit_bytes=VMEM_LIMIT
        ),
    )(*arrays)
    blocks = math.prod(grid.shape())
    return [o.reshape(a.shape[:-2] + (blocks * a.shape[-2], a.shape[-1])) for o, a in zip(got, arrays)]


def spread_small(table_ref, thin_refs, wide_refs, rows, blocks):
    lines = table_ref.shape[-2]
    table = table_ref[...].reshape(blocks * lines, 128)

    def picker(per, width):
        column = lax.broadcasted_iota(jnp.int32, (128, width), 1)
        scale = -(-(1 << 20) // per)
        rest = column - lax.shift_right_logical(column * scale, 20) * per
        hot = (lax.broadcasted_iota(jnp.int32, (128, width), 0) == rest).astype(F32).astype(BF)
        place = lax.broadcasted_iota(jnp.int32, (blocks, lines, width), 2)
        owner = lax.broadcasted_iota(jnp.int32, (blocks, lines, width), 0)
        return hot, lax.shift_right_logical(place * scale, 20) == owner

    thin_width = thin_refs[0].shape[-1]
    hot, keep = picker(rows, thin_width)
    wide = mm(table, hot).reshape(blocks, lines, thin_width)
    vectors = jnp.sum(jnp.where(keep, wide, 0.0), axis=0)
    for layer, ref in enumerate(thin_refs):
        ref[...] = vectors[layer * 16 : layer * 16 + ROWS]
    step = 1024
    for first in range(0, wide_refs[0].shape[-1], step):
        scale = -(-(1 << 20) // (4 * rows))
        column = lax.broadcasted_iota(jnp.int32, (128, step), 1) + first
        rest = column - lax.shift_right_logical(column * scale, 20) * (4 * rows)
        hot = (lax.broadcasted_iota(jnp.int32, (128, step), 0) == rest).astype(F32).astype(BF)
        place = lax.broadcasted_iota(jnp.int32, (blocks, lines, step), 2) + first
        owner = lax.broadcasted_iota(jnp.int32, (blocks, lines, step), 0)
        full = mm(table, hot).reshape(blocks, lines, step)
        part = jnp.sum(jnp.where(lax.shift_right_logical(place * scale, 20) == owner, full, 0.0), axis=0)
        for layer, ref in enumerate(wide_refs):
            ref[:, first : first + step] = part[layer * 16 + 8 : layer * 16 + 9]


def front_kernel(grid, shapes, *refs):
    count = len(shapes)
    srcs, refs = refs[:count], refs[count:]
    tokens_ref, refs = refs[0], refs[1:]
    fulls, refs = refs[: count - 1], refs[count - 1 :]
    x_ref, refs = refs[0], refs[1:]
    p1_ref, p2_ref, eb1_ref, eb2_ref, q_ref, kv_ref, far_ref, att_ref, lse_ref = refs[:9]
    out_ref, xhat1_ref, scale1_ref, act_ref, slope_ref, xhat2_ref, scale2_ref = refs[9:16]
    table_ref, w4_ref, r_ref, e_ref, hidden_ref, low_ref, total_ref = refs[16:23]
    send_sem, recv_sem, own_sem, load_sem = refs[23:]
    n, d = x_ref.shape
    ff = e_ref.shape[-1]
    me = grid.here()
    grid.barrier(me)
    sender = Sender(grid, me, send_sem, recv_sem)
    turns = gather_turns(sender, shapes, srcs, (table_ref,) + tuple(fulls), own_sem)
    left = [len(cuts_of(shapes)) + 4]

    def advance(steps=1):
        for _ in range(min(steps, left[0])):
            next(turns)
            left[0] -= 1

    def load(source, target, k):
        copy = pltpu.make_async_copy(source, target, load_sem.at[k])
        copy.start()
        return copy

    def joined(blocks):
        return blocks.astype(F32).reshape(-1, blocks.shape[-1]).astype(BF)

    advance(1)
    rows = tokens_ref.shape[1]
    crossed = sender.send(tokens_ref.at[1 - me["y"]], x_ref.at[pl.ds(rows, rows)], "y", 1)
    x_ref[pl.ds(0, rows), :] = tokens_ref[me["y"]]
    advance(4)
    blocks = math.prod(grid.shape())
    spread_small(table_ref, (p1_ref, p2_ref), (eb1_ref, eb2_ref), shapes[1][-2], blocks)
    advance(2)
    load(fulls[0], w4_ref, 0).wait()
    crossed.wait_recv()
    x = x_ref[...]
    kv_ref[0] = mm(x, joined(w4_ref[1])).astype(BF)
    kv_ref[1] = (mm(x, joined(w4_ref[2])) + p1_ref[1:2, :]).astype(BF)
    swapped = sender.send(kv_ref, far_ref, "c", 1)
    q_ref[...] = (mm(x, joined(w4_ref[0])) + p1_ref[0:1, :]).astype(BF)
    advance(1)
    swapped.wait_recv()
    for pair in range(d // (2 * HD)):
        lanes = slice(pair * 2 * HD, (pair + 1) * 2 * HD)
        kvs = [(r[0, :, lanes], r[1, :, lanes]) for r in (kv_ref, far_ref)]
        att_ref[:, lanes], lse_ref[:, lanes] = attend_pair(q_ref[:, lanes], kvs, None)
        if pair % 2:
            advance(1)
        if pair == 1:
            loads = [load(fulls[1], r_ref, 1)]
    loads.append(load(fulls[2], e_ref, 2))
    summed = x.astype(F32) + mm(att_ref[...], joined(w4_ref[3])) + p1_ref[2:3, :]
    xhat, scale = normed(summed)
    xhat1_ref[...] = xhat
    scale1_ref[...] = jnp.broadcast_to(scale, scale1_ref.shape)
    hidden = xhat * p1_ref[3:4, :] + p1_ref[4:5, :]
    hidden_ref[...] = hidden
    low_ref[...] = hidden.astype(BF)
    for copy in loads:
        copy.wait()
    step = 512
    for first in range(0, ff, step):
        part = slice(first, first + step)
        active, slope = gelu_pair(mm(low_ref[...], joined(e_ref[..., part])) + eb1_ref[:, part])
        active = active.astype(BF)
        act_ref[:, part] = active
        slope_ref[:, part] = slope.astype(BF)
        more = mm(active, r_ref[...].reshape(ff, d)[part, :])
        total_ref[...] = more if first == 0 else total_ref[...] + more
        if first // step % 2:
            advance(1)
    pre = hidden_ref[...] + total_ref[...] + p1_ref[5:6, :]
    xhat, scale = normed(pre)
    xhat2_ref[...] = xhat
    scale2_ref[...] = jnp.broadcast_to(scale, scale2_ref.shape)
    out_ref[...] = (xhat * p1_ref[6:7, :] + p1_ref[7:8, :]).astype(BF)
    advance(left[0])
    sender.finish()


def front(grid, arrays, tokens, name, collective_id):
    shapes = [a.shape for a in arrays]
    n, d = tokens.shape[0] * tokens.shape[1], tokens.shape[2]
    ff = arrays[3].shape[1]
    count = copies_in(grid, shapes) + 2
    vmem = pl.BlockSpec(memory_space=pltpu.VMEM)
    hbm = pl.BlockSpec(memory_space=pl.ANY)
    fulls = [jax.ShapeDtypeStruct(a.shape[:-2] + grid.shape() + a.shape[-2:], BF) for a in arrays[1:]]
    local = [
        ((n, d), BF),
        ((ROWS, d), F32), ((ROWS, d), F32), ((1, ff), F32), ((1, ff), F32),
        ((n, d), BF), ((2, n, d), BF), ((2, n, d), BF), ((n, d), BF), ((n, d), F32),
        ((n, d), BF), ((n, d), F32), ((n, 128), F32), ((n, ff), BF), ((n, ff), BF), ((n, d), F32), ((n, 128), F32),
    ]
    got = pl.pallas_call(
        partial(front_kernel, grid, shapes),
        name=name,
        in_specs=[vmem] * (len(arrays) + 1),
        out_specs=[hbm] * len(fulls) + [vmem] * len(local),
        out_shape=fulls + [jax.ShapeDtypeStruct(*s) for s in local],
        scratch_shapes=[
            pltpu.VMEM(grid.shape() + arrays[0].shape, BF),
            pltpu.VMEM(fulls[0].shape, BF),
            pltpu.VMEM(fulls[1].shape, BF),
            pltpu.VMEM(fulls[2].shape, BF),
            pltpu.VMEM((n, d), F32),
            pltpu.VMEM((n, d), BF),
            pltpu.VMEM((n, d), F32),
            pltpu.SemaphoreType.DMA((count,)),
            pltpu.SemaphoreType.DMA((count,)),
            pltpu.SemaphoreType.DMA((len(arrays),)),
            pltpu.SemaphoreType.DMA((3,)),
        ],
        compiler_params=pltpu.CompilerParams(
            collective_id=collective_id, has_side_effects=True, vmem_limit_bytes=VMEM_LIMIT
        ),
    )(*arrays, tokens)
    blocks = math.prod(grid.shape())
    weights = [
        o.reshape(a.shape[:-2] + (blocks * a.shape[-2], a.shape[-1])) for o, a in zip(got, arrays[1:])
    ]
    return weights, got[len(fulls) :]


BACK_ORDERS = (("c", "x", "y", "z"), ("c", "y", "x", "z"))


def left_axes(order, stage):
    return [axis for axis in "zxyc" if axis not in order[:stage]]


class Scatter:
    def __init__(self, grid, plan, refs):
        shapes, layouts = plan.shapes, plan.layouts
        count = len(shapes)
        self.grid, self.shapes = grid, shapes
        self.me = grid.here()
        self.srcs, self.outs = refs[:count], refs[count : 2 * count]
        held = refs[2 * count : -3]
        send_sem, recv_sem, own_sem = refs[-3:]
        self.groups = fine_cuts_of(shapes)
        self.near = {peer: grid.shifted(self.me, *peer) for peer in grid.peers()}
        devices = {peer: grid.device(at) for peer, at in self.near.items()}
        self.buffers, self.own, self.flights = {}, {}, {}
        position = piece = number = 0
        for g, group in enumerate(self.groups):
            for side, cut in enumerate(group):
                order = BACK_ORDERS[side % 2]
                head = (slice(None),) if self.lead_of(cut) else ()
                for stage in range(len(layouts[piece])):
                    buf = held[position]
                    position += 1
                    self.buffers[g, side, stage] = buf
                    axis = order[stage]
                    copies = []
                    for step in range(1, grid.sizes[axis]):
                        there = self.near[axis, step]
                        if stage == 0:
                            src = region(self.srcs[cut[0]], shapes[cut[0]], cut, picked(there, "zxy"))
                        else:
                            index = tuple(
                                there[a] if a == axis else slice(None) for a in left_axes(order, stage)
                            )
                            src = self.buffers[g, side, stage - 1].at[(0,) + head + index]
                        slot = step - 1 if stage == len(layouts[piece]) - 1 else step
                        copies.append(
                            pltpu.make_async_remote_copy(
                                src_ref=src, dst_ref=buf.at[slot],
                                send_sem=send_sem.at[number], recv_sem=recv_sem.at[number],
                                device_id=devices[axis, step], device_id_type=MESH,
                            )
                        )
                        number += 1
                    self.flights[g, side, stage] = copies
                src = region(self.srcs[cut[0]], shapes[cut[0]], cut, picked(self.me, "zxy"))
                self.own[g, side] = pltpu.make_async_copy(src, self.buffers[g, side, 0].at[0], own_sem.at[piece])
                piece += 1

    def lead_of(self, cut):
        return len(self.shapes[cut[0]]) == 3

    def start(self):
        self.grid.barrier(self.me)
        for g, group in enumerate(self.groups):
            for side in range(len(group)):
                self.own[g, side].start()
                for copy in self.flights[g, side, 0]:
                    copy.start()

    def turn(self, number):
        depth = 4
        for stage in range(depth):
            g = number - stage
            if not 0 <= g < len(self.groups):
                continue
            for side, cut in enumerate(self.groups[g]):
                order = BACK_ORDERS[side % 2]
                buf = self.buffers[g, side, stage]
                for copy in self.flights[g, side, stage]:
                    copy.wait_recv()
                if stage == 0:
                    self.own[g, side].wait()
                    add_into(buf, self.lead_of(cut))
                else:
                    source = self.buffers[g, side, stage - 1]
                    rest = left_axes(order, stage)
                    if stage == depth - 1:
                        head = (slice(None),) if self.lead_of(cut) else ()
                        total = source[(0,) + head + tuple(self.me[a] for a in rest)].astype(F32)
                        for slot in range(buf.shape[0]):
                            total = total + buf[slot].astype(F32)
                        region(self.outs[cut[0]], self.shapes[cut[0]], cut, ())[...] = total
                        continue
                    merge(source, buf, self.me, rest, order[stage], self.lead_of(cut))
                for copy in self.flights[g, side, stage + 1]:
                    copy.start()

    def finish(self):
        for copies in self.flights.values():
            for copy in copies:
                copy.wait_send()

    def turns(self):
        steps = [partial(self.turn, k) for k in range(len(self.groups) + 3)]
        return [self.start] + steps + [self.finish]


def total_of(values):
    if len(values) == 2:
        return values[0] + values[1]
    total = values[0].astype(F32)
    for value in values[1:]:
        total = total + value.astype(F32)
    return total.astype(values[0].dtype)


def add_into(buf, lead):
    head = (slice(None),) if lead else ()

    def body(i, carry):
        at = head + (i,)
        buf[(0,) + at] = total_of([buf[(slot,) + at] for slot in range(buf.shape[0])])
        return carry

    lax.fori_loop(0, buf.shape[1 + len(head)], body, 0)


def merge(source, buf, me, axes, axis, lead):
    head = (slice(None),) if lead else ()
    inner = tuple(me[a] if a == axis else slice(None) for a in axes[1:])

    def body(i, carry):
        at = head + (i,)
        values = [source[(0,) + at + inner]] + [buf[(slot,) + at] for slot in range(1, buf.shape[0])]
        buf[(0,) + at] = total_of(values)
        return carry

    lax.fori_loop(0, buf.shape[1 + len(head)], body, 0)


class ScatterPlan:
    def __init__(self, grid, arrays):
        blocks = math.prod(grid.shape())
        self.shapes = [a.shape[:-2] + (a.shape[-2] // blocks, a.shape[-1]) for a in arrays]
        self.views = [a.reshape(s[:-2] + grid.shape() + s[-2:]) for a, s in zip(arrays, self.shapes)]
        self.layouts = []
        self.scratch = []
        for group in fine_cuts_of(self.shapes):
            for side, cut in enumerate(group):
                shape = self.shapes[cut[0]]
                order = BACK_ORDERS[side % 2]
                head = ()
                if len(shape) == 3:
                    head = (shape[0] if cut[1] is None else cut[1][1] - cut[1][0],)
                stages = []
                for stage in range(4):
                    rest = left_axes(order, stage + 1)
                    slots = grid.sizes[order[stage]] - (1 if stage == 3 else 0)
                    stages.append((slots,) + head + tuple(grid.sizes[a] for a in rest) + (cut[2][1], cut[3][1]))
                self.layouts.append(stages)
                self.scratch += [pltpu.VMEM(s, arrays[cut[0]].dtype) for s in stages]
        count = len(self.layouts) * len(grid.peers())
        self.scratch += [
            pltpu.SemaphoreType.DMA((count,)),
            pltpu.SemaphoreType.DMA((count,)),
            pltpu.SemaphoreType.DMA((len(self.layouts),)),
        ]
        self.outs = [jax.ShapeDtypeStruct(s, F32) for s in self.shapes]


def scatter(grid, arrays, name, collective_id):
    plan = ScatterPlan(grid, arrays)

    def kernel(*refs):
        for step in Scatter(grid, plan, refs).turns():
            step()

    return pl.pallas_call(
        kernel,
        name=name,
        in_specs=[pl.BlockSpec(memory_space=pl.ANY)] * len(arrays),
        out_specs=[pl.BlockSpec(memory_space=pltpu.VMEM)] * len(arrays),
        out_shape=plan.outs,
        scratch_shapes=plan.scratch,
        compiler_params=pltpu.CompilerParams(
            collective_id=collective_id, has_side_effects=True, vmem_limit_bytes=VMEM_LIMIT
        ),
    )(*plan.views)


def stepped(body, ride, name, steps, args, in_specs, out_specs, out_shape, scratch, cost):
    if ride is None:
        out = pl.pallas_call(
            body, name=name, grid=(steps,), in_specs=in_specs, out_specs=out_specs, out_shape=out_shape,
            scratch_shapes=scratch, compiler_params=params_of(("arbitrary",)), cost_estimate=cost,
        )(*args)
        return out, ()
    grid, arrays, collective_id = ride
    plan = ScatterPlan(grid, arrays)
    count, riders = len(args), len(arrays)
    results, locals_ = len(out_shape), len(scratch)

    def kernel(*refs):
        ins, refs = refs[:count], refs[count:]
        views, refs = refs[:riders], refs[riders:]
        outs, refs = refs[:results], refs[results:]
        sums, refs = refs[:riders], refs[riders:]
        own, refs = refs[:locals_], refs[locals_:]
        turns = Scatter(grid, plan, views + sums + refs).turns()
        j = pl.program_id(0)
        for k, turn in enumerate(turns[:steps]):
            pl.when(j == k)(turn)
        body(*ins, *outs, *own)

        @pl.when(j == steps - 1)
        def _():
            for turn in turns[steps:]:
                turn()

    out = pl.pallas_call(
        kernel,
        name=name,
        grid=(steps,),
        in_specs=in_specs + [pl.BlockSpec(memory_space=pl.ANY)] * riders,
        out_specs=out_specs + [whole(s.shape) for s in plan.outs],
        out_shape=out_shape + plan.outs,
        scratch_shapes=scratch + plan.scratch,
        compiler_params=pltpu.CompilerParams(
            dimension_semantics=("arbitrary",), collective_id=collective_id, has_side_effects=True,
            vmem_limit_bytes=VMEM_LIMIT,
        ),
        cost_estimate=cost,
    )(*args, *plan.views)
    return out[:results], out[results:]


ROWS = 8
ROW_AT = (1, 4, 6, 7, 8, 12, 13, 14)


def pack_small(layers):
    parts = []
    for params in layers:
        parts += [params[k] for k in ROW_AT] + [params[10]]
    flat = jnp.concatenate(parts)
    size = 1024 * -(-flat.shape[0] // 1024)
    return jnp.pad(flat, (0, size - flat.shape[0])).reshape(size // 128, 128)


def small_table(layers):
    lines = []
    for params in layers:
        for k in ROW_AT + (10,):
            lines.append(jnp.pad(params[k], (0, 128 - params[k].shape[0])))
        lines += [jnp.zeros((128,), BF)] * 7
    return jnp.stack(lines)


def unpack_small(full, blocks, rows, layers):
    per = full.shape[0] // blocks * full.shape[1]
    flat = full.reshape(blocks, per)
    out = []
    width = (ROWS + 4) * rows
    for layer in range(layers):
        part = flat[:, layer * width : (layer + 1) * width].astype(F32)
        thin = part[:, : ROWS * rows].reshape(blocks, ROWS, rows).transpose(1, 0, 2).reshape(ROWS, blocks * rows)
        out.append((thin, part[:, ROWS * rows :].reshape(1, blocks * 4 * rows)))
    return out


def pack_grads(grads, blocks, rows):
    parts = []
    for thin, wide in grads:
        parts.append(thin.reshape(ROWS, blocks, rows).transpose(1, 0, 2).reshape(blocks, ROWS * rows))
        parts.append(wide.reshape(blocks, 4 * rows))
    flat = jnp.concatenate(parts, axis=1)
    size = 1024 * -(-flat.shape[1] // 1024)
    return jnp.pad(flat, ((0, 0), (0, size - flat.shape[1]))).reshape(blocks * (size // 128), 128)


def on_device(grid, tokens, early, cot_backbone, cot_head, lengths, cls_pos, *weights):
    layers = (weights[:15], weights[15:])
    members = lax.axis_size("seq")
    blocks = math.prod(grid.shape())
    seqs, rows, width = tokens.shape
    half = members // seqs
    spot = lax.axis_index("seq")
    mine = spot // half
    swap = [(i, (i + half) % members) for i in range(members)]
    far = lax.rem(spot + half, members)
    masked = rows * members > MIN_LEN

    def spread(value):
        kept = lax.dynamic_index_in_dim(value, mine, 0, keepdims=False)
        sent = lax.dynamic_index_in_dim(value, 1 - mine, 0, keepdims=False)
        return jnp.concatenate([kept, lax.ppermute(sent, "seq", swap)], axis=0)

    def cross(value):
        return lax.ppermute(value[rows:], "seq", swap)

    def collect(value, got):
        kept = value[:rows]
        return jnp.where(mine == 0, jnp.stack([kept, got]), jnp.stack([got, kept]))

    def around(value, step):
        pairs = [(i, i // half * half + (i % half + step) % half) for i in range(members)]
        return lax.ppermute(value, "seq", pairs)

    length = lax.dynamic_index_in_dim(lengths, mine, 0, keepdims=False)
    cls = lax.dynamic_index_in_dim(cls_pos, mine, 0, keepdims=False)
    line = jnp.arange(rows, dtype=jnp.int32)
    positions = jnp.concatenate([spot * rows + line, far * rows + line])
    is_cls = (positions == cls)[:, None]
    valid = (positions < length)[:, None]
    biases = None
    if masked:
        steps = []
        for step in range(half):
            member = mine * half + lax.rem(lax.rem(spot, half) - step + half, half)
            other = lax.rem(member + half, members)
            place = jnp.concatenate([member * rows + line, other * rows + line])
            steps.append(jnp.where(place < length, 0.0, NEG)[None, :])
        biases = jnp.stack(steps)

    x_early = spread(early)
    g_back = spread(cot_backbone)
    g_head = spread(cot_head)
    if masked:
        g_back = jnp.where(valid, g_back, jnp.zeros_like(g_back))
        g_head = jnp.where(valid, g_head, jnp.zeros_like(g_head))

    shard = layers[0][0].shape[0]
    stacked = [jnp.stack([p[0], p[2], p[3], p[5]]) for p in layers]
    fused = shard % 8 == 0 and half == 2 and not masked
    if fused:
        travel = [small_table(layers)]
        for k in range(2):
            travel += [stacked[k], layers[k][11], layers[k][9]]
        (w4_back, r_back, e_back, w4_head, r_head, e_head), kept = front(grid, travel, tokens, "front", 0)
        x_back, kept = kept[0], kept[1:]
        p_back, p_head, eb_back, eb_head, q, kv, far_kv, att, lse, back_low = kept[:10]
        back_kept = (q, [kv, far_kv], lse, (x_back, att) + tuple(kept[10:]))
    else:
        x_back = spread(tokens)
        small = pack_small(layers)
        w4_back, e_back, r_back, small_full = gather(
            grid, [stacked[0], layers[0][9], layers[0][11], small], "gather_back", 0
        )
        w4_head, e_head, r_head = gather(grid, [stacked[1], layers[1][9], layers[1][11]], "gather_head", 1)
        (p_back, eb_back), (p_head, eb_head) = unpack_small(small_full, blocks, shard, 2)

    def forward(x, w4, e, r, params, eb, held=None):
        q, kv = qkv(x, w4, params)
        kvs = [kv] + [around(kv, step) for step in range(1, half)]
        att, lse = attend(q, kvs, biases)
        if held is not None:
            att, held = lax.optimization_barrier((att, held))
        out, xhat1, scale1, act, slope, xhat2, scale2 = post(x, att, w4, e, eb, r, params)
        return out, (q, kvs, lse, (x, att, xhat1, scale1, act, slope, xhat2, scale2)), held

    def backward(g, kept, w4, e, r, params, before, number, held):
        q, kvs, lse, saved = kept
        x, att = saved[:2]
        ride = None if before is None else (grid, before, number)
        (gr, ge, geb, dsum, go, datt, small_a), sums = ffn_back(g, saved, w4, e, r, params, ride)
        datt, held = lax.optimization_barrier((datt, held))
        dq, dkvs, wide = attend_back(q, datt, att, lse, kvs, biases, (grid, [ge, gr], number + 1))
        others = [around(dkvs[step], half - step) for step in range(1, half)]
        g3, dx, small_b = input_back(x, dq, dkvs[0], others, w4, dsum)
        return dx, [g3, go[None]], (small_a + small_b, geb), wide, sums, held

    if not fused:
        back_low, back_kept, _ = forward(x_back, w4_back, e_back, r_back, p_back, eb_back)
    head_in = jnp.where(is_cls, back_low, x_early)
    head_low, head_kept, back_far = forward(head_in, w4_head, e_head, r_head, p_head, eb_head, cross(back_low))
    dx_head, narrow_head, small_head, (seh, srh), _, head_far = backward(
        g_head, head_kept, w4_head, e_head, r_head, p_head, None, 2, cross(head_low)
    )
    early_low = jnp.where(is_cls, 0.0, dx_head).astype(BF)
    g_mixed = g_back.astype(F32) + jnp.where(is_cls, dx_head, 0.0)
    dx_back, narrow_back, small_back, (seb, srb), (s3h, soh), early_far = backward(
        g_mixed, back_kept, w4_back, e_back, r_back, p_back, narrow_head, 4, cross(early_low)
    )
    packed = pack_grads([small_back, small_head], blocks, shard)
    s3b, sob, small_sum = scatter(grid, narrow_back + [packed], "scatter_back", 6)

    back_grad = dx_back.astype(BF)
    flat = small_sum.reshape(-1)

    def layer_grads(layer, s3, so, se, sr):
        base = layer * (ROWS + 4) * shard
        thin = [flat[base + k * shard : base + (k + 1) * shard] for k in range(ROWS)]
        wide = flat[base + ROWS * shard : base + (ROWS + 4) * shard]
        return (
            s3[0], thin[0], s3[1], s3[2], thin[1], so[0], thin[2], thin[3], thin[4],
            se, wide, sr, thin[5], thin[6], thin[7],
        )

    return (
        collect(back_low, back_far),
        collect(head_low, head_far),
        collect(back_grad, cross(back_grad)),
        collect(early_low, early_far),
    ) + layer_grads(0, s3b, sob, seb, srb) + layer_grads(1, s3h, soh, seh, srh)


def solution(mesh):
    rows = P("dp", "seq", None)
    wide = P(("dp", "seq"), None)
    thin = P(("dp", "seq"))
    layer = tuple(thin if k in (1, 4, 6, 7, 8, 10, 12, 13, 14) else wide for k in range(15))
    grid = Grid(mesh.shape["dp"], mesh.shape["seq"])
    return jax.shard_map(
        partial(on_device, grid),
        mesh=mesh,
        in_specs=(rows,) * 4 + (P("dp"),) * 2 + layer + layer,
        out_specs=(rows,) * 4 + layer + layer,
        check_vma=False,
    )
```

```python
from functools import partial
import math

import jax
import jax.numpy as jnp
from jax import lax
from jax.experimental import pallas as pl
from jax.experimental.pallas import tpu as pltpu
from jax.sharding import PartitionSpec as P

H = 12
HD = 64
EPS = 1e-12
NEG = -1e30
MIN_LEN = 1024
BF = jnp.bfloat16
F32 = jnp.float32
MESH = pl.DeviceIdType.MESH
VMEM_LIMIT = 60 * 1024 * 1024


def mm(left, right):
    return lax.dot_general(left, right, (((1,), (0,)), ((), ())), preferred_element_type=F32)


def mm_nt(left, right):
    return lax.dot_general(left, right, (((1,), (1,)), ((), ())), preferred_element_type=F32)


def mm_tn(left, right):
    return lax.dot_general(left, right, (((0,), (0,)), ((), ())), preferred_element_type=F32)


def whole(shape):
    return pl.BlockSpec(shape, lambda *_: (0,) * len(shape))


def params_of(semantics):
    return pltpu.CompilerParams(dimension_semantics=semantics, vmem_limit_bytes=VMEM_LIMIT)


def qkv_kernel(x_ref, w_ref, p_ref, q_ref, kv_ref):
    j = pl.program_id(0)
    out = mm(x_ref[...], w_ref[0])

    @pl.when(j == 0)
    def _():
        q_ref[...] = (out + p_ref[0:1, :]).astype(BF)

    @pl.when(j == 1)
    def _():
        kv_ref[0] = out.astype(BF)

    @pl.when(j == 2)
    def _():
        kv_ref[0] = (out + p_ref[1:2, :]).astype(BF)


def qkv(x, w4, params):
    n, d = x.shape
    return pl.pallas_call(
        qkv_kernel,
        name="qkv",
        grid=(3,),
        in_specs=[
            whole((n, d)),
            pl.BlockSpec((1, d, d), lambda j: (j, 0, 0)),
            whole(params.shape),
        ],
        out_specs=[
            whole((n, d)),
            pl.BlockSpec((1, n, d), lambda j: (jnp.maximum(j - 1, 0), 0, 0)),
        ],
        out_shape=[
            jax.ShapeDtypeStruct((n, d), BF),
            jax.ShapeDtypeStruct((2, n, d), BF),
        ],
        compiler_params=params_of(("arbitrary",)),
        cost_estimate=pl.CostEstimate(flops=6 * n * d * d, bytes_accessed=6 * d * d + 8 * n * d, transcendentals=0),
    )(x, w4, params)


def half_masks(n):
    lane = lax.broadcasted_iota(jnp.int32, (n, 2 * HD), 1)
    return lane < HD


def attend_pair(q, kvs, biases):
    n = q.shape[0]
    low = half_masks(n)
    q = q * jnp.asarray(HD**-0.5, BF)
    outs = []
    logs = []
    for side in range(2):
        qm = jnp.where(low if side == 0 else ~low, q, jnp.zeros_like(q))
        scores = []
        for t, (key, _) in enumerate(kvs):
            s = mm_nt(qm, key)
            if biases is not None:
                s = s + biases[t]
            scores.append(s)
        top = scores[0].max(axis=-1, keepdims=True)
        for s in scores[1:]:
            top = jnp.maximum(top, s.max(axis=-1, keepdims=True))
        total = jnp.zeros((n, 1), F32)
        numer = jnp.zeros((n, 2 * HD), F32)
        for t, (_, value) in enumerate(kvs):
            weight = jnp.exp(scores[t] - top)
            total = total + weight.sum(axis=-1, keepdims=True)
            numer = numer + mm(weight.astype(BF), value)
        outs.append(numer / total)
        logs.append(top + jnp.log(total))
    return jnp.where(low, outs[0], outs[1]).astype(BF), jnp.where(low, logs[0], logs[1])


def attend_kernel(pieces, masked, *refs):
    q_ref = refs[0]
    kv_refs = refs[1 : 1 + pieces]
    refs = refs[1 + pieces :]
    biases = None
    if masked:
        biases, refs = [refs[0][t] for t in range(pieces)], refs[1:]
    att_ref, lse_ref = refs
    att_ref[...], lse_ref[...] = attend_pair(q_ref[...], [(r[0], r[1]) for r in kv_refs], biases)


def attend(q, kvs, biases):
    n, d = q.shape
    pieces = len(kvs)
    masked = biases is not None
    pair = 2 * HD
    col = pl.BlockSpec((n, pair), lambda j: (0, j))
    kv_spec = pl.BlockSpec((2, n, pair), lambda j: (0, 0, j))
    extra = (biases,) if masked else ()
    return pl.pallas_call(
        partial(attend_kernel, pieces, masked),
        name="attend",
        grid=(d // pair,),
        in_specs=[col] + [kv_spec] * pieces + [whole(b.shape) for b in extra],
        out_specs=[col, col],
        out_shape=[jax.ShapeDtypeStruct((n, d), BF), jax.ShapeDtypeStruct((n, d), F32)],
        compiler_params=params_of(("arbitrary",)),
        cost_estimate=pl.CostEstimate(
            flops=4 * n * n * pieces * d, bytes_accessed=(8 + 4 * pieces) * n * d, transcendentals=n * n * pieces * H
        ),
    )(q, *kvs, *extra)


def attend_back_kernel(pieces, masked, *refs):
    q_ref, do_ref, att_ref, lse_ref = refs[:4]
    kv_refs = refs[4 : 4 + pieces]
    refs = refs[4 + pieces :]
    bias_ref = None
    if masked:
        bias_ref, refs = refs[0], refs[1:]
    dq_ref = refs[0]
    dkv_refs = refs[1:]
    n = q_ref.shape[0]
    scale = HD**-0.5
    low = half_masks(n)
    q = q_ref[...] * jnp.asarray(scale, BF)
    do = do_ref[...]
    prod = do.astype(F32) * att_ref[...].astype(F32)
    dq = jnp.zeros((n, 2 * HD), F32)
    qms, doms, deltas, lses = [], [], [], []
    for side in range(2):
        mask = low if side == 0 else ~low
        qms.append(jnp.where(mask, q, jnp.zeros_like(q)))
        doms.append(jnp.where(mask, do, jnp.zeros_like(do)))
        deltas.append(jnp.sum(jnp.where(mask, prod, 0.0), axis=-1, keepdims=True))
        lses.append(lse_ref[:, side * HD : side * HD + 1])
    dqs = [jnp.zeros((n, 2 * HD), F32) for _ in range(2)]
    for t in range(pieces):
        k = kv_refs[t][0]
        v = kv_refs[t][1]
        dk = jnp.zeros((n, 2 * HD), F32)
        dv = jnp.zeros((n, 2 * HD), F32)
        for side in range(2):
            s = mm_nt(qms[side], k)
            if masked:
                s = s + bias_ref[t]
            p = jnp.exp(s - lses[side])
            dp = mm_nt(doms[side], v)
            ds = (p * (dp - deltas[side])).astype(BF)
            dv = dv + mm_tn(p.astype(BF), doms[side])
            dk = dk + mm_tn(ds, qms[side])
            dqs[side] = dqs[side] + mm(ds, k)
        dkv_refs[t][0] = dk.astype(BF)
        dkv_refs[t][1] = dv.astype(BF)
    dq_ref[...] = (jnp.where(low, dqs[0], dqs[1]) * scale).astype(BF)


def attend_back(q, do, att, lse, kvs, biases, ride=None):
    n, d = q.shape
    pieces = len(kvs)
    masked = biases is not None
    pair = 2 * HD
    col = pl.BlockSpec((n, pair), lambda j: (0, j))
    kv_spec = pl.BlockSpec((2, n, pair), lambda j: (0, 0, j))
    extra = (biases,) if masked else ()
    out, sums = stepped(
        partial(attend_back_kernel, pieces, masked),
        ride,
        "attend_back",
        d // pair,
        (q, do, att, lse, *kvs, *extra),
        [col] * 4 + [kv_spec] * pieces + [whole(b.shape) for b in extra],
        [col] + [kv_spec] * pieces,
        [jax.ShapeDtypeStruct((n, d), BF)] + [jax.ShapeDtypeStruct((2, n, d), BF)] * pieces,
        [],
        pl.CostEstimate(
            flops=10 * n * n * pieces * d, bytes_accessed=(12 + 8 * pieces) * n * d, transcendentals=n * n * pieces * H
        ),
    )
    return out[0], out[1:], sums


def normed(value):
    mean = jnp.mean(value, axis=-1, keepdims=True)
    centred = value - mean
    spread = jnp.mean(centred * centred, axis=-1, keepdims=True)
    scale = lax.rsqrt(spread + EPS)
    return centred * scale, scale


def norm_back(grad, xhat, scale):
    mean_grad = jnp.mean(grad, axis=-1, keepdims=True)
    mean_dot = jnp.mean(grad * xhat, axis=-1, keepdims=True)
    return scale * (grad - mean_grad - xhat * mean_dot)


def gelu_pair(value):
    cdf = 0.5 + 0.5 * lax.erf(value * (0.5**0.5))
    pdf = jnp.exp(-0.5 * value * value) * ((2.0 * math.pi) ** -0.5)
    return value * cdf, cdf + value * pdf


def post_kernel(
    x_ref, att_ref, w_ref, e_ref, eb_ref, r_ref, p_ref,
    out_ref, xhat1_ref, scale1_ref, act_ref, slope_ref, xhat2_ref, scale2_ref,
    hidden_ref, low_ref, total_ref,
):
    j = pl.program_id(0)
    lanes = scale1_ref.shape

    @pl.when(j == 0)
    def _():
        summed = x_ref[...].astype(F32) + mm(att_ref[...], w_ref[0]) + p_ref[2:3, :]
        xhat, scale = normed(summed)
        xhat1_ref[...] = xhat
        scale1_ref[...] = jnp.broadcast_to(scale, lanes)
        hidden = xhat * p_ref[3:4, :] + p_ref[4:5, :]
        hidden_ref[...] = hidden
        low_ref[...] = hidden.astype(BF)
        total_ref[...] = jnp.zeros_like(total_ref)

    inner = mm(low_ref[...], e_ref[...]) + eb_ref[...]
    active, slope = gelu_pair(inner)
    active = active.astype(BF)
    act_ref[...] = active
    slope_ref[...] = slope.astype(BF)
    total_ref[...] += mm(active, r_ref[...])

    @pl.when(j == pl.num_programs(0) - 1)
    def _():
        pre = hidden_ref[...] + total_ref[...] + p_ref[5:6, :]
        xhat, scale = normed(pre)
        xhat2_ref[...] = xhat
        scale2_ref[...] = jnp.broadcast_to(scale, lanes)
        out_ref[...] = (xhat * p_ref[6:7, :] + p_ref[7:8, :]).astype(BF)


def post(x, att, w4, e, eb, r, params):
    n, d = x.shape
    ff = e.shape[1]
    fc = min(ff, 512)
    full = whole((n, d))
    thin = whole((n, 128))
    tall = pl.BlockSpec((n, fc), lambda j: (0, j))
    return pl.pallas_call(
        post_kernel,
        name="post",
        grid=(ff // fc,),
        in_specs=[
            full, full,
            pl.BlockSpec((1, d, d), lambda j: (3, 0, 0)),
            pl.BlockSpec((d, fc), lambda j: (0, j)),
            pl.BlockSpec((1, fc), lambda j: (0, j)),
            pl.BlockSpec((fc, d), lambda j: (j, 0)),
            whole(params.shape),
        ],
        out_specs=[full, full, thin, tall, tall, full, thin],
        out_shape=[
            jax.ShapeDtypeStruct((n, d), BF),
            jax.ShapeDtypeStruct((n, d), F32),
            jax.ShapeDtypeStruct((n, 128), F32),
            jax.ShapeDtypeStruct((n, ff), BF),
            jax.ShapeDtypeStruct((n, ff), BF),
            jax.ShapeDtypeStruct((n, d), F32),
            jax.ShapeDtypeStruct((n, 128), F32),
        ],
        scratch_shapes=[pltpu.VMEM((n, d), F32), pltpu.VMEM((n, d), BF), pltpu.VMEM((n, d), F32)],
        compiler_params=params_of(("arbitrary",)),
        cost_estimate=pl.CostEstimate(
            flops=2 * n * d * (d + 2 * ff), bytes_accessed=2 * d * (d + 2 * ff) + 4 * n * ff + 16 * n * d, transcendentals=2 * n * ff
        ),
    )(x, att, w4, e, eb, r, params)


def rows_sum(value):
    return jnp.sum(value, axis=0, keepdims=True)


def ffn_back_kernel(
    g_ref, xhat2_ref, scale2_ref, p_ref, act_ref, slope_ref, r_ref, e_ref, xhat1_ref, scale1_ref, att_ref, w_ref,
    gr_ref, ge_ref, geb_ref, dsum_ref, go_ref, datt_ref, small_ref,
    outer_ref, low_ref, total_ref,
):
    j = pl.program_id(0)

    @pl.when(j == 0)
    def _():
        g = g_ref[...].astype(F32)
        xhat = xhat2_ref[...]
        d_pre = norm_back(g * p_ref[6:7, :], xhat, scale2_ref[:, 0:1])
        outer = d_pre.astype(BF)
        outer_ref[...] = outer
        total_ref[...] = d_pre
        small_ref[0:1, :] = jnp.zeros_like(small_ref[0:1, :])
        small_ref[1:2, :] = jnp.zeros_like(small_ref[1:2, :])
        small_ref[5:6, :] = rows_sum(outer.astype(F32))
        small_ref[6:7, :] = rows_sum(g * xhat)
        small_ref[7:8, :] = rows_sum(g)
        low_ref[...] = (xhat1_ref[...] * p_ref[3:4, :] + p_ref[4:5, :]).astype(BF)

    outer = outer_ref[...]
    d_active = mm_nt(outer, r_ref[...])
    d_inner_full = d_active * slope_ref[...].astype(F32)
    d_inner = d_inner_full.astype(BF)
    gr_ref[...] = mm_tn(act_ref[...], outer).astype(BF)
    ge_ref[...] = mm_tn(low_ref[...], d_inner).astype(BF)
    geb_ref[...] = rows_sum(d_inner.astype(F32))
    total_ref[...] += mm_nt(d_inner, e_ref[...])

    @pl.when(j == pl.num_programs(0) - 1)
    def _():
        d_hidden = total_ref[...]
        xhat = xhat1_ref[...]
        d_summed = norm_back(d_hidden * p_ref[3:4, :], xhat, scale1_ref[:, 0:1])
        dsum_ref[...] = d_summed
        branch = d_summed.astype(BF)
        small_ref[2:3, :] = rows_sum(branch.astype(F32))
        small_ref[3:4, :] = rows_sum(d_hidden * xhat)
        small_ref[4:5, :] = rows_sum(d_hidden)
        go_ref[...] = mm_tn(att_ref[...], branch).astype(BF)
        datt_ref[...] = mm_nt(branch, w_ref[0]).astype(BF)


def ffn_back(g, saved, w4, e, r, params, ride=None):
    x, att, xhat1, scale1, act, slope, xhat2, scale2 = saved
    n, d = x.shape
    ff = e.shape[1]
    fc = min(ff, 512)
    full = whole((n, d))
    thin = whole((n, 128))
    tall = pl.BlockSpec((n, fc), lambda j: (0, j))
    e_spec = pl.BlockSpec((d, fc), lambda j: (0, j))
    r_spec = pl.BlockSpec((fc, d), lambda j: (j, 0))
    return stepped(
        ffn_back_kernel,
        ride,
        "ffn_back",
        ff // fc,
        (g, xhat2, scale2, params, act, slope, r, e, xhat1, scale1, att, w4),
        [
            full, full, thin, whole(params.shape), tall, tall, r_spec, e_spec, full, thin, full,
            pl.BlockSpec((1, d, d), lambda j: (3, 0, 0)),
        ],
        [
            r_spec, e_spec, pl.BlockSpec((1, fc), lambda j: (0, j)), full, whole((d, d)), full, whole((8, d)),
        ],
        [
            jax.ShapeDtypeStruct((ff, d), BF),
            jax.ShapeDtypeStruct((d, ff), BF),
            jax.ShapeDtypeStruct((1, ff), F32),
            jax.ShapeDtypeStruct((n, d), F32),
            jax.ShapeDtypeStruct((d, d), BF),
            jax.ShapeDtypeStruct((n, d), BF),
            jax.ShapeDtypeStruct((8, d), F32),
        ],
        [pltpu.VMEM((n, d), BF), pltpu.VMEM((n, d), BF), pltpu.VMEM((n, d), F32)],
        pl.CostEstimate(
            flops=4 * n * d * (d + 2 * ff), bytes_accessed=4 * d * (d + 2 * ff) + 4 * n * ff + 24 * n * d, transcendentals=0
        ),
    )


def input_back_kernel(others, x_ref, dq_ref, own_ref, *refs):
    other_refs = refs[:others]
    w_ref, dsum_ref, g3_ref, dx_ref, small_ref = refs[others:]
    j = pl.program_id(0)

    def step(grad, row):
        g3_ref[0] = mm_tn(x_ref[...], grad).astype(BF)
        if row is not None:
            small_ref[row : row + 1, :] = rows_sum(grad.astype(F32))
        return mm_nt(grad, w_ref[0])

    def joined(index):
        value = own_ref[index].astype(F32)
        for ref in other_refs:
            value = value + ref[index].astype(F32)
        return value.astype(BF)

    @pl.when(j == 0)
    def _():
        small_ref[...] = jnp.zeros_like(small_ref)
        dx_ref[...] = dsum_ref[...] + step(dq_ref[...], 0)

    @pl.when(j == 1)
    def _():
        dx_ref[...] += step(joined(0), None)

    @pl.when(j == 2)
    def _():
        dx_ref[...] += step(joined(1), 1)


def input_back(x, dq, own, others, w4, dsum):
    n, d = x.shape
    full = whole((n, d))
    return pl.pallas_call(
        partial(input_back_kernel, len(others)),
        name="input_back",
        grid=(3,),
        in_specs=[full, full, whole((2, n, d))]
        + [whole((2, n, d))] * len(others)
        + [pl.BlockSpec((1, d, d), lambda j: (j, 0, 0)), full],
        out_specs=[pl.BlockSpec((1, d, d), lambda j: (j, 0, 0)), full, whole((8, d))],
        out_shape=[
            jax.ShapeDtypeStruct((3, d, d), BF),
            jax.ShapeDtypeStruct((n, d), F32),
            jax.ShapeDtypeStruct((8, d), F32),
        ],
        compiler_params=params_of(("arbitrary",)),
        cost_estimate=pl.CostEstimate(flops=12 * n * d * d, bytes_accessed=12 * d * d + 16 * n * d, transcendentals=0),
    )(x, dq, own, *others, w4, dsum)


class Grid:
    def __init__(self, dp, seq):
        self.ny = max(seq // 2, 1)
        self.nc = seq // self.ny
        self.nx = self.ny if dp % self.ny == 0 else 1
        self.nz = dp // self.nx
        self.sizes = {"z": self.nz, "x": self.nx, "y": self.ny, "c": self.nc}

    def here(self):
        d = lax.axis_index("dp")
        s = lax.axis_index("seq")
        return {"z": d // self.nx, "x": lax.rem(d, self.nx), "y": s // self.nc, "c": lax.rem(s, self.nc)}

    def device(self, at):
        return (at["z"] * self.nx + at["x"], at["y"] * self.nc + at["c"])

    def shifted(self, me, axis, step):
        other = dict(me)
        other[axis] = lax.rem(me[axis] + step, self.sizes[axis])
        return other

    def shape(self):
        return (self.nz, self.nx, self.ny, self.nc)

    def peers(self):
        return [(axis, step) for axis in "zxyc" for step in range(1, self.sizes[axis])]

    def barrier(self, me):
        sem = pltpu.get_barrier_semaphore()
        for axis, step in self.peers():
            pl.semaphore_signal(
                sem, inc=1, device_id=self.device(self.shifted(me, axis, step)), device_id_type=MESH
            )
        pl.semaphore_wait(sem, len(self.peers()))


def picked(place, axes):
    return tuple(slice(None) if axis in axes else place[axis] for axis in "zxyc")


def fine_cuts_of(shapes):
    groups = []
    for group in cuts_of(shapes):
        if len(group) == 1 and groups:
            groups[-1] = groups[-1] + group
            continue
        if any(cut[3][1] % 256 for cut in group):
            groups.append(group)
            continue
        for part in range(2):
            groups.append(
                [
                    (number, lead, rows, (first + part * count // 2, count // 2))
                    for number, lead, rows, (first, count) in group
                ]
            )
    return groups


def cuts_of(shapes):
    groups = []
    for number, shape in enumerate(shapes):
        rows, columns = shape[-2:]
        lead = shape[0] if len(shape) == 3 else None
        if columns % 256:
            groups.append([(number, None, (0, rows), (0, columns))])
            continue
        if lead is not None and lead % 2 == 0:
            pieces = [(number, (k, k + 1), (0, rows), (0, columns)) for k in range(lead)]
        elif lead == 3:
            left, right = (0, columns // 2), (columns // 2, columns // 2)
            pieces = [(number, (0, 1), (0, rows), (0, columns)), (number, (1, 2), (0, rows), (0, columns))]
            pieces += [(number, (2, 3), (0, rows), left), (number, (2, 3), (0, rows), right)]
        elif columns % 1024 == 0:
            pieces = [(number, None, (0, rows), (k * columns // 4, columns // 4)) for k in range(4)]
        elif rows % 32 == 0:
            pieces = [(number, None, (k * rows // 4, rows // 4), (0, columns)) for k in range(4)]
        elif columns % 256 == 0:
            pieces = [(number, None, (0, rows), (k * columns // 2, columns // 2)) for k in range(2)]
        else:
            groups.append([(number, None, (0, rows), (0, columns))])
            continue
        groups += [pieces[k : k + 2] for k in range(0, len(pieces), 2)]
    return groups


def region(ref, shape, cut, index):
    _, lead, rows, columns = cut
    head = ()
    if len(shape) == 3:
        head = (slice(None) if lead is None else slice(*lead),)
    return ref.at[head + tuple(index) + (slice(rows[0], sum(rows)), slice(columns[0], sum(columns)))]


ORDERS = (("z", "x", "y", "c"), ("z", "y", "x", "c"))


class Sender:
    def __init__(self, grid, me, send_sem, recv_sem):
        self.grid, self.me, self.send_sem, self.recv_sem = grid, me, send_sem, recv_sem
        self.started = []

    def send(self, src, dst, axis, step):
        return self.send_to(src, dst, self.grid.device(self.grid.shifted(self.me, axis, step)))

    def send_to(self, src, dst, device):
        k = len(self.started)
        copy = pltpu.make_async_remote_copy(
            src_ref=src, dst_ref=dst, send_sem=self.send_sem.at[k], recv_sem=self.recv_sem.at[k],
            device_id=device, device_id_type=MESH,
        )
        copy.start()
        self.started.append(copy)
        return copy

    def finish(self):
        for copy in self.started:
            copy.wait_send()


def gather_turns(sender, shapes, srcs, dsts, own_sem):
    grid, me = sender.grid, sender.me
    groups = cuts_of(shapes)
    own = []
    first = []
    for group in groups:
        copies = []
        for cut in group:
            shape = shapes[cut[0]]
            src = region(srcs[cut[0]], shape, cut, ())
            dst = region(dsts[cut[0]], shape, cut, picked(me, ""))
            copies.append([sender.send(src, dst, "z", step) for step in range(1, grid.nz)])
        first.append(copies)
    for k in range(len(shapes)):
        head = (slice(None),) if len(shapes[k]) == 3 else ()
        copy = pltpu.make_async_copy(srcs[k], dsts[k].at[head + picked(me, "")], own_sem.at[k])
        copy.start()
        own.append(copy)
    for copy in own:
        copy.wait()
    yield
    stages = {0: first}
    total = len(groups)
    depth = len(ORDERS[0])
    for turn in range(total + depth - 1):
        for stage in range(1, depth):
            g = turn - (stage - 1)
            if not 0 <= g < total:
                continue
            copies = []
            for side, cut in enumerate(groups[g]):
                order = ORDERS[side % 2]
                for copy in stages[stage - 1][g][side]:
                    copy.wait_recv()
                block = region(dsts[cut[0]], shapes[cut[0]], cut, picked(me, order[:stage]))
                copies.append(
                    [sender.send(block, block, order[stage], step) for step in range(1, grid.sizes[order[stage]])]
                )
            stages.setdefault(stage, {})[g] = copies
        g = turn - (depth - 1)
        if 0 <= g < total:
            for copies in stages[depth - 1][g]:
                for copy in copies:
                    copy.wait_recv()
        yield


def gather_kernel(grid, shapes, *refs):
    count = len(shapes)
    me = grid.here()
    grid.barrier(me)
    sender = Sender(grid, me, *refs[2 * count : 2 * count + 2])
    for _ in gather_turns(sender, shapes, refs[:count], refs[count : 2 * count], refs[-1]):
        pass
    sender.finish()


def copies_in(grid, shapes):
    return sum(len(group) for group in cuts_of(shapes)) * len(grid.peers())


def gather(grid, arrays, name, collective_id):
    shapes = [a.shape for a in arrays]
    outs = [a.shape[:-2] + grid.shape() + a.shape[-2:] for a in arrays]
    count = copies_in(grid, shapes)
    got = pl.pallas_call(
        partial(gather_kernel, grid, shapes),
        name=name,
        in_specs=[pl.BlockSpec(memory_space=pltpu.VMEM)] * len(arrays),
        out_specs=[pl.BlockSpec(memory_space=pl.ANY)] * len(arrays),
        out_shape=[jax.ShapeDtypeStruct(s, a.dtype) for s, a in zip(outs, arrays)],
        scratch_shapes=[
            pltpu.SemaphoreType.DMA((count,)),
            pltpu.SemaphoreType.DMA((count,)),
            pltpu.SemaphoreType.DMA((len(arrays),)),
        ],
        compiler_params=pltpu.CompilerParams(
            collective_id=collective_id, has_side_effects=True, vmem_limit_bytes=VMEM_LIMIT
        ),
    )(*arrays)
    blocks = math.prod(grid.shape())
    return [o.reshape(a.shape[:-2] + (blocks * a.shape[-2], a.shape[-1])) for o, a in zip(got, arrays)]


def spread_small(table_ref, thin_refs, wide_refs, rows, blocks):
    lines = table_ref.shape[-2]
    table = table_ref[...].reshape(blocks * lines, 128)

    def picker(per, width):
        column = lax.broadcasted_iota(jnp.int32, (128, width), 1)
        scale = -(-(1 << 20) // per)
        rest = column - lax.shift_right_logical(column * scale, 20) * per
        hot = (lax.broadcasted_iota(jnp.int32, (128, width), 0) == rest).astype(F32).astype(BF)
        place = lax.broadcasted_iota(jnp.int32, (blocks, lines, width), 2)
        owner = lax.broadcasted_iota(jnp.int32, (blocks, lines, width), 0)
        return hot, lax.shift_right_logical(place * scale, 20) == owner

    thin_width = thin_refs[0].shape[-1]
    hot, keep = picker(rows, thin_width)
    wide = mm(table, hot).reshape(blocks, lines, thin_width)
    vectors = jnp.sum(jnp.where(keep, wide, 0.0), axis=0)
    for layer, ref in enumerate(thin_refs):
        ref[...] = vectors[layer * 16 : layer * 16 + ROWS]
    step = 1024
    for first in range(0, wide_refs[0].shape[-1], step):
        scale = -(-(1 << 20) // (4 * rows))
        column = lax.broadcasted_iota(jnp.int32, (128, step), 1) + first
        rest = column - lax.shift_right_logical(column * scale, 20) * (4 * rows)
        hot = (lax.broadcasted_iota(jnp.int32, (128, step), 0) == rest).astype(F32).astype(BF)
        place = lax.broadcasted_iota(jnp.int32, (blocks, lines, step), 2) + first
        owner = lax.broadcasted_iota(jnp.int32, (blocks, lines, step), 0)
        full = mm(table, hot).reshape(blocks, lines, step)
        part = jnp.sum(jnp.where(lax.shift_right_logical(place * scale, 20) == owner, full, 0.0), axis=0)
        for layer, ref in enumerate(wide_refs):
            ref[:, first : first + step] = part[layer * 16 + 8 : layer * 16 + 9]


def front_kernel(grid, shapes, *refs):
    count = len(shapes)
    srcs, refs = refs[:count], refs[count:]
    tokens_ref, refs = refs[0], refs[1:]
    fulls, refs = refs[: count - 1], refs[count - 1 :]
    x_ref, refs = refs[0], refs[1:]
    p1_ref, p2_ref, eb1_ref, eb2_ref, q_ref, kv_ref, far_ref, att_ref, lse_ref = refs[:9]
    out_ref, xhat1_ref, scale1_ref, act_ref, slope_ref, xhat2_ref, scale2_ref = refs[9:16]
    table_ref, w4_ref, r_ref, e_ref, hidden_ref, low_ref, total_ref = refs[16:23]
    send_sem, recv_sem, own_sem, load_sem = refs[23:]
    n, d = x_ref.shape
    ff = e_ref.shape[-1]
    me = grid.here()
    grid.barrier(me)
    sender = Sender(grid, me, send_sem, recv_sem)
    turns = gather_turns(sender, shapes, srcs, (table_ref,) + tuple(fulls), own_sem)
    left = [len(cuts_of(shapes)) + 4]

    def advance(steps=1):
        for _ in range(min(steps, left[0])):
            next(turns)
            left[0] -= 1

    def load(source, target, k):
        copy = pltpu.make_async_copy(source, target, load_sem.at[k])
        copy.start()
        return copy

    def joined(blocks):
        return blocks.astype(F32).reshape(-1, blocks.shape[-1]).astype(BF)

    advance(1)
    rows = tokens_ref.shape[1]
    crossed = sender.send(tokens_ref.at[1 - me["y"]], x_ref.at[pl.ds(rows, rows)], "y", 1)
    x_ref[pl.ds(0, rows), :] = tokens_ref[me["y"]]
    advance(4)
    blocks = math.prod(grid.shape())
    spread_small(table_ref, (p1_ref, p2_ref), (eb1_ref, eb2_ref), shapes[1][-2], blocks)
    advance(2)
    load(fulls[0], w4_ref, 0).wait()
    crossed.wait_recv()
    x = x_ref[...]
    kv_ref[0] = mm(x, joined(w4_ref[1])).astype(BF)
    kv_ref[1] = (mm(x, joined(w4_ref[2])) + p1_ref[1:2, :]).astype(BF)
    swapped = sender.send(kv_ref, far_ref, "c", 1)
    q_ref[...] = (mm(x, joined(w4_ref[0])) + p1_ref[0:1, :]).astype(BF)
    advance(1)
    swapped.wait_recv()
    for pair in range(d // (2 * HD)):
        lanes = slice(pair * 2 * HD, (pair + 1) * 2 * HD)
        kvs = [(r[0, :, lanes], r[1, :, lanes]) for r in (kv_ref, far_ref)]
        att_ref[:, lanes], lse_ref[:, lanes] = attend_pair(q_ref[:, lanes], kvs, None)
        if pair % 2:
            advance(1)
        if pair == 1:
            loads = [load(fulls[1], r_ref, 1)]
    loads.append(load(fulls[2], e_ref, 2))
    summed = x.astype(F32) + mm(att_ref[...], joined(w4_ref[3])) + p1_ref[2:3, :]
    xhat, scale = normed(summed)
    xhat1_ref[...] = xhat
    scale1_ref[...] = jnp.broadcast_to(scale, scale1_ref.shape)
    hidden = xhat * p1_ref[3:4, :] + p1_ref[4:5, :]
    hidden_ref[...] = hidden
    low_ref[...] = hidden.astype(BF)
    for copy in loads:
        copy.wait()
    step = 512
    for first in range(0, ff, step):
        part = slice(first, first + step)
        active, slope = gelu_pair(mm(low_ref[...], joined(e_ref[..., part])) + eb1_ref[:, part])
        active = active.astype(BF)
        act_ref[:, part] = active
        slope_ref[:, part] = slope.astype(BF)
        more = mm(active, r_ref[...].reshape(ff, d)[part, :])
        total_ref[...] = more if first == 0 else total_ref[...] + more
        if first // step % 2:
            advance(1)
    pre = hidden_ref[...] + total_ref[...] + p1_ref[5:6, :]
    xhat, scale = normed(pre)
    xhat2_ref[...] = xhat
    scale2_ref[...] = jnp.broadcast_to(scale, scale2_ref.shape)
    out_ref[...] = (xhat * p1_ref[6:7, :] + p1_ref[7:8, :]).astype(BF)
    advance(left[0])
    sender.finish()


def front(grid, arrays, tokens, name, collective_id):
    shapes = [a.shape for a in arrays]
    n, d = tokens.shape[0] * tokens.shape[1], tokens.shape[2]
    ff = arrays[3].shape[1]
    count = copies_in(grid, shapes) + 2
    vmem = pl.BlockSpec(memory_space=pltpu.VMEM)
    hbm = pl.BlockSpec(memory_space=pl.ANY)
    fulls = [jax.ShapeDtypeStruct(a.shape[:-2] + grid.shape() + a.shape[-2:], BF) for a in arrays[1:]]
    local = [
        ((n, d), BF),
        ((ROWS, d), F32), ((ROWS, d), F32), ((1, ff), F32), ((1, ff), F32),
        ((n, d), BF), ((2, n, d), BF), ((2, n, d), BF), ((n, d), BF), ((n, d), F32),
        ((n, d), BF), ((n, d), F32), ((n, 128), F32), ((n, ff), BF), ((n, ff), BF), ((n, d), F32), ((n, 128), F32),
    ]
    got = pl.pallas_call(
        partial(front_kernel, grid, shapes),
        name=name,
        in_specs=[vmem] * (len(arrays) + 1),
        out_specs=[hbm] * len(fulls) + [vmem] * len(local),
        out_shape=fulls + [jax.ShapeDtypeStruct(*s) for s in local],
        scratch_shapes=[
            pltpu.VMEM(grid.shape() + arrays[0].shape, BF),
            pltpu.VMEM(fulls[0].shape, BF),
            pltpu.VMEM(fulls[1].shape, BF),
            pltpu.VMEM(fulls[2].shape, BF),
            pltpu.VMEM((n, d), F32),
            pltpu.VMEM((n, d), BF),
            pltpu.VMEM((n, d), F32),
            pltpu.SemaphoreType.DMA((count,)),
            pltpu.SemaphoreType.DMA((count,)),
            pltpu.SemaphoreType.DMA((len(arrays),)),
            pltpu.SemaphoreType.DMA((3,)),
        ],
        compiler_params=pltpu.CompilerParams(
            collective_id=collective_id, has_side_effects=True, vmem_limit_bytes=VMEM_LIMIT
        ),
    )(*arrays, tokens)
    blocks = math.prod(grid.shape())
    weights = [
        o.reshape(a.shape[:-2] + (blocks * a.shape[-2], a.shape[-1])) for o, a in zip(got, arrays[1:])
    ]
    return weights, got[len(fulls) :]


BACK_ORDERS = (("c", "x", "y", "z"), ("c", "y", "x", "z"))


def left_axes(order, stage):
    return [axis for axis in "zxyc" if axis not in order[:stage]]


class Scatter:
    def __init__(self, grid, plan, refs):
        shapes, layouts = plan.shapes, plan.layouts
        count = len(shapes)
        self.grid, self.shapes = grid, shapes
        self.me = grid.here()
        self.srcs, self.outs = refs[:count], refs[count : 2 * count]
        held = refs[2 * count : -3]
        send_sem, recv_sem, own_sem = refs[-3:]
        self.groups = fine_cuts_of(shapes)
        self.near = {peer: grid.shifted(self.me, *peer) for peer in grid.peers()}
        devices = {peer: grid.device(at) for peer, at in self.near.items()}
        self.buffers, self.own, self.flights = {}, {}, {}
        position = piece = number = 0
        for g, group in enumerate(self.groups):
            for side, cut in enumerate(group):
                order = BACK_ORDERS[side % 2]
                head = (slice(None),) if self.lead_of(cut) else ()
                for stage in range(len(layouts[piece])):
                    buf = held[position]
                    position += 1
                    self.buffers[g, side, stage] = buf
                    axis = order[stage]
                    copies = []
                    for step in range(1, grid.sizes[axis]):
                        there = self.near[axis, step]
                        if stage == 0:
                            src = region(self.srcs[cut[0]], shapes[cut[0]], cut, picked(there, "zxy"))
                        else:
                            index = tuple(
                                there[a] if a == axis else slice(None) for a in left_axes(order, stage)
                            )
                            src = self.buffers[g, side, stage - 1].at[(0,) + head + index]
                        slot = step - 1 if stage == len(layouts[piece]) - 1 else step
                        copies.append(
                            pltpu.make_async_remote_copy(
                                src_ref=src, dst_ref=buf.at[slot],
                                send_sem=send_sem.at[number], recv_sem=recv_sem.at[number],
                                device_id=devices[axis, step], device_id_type=MESH,
                            )
                        )
                        number += 1
                    self.flights[g, side, stage] = copies
                src = region(self.srcs[cut[0]], shapes[cut[0]], cut, picked(self.me, "zxy"))
                self.own[g, side] = pltpu.make_async_copy(src, self.buffers[g, side, 0].at[0], own_sem.at[piece])
                piece += 1

    def lead_of(self, cut):
        return len(self.shapes[cut[0]]) == 3

    def start(self):
        self.grid.barrier(self.me)
        for g, group in enumerate(self.groups):
            for side in range(len(group)):
                self.own[g, side].start()
                for copy in self.flights[g, side, 0]:
                    copy.start()

    def turn(self, number):
        depth = 4
        for stage in range(depth):
            g = number - stage
            if not 0 <= g < len(self.groups):
                continue
            for side, cut in enumerate(self.groups[g]):
                order = BACK_ORDERS[side % 2]
                buf = self.buffers[g, side, stage]
                for copy in self.flights[g, side, stage]:
                    copy.wait_recv()
                if stage == 0:
                    self.own[g, side].wait()
                    add_into(buf, self.lead_of(cut))
                else:
                    source = self.buffers[g, side, stage - 1]
                    rest = left_axes(order, stage)
                    if stage == depth - 1:
                        head = (slice(None),) if self.lead_of(cut) else ()
                        total = source[(0,) + head + tuple(self.me[a] for a in rest)].astype(F32)
                        for slot in range(buf.shape[0]):
                            total = total + buf[slot].astype(F32)
                        region(self.outs[cut[0]], self.shapes[cut[0]], cut, ())[...] = total
                        continue
                    merge(source, buf, self.me, rest, order[stage], self.lead_of(cut))
                for copy in self.flights[g, side, stage + 1]:
                    copy.start()

    def finish(self):
        for copies in self.flights.values():
            for copy in copies:
                copy.wait_send()

    def turns(self):
        steps = [partial(self.turn, k) for k in range(len(self.groups) + 3)]
        return [self.start] + steps + [self.finish]


def total_of(values):
    if len(values) == 2:
        return values[0] + values[1]
    total = values[0].astype(F32)
    for value in values[1:]:
        total = total + value.astype(F32)
    return total.astype(values[0].dtype)


def add_into(buf, lead):
    head = (slice(None),) if lead else ()

    def body(i, carry):
        at = head + (i,)
        buf[(0,) + at] = total_of([buf[(slot,) + at] for slot in range(buf.shape[0])])
        return carry

    lax.fori_loop(0, buf.shape[1 + len(head)], body, 0)


def merge(source, buf, me, axes, axis, lead):
    head = (slice(None),) if lead else ()
    inner = tuple(me[a] if a == axis else slice(None) for a in axes[1:])

    def body(i, carry):
        at = head + (i,)
        values = [source[(0,) + at + inner]] + [buf[(slot,) + at] for slot in range(1, buf.shape[0])]
        buf[(0,) + at] = total_of(values)
        return carry

    lax.fori_loop(0, buf.shape[1 + len(head)], body, 0)


class ScatterPlan:
    def __init__(self, grid, arrays):
        blocks = math.prod(grid.shape())
        self.shapes = [a.shape[:-2] + (a.shape[-2] // blocks, a.shape[-1]) for a in arrays]
        self.views = [a.reshape(s[:-2] + grid.shape() + s[-2:]) for a, s in zip(arrays, self.shapes)]
        self.layouts = []
        self.scratch = []
        for group in fine_cuts_of(self.shapes):
            for side, cut in enumerate(group):
                shape = self.shapes[cut[0]]
                order = BACK_ORDERS[side % 2]
                head = ()
                if len(shape) == 3:
                    head = (shape[0] if cut[1] is None else cut[1][1] - cut[1][0],)
                stages = []
                for stage in range(4):
                    rest = left_axes(order, stage + 1)
                    slots = grid.sizes[order[stage]] - (1 if stage == 3 else 0)
                    stages.append((slots,) + head + tuple(grid.sizes[a] for a in rest) + (cut[2][1], cut[3][1]))
                self.layouts.append(stages)
                self.scratch += [pltpu.VMEM(s, arrays[cut[0]].dtype) for s in stages]
        count = len(self.layouts) * len(grid.peers())
        self.scratch += [
            pltpu.SemaphoreType.DMA((count,)),
            pltpu.SemaphoreType.DMA((count,)),
            pltpu.SemaphoreType.DMA((len(self.layouts),)),
        ]
        self.outs = [jax.ShapeDtypeStruct(s, F32) for s in self.shapes]


def scatter(grid, arrays, name, collective_id):
    plan = ScatterPlan(grid, arrays)

    def kernel(*refs):
        for step in Scatter(grid, plan, refs).turns():
            step()

    return pl.pallas_call(
        kernel,
        name=name,
        in_specs=[pl.BlockSpec(memory_space=pl.ANY)] * len(arrays),
        out_specs=[pl.BlockSpec(memory_space=pltpu.VMEM)] * len(arrays),
        out_shape=plan.outs,
        scratch_shapes=plan.scratch,
        compiler_params=pltpu.CompilerParams(
            collective_id=collective_id, has_side_effects=True, vmem_limit_bytes=VMEM_LIMIT
        ),
    )(*plan.views)


def stepped(body, ride, name, steps, args, in_specs, out_specs, out_shape, scratch, cost):
    if ride is None:
        out = pl.pallas_call(
            body, name=name, grid=(steps,), in_specs=in_specs, out_specs=out_specs, out_shape=out_shape,
            scratch_shapes=scratch, compiler_params=params_of(("arbitrary",)), cost_estimate=cost,
        )(*args)
        return out, ()
    grid, arrays, collective_id = ride
    plan = ScatterPlan(grid, arrays)
    count, riders = len(args), len(arrays)
    results, locals_ = len(out_shape), len(scratch)

    def kernel(*refs):
        ins, refs = refs[:count], refs[count:]
        views, refs = refs[:riders], refs[riders:]
        outs, refs = refs[:results], refs[results:]
        sums, refs = refs[:riders], refs[riders:]
        own, refs = refs[:locals_], refs[locals_:]
        turns = Scatter(grid, plan, views + sums + refs).turns()
        j = pl.program_id(0)
        for k, turn in enumerate(turns[:steps]):
            pl.when(j == k)(turn)
        body(*ins, *outs, *own)

        @pl.when(j == steps - 1)
        def _():
            for turn in turns[steps:]:
                turn()

    out = pl.pallas_call(
        kernel,
        name=name,
        grid=(steps,),
        in_specs=in_specs + [pl.BlockSpec(memory_space=pl.ANY)] * riders,
        out_specs=out_specs + [whole(s.shape) for s in plan.outs],
        out_shape=out_shape + plan.outs,
        scratch_shapes=scratch + plan.scratch,
        compiler_params=pltpu.CompilerParams(
            dimension_semantics=("arbitrary",), collective_id=collective_id, has_side_effects=True,
            vmem_limit_bytes=VMEM_LIMIT,
        ),
        cost_estimate=cost,
    )(*args, *plan.views)
    return out[:results], out[results:]


ROWS = 8
ROW_AT = (1, 4, 6, 7, 8, 12, 13, 14)


def pack_small(layers):
    parts = []
    for params in layers:
        parts += [params[k] for k in ROW_AT] + [params[10]]
    flat = jnp.concatenate(parts)
    size = 1024 * -(-flat.shape[0] // 1024)
    return jnp.pad(flat, (0, size - flat.shape[0])).reshape(size // 128, 128)


def small_table(layers):
    lines = []
    for params in layers:
        for k in ROW_AT + (10,):
            lines.append(jnp.pad(params[k], (0, 128 - params[k].shape[0])))
        lines += [jnp.zeros((128,), BF)] * 7
    return jnp.stack(lines)


def unpack_small(full, blocks, rows, layers):
    per = full.shape[0] // blocks * full.shape[1]
    flat = full.reshape(blocks, per)
    out = []
    width = (ROWS + 4) * rows
    for layer in range(layers):
        part = flat[:, layer * width : (layer + 1) * width].astype(F32)
        thin = part[:, : ROWS * rows].reshape(blocks, ROWS, rows).transpose(1, 0, 2).reshape(ROWS, blocks * rows)
        out.append((thin, part[:, ROWS * rows :].reshape(1, blocks * 4 * rows)))
    return out


def pack_grads(grads, blocks, rows):
    parts = []
    for thin, wide in grads:
        parts.append(thin.reshape(ROWS, blocks, rows).transpose(1, 0, 2).reshape(blocks, ROWS * rows))
        parts.append(wide.reshape(blocks, 4 * rows))
    flat = jnp.concatenate(parts, axis=1)
    size = 1024 * -(-flat.shape[1] // 1024)
    return jnp.pad(flat, ((0, 0), (0, size - flat.shape[1]))).reshape(blocks * (size // 128), 128)


def on_device(grid, tokens, early, cot_backbone, cot_head, lengths, cls_pos, *weights):
    layers = (weights[:15], weights[15:])
    members = lax.axis_size("seq")
    blocks = math.prod(grid.shape())
    seqs, rows, width = tokens.shape
    half = members // seqs
    spot = lax.axis_index("seq")
    mine = spot // half
    swap = [(i, (i + half) % members) for i in range(members)]
    far = lax.rem(spot + half, members)
    masked = rows * members > MIN_LEN

    def spread(value):
        kept = lax.dynamic_index_in_dim(value, mine, 0, keepdims=False)
        sent = lax.dynamic_index_in_dim(value, 1 - mine, 0, keepdims=False)
        return jnp.concatenate([kept, lax.ppermute(sent, "seq", swap)], axis=0)

    def cross(value):
        return lax.ppermute(value[rows:], "seq", swap)

    def collect(value, got):
        kept = value[:rows]
        return jnp.where(mine == 0, jnp.stack([kept, got]), jnp.stack([got, kept]))

    def around(value, step):
        pairs = [(i, i // half * half + (i % half + step) % half) for i in range(members)]
        return lax.ppermute(value, "seq", pairs)

    length = lax.dynamic_index_in_dim(lengths, mine, 0, keepdims=False)
    cls = lax.dynamic_index_in_dim(cls_pos, mine, 0, keepdims=False)
    line = jnp.arange(rows, dtype=jnp.int32)
    positions = jnp.concatenate([spot * rows + line, far * rows + line])
    is_cls = (positions == cls)[:, None]
    valid = (positions < length)[:, None]
    biases = None
    if masked:
        steps = []
        for step in range(half):
            member = mine * half + lax.rem(lax.rem(spot, half) - step + half, half)
            other = lax.rem(member + half, members)
            place = jnp.concatenate([member * rows + line, other * rows + line])
            steps.append(jnp.where(place < length, 0.0, NEG)[None, :])
        biases = jnp.stack(steps)

    x_early = spread(early)
    g_back = spread(cot_backbone)
    g_head = spread(cot_head)
    if masked:
        g_back = jnp.where(valid, g_back, jnp.zeros_like(g_back))
        g_head = jnp.where(valid, g_head, jnp.zeros_like(g_head))

    shard = layers[0][0].shape[0]
    stacked = [jnp.stack([p[0], p[2], p[3], p[5]]) for p in layers]
    fused = shard % 8 == 0 and half == 2 and not masked
    if fused:
        travel = [small_table(layers)]
        for k in range(2):
            travel += [stacked[k], layers[k][11], layers[k][9]]
        (w4_back, r_back, e_back, w4_head, r_head, e_head), kept = front(grid, travel, tokens, "front", 0)
        x_back, kept = kept[0], kept[1:]
        p_back, p_head, eb_back, eb_head, q, kv, far_kv, att, lse, back_low = kept[:10]
        back_kept = (q, [kv, far_kv], lse, (x_back, att) + tuple(kept[10:]))
    else:
        x_back = spread(tokens)
        small = pack_small(layers)
        w4_back, e_back, r_back, small_full = gather(
            grid, [stacked[0], layers[0][9], layers[0][11], small], "gather_back", 0
        )
        w4_head, e_head, r_head = gather(grid, [stacked[1], layers[1][9], layers[1][11]], "gather_head", 1)
        (p_back, eb_back), (p_head, eb_head) = unpack_small(small_full, blocks, shard, 2)

    def forward(x, w4, e, r, params, eb, held=None):
        q, kv = qkv(x, w4, params)
        kvs = [kv] + [around(kv, step) for step in range(1, half)]
        att, lse = attend(q, kvs, biases)
        if held is not None:
            att, held = lax.optimization_barrier((att, held))
        out, xhat1, scale1, act, slope, xhat2, scale2 = post(x, att, w4, e, eb, r, params)
        return out, (q, kvs, lse, (x, att, xhat1, scale1, act, slope, xhat2, scale2)), held

    def backward(g, kept, w4, e, r, params, before, number, held):
        q, kvs, lse, saved = kept
        x, att = saved[:2]
        ride = None if before is None else (grid, before, number)
        (gr, ge, geb, dsum, go, datt, small_a), sums = ffn_back(g, saved, w4, e, r, params, ride)
        datt, held = lax.optimization_barrier((datt, held))
        dq, dkvs, wide = attend_back(q, datt, att, lse, kvs, biases, (grid, [ge, gr], number + 1))
        others = [around(dkvs[step], half - step) for step in range(1, half)]
        g3, dx, small_b = input_back(x, dq, dkvs[0], others, w4, dsum)
        return dx, [g3, go[None]], (small_a + small_b, geb), wide, sums, held

    if not fused:
        back_low, back_kept, _ = forward(x_back, w4_back, e_back, r_back, p_back, eb_back)
    head_in = jnp.where(is_cls, back_low, x_early)
    head_low, head_kept, back_far = forward(head_in, w4_head, e_head, r_head, p_head, eb_head, cross(back_low))
    dx_head, narrow_head, small_head, (seh, srh), _, head_far = backward(
        g_head, head_kept, w4_head, e_head, r_head, p_head, None, 2, cross(head_low)
    )
    early_low = jnp.where(is_cls, 0.0, dx_head).astype(BF)
    g_mixed = g_back.astype(F32) + jnp.where(is_cls, dx_head, 0.0)
    dx_back, narrow_back, small_back, (seb, srb), (s3h, soh), early_far = backward(
        g_mixed, back_kept, w4_back, e_back, r_back, p_back, narrow_head, 4, cross(early_low)
    )
    packed = pack_grads([small_back, small_head], blocks, shard)
    s3b, sob, small_sum = scatter(grid, narrow_back + [packed], "scatter_back", 6)

    back_grad = dx_back.astype(BF)
    flat = small_sum.reshape(-1)

    def layer_grads(layer, s3, so, se, sr):
        base = layer * (ROWS + 4) * shard
        thin = [flat[base + k * shard : base + (k + 1) * shard] for k in range(ROWS)]
        wide = flat[base + ROWS * shard : base + (ROWS + 4) * shard]
        return (
            s3[0], thin[0], s3[1], s3[2], thin[1], so[0], thin[2], thin[3], thin[4],
            se, wide, sr, thin[5], thin[6], thin[7],
        )

    return (
        collect(back_low, back_far),
        collect(head_low, head_far),
        collect(back_grad, cross(back_grad)),
        collect(early_low, early_far),
    ) + layer_grads(0, s3b, sob, seb, srb) + layer_grads(1, s3h, soh, seh, srh)


def solution(mesh):
    rows = P("dp", "seq", None)
    wide = P(("dp", "seq"), None)
    thin = P(("dp", "seq"))
    layer = tuple(thin if k in (1, 4, 6, 7, 8, 10, 12, 13, 14) else wide for k in range(15))
    grid = Grid(mesh.shape["dp"], mesh.shape["seq"])
    return jax.shard_map(
        partial(on_device, grid),
        mesh=mesh,
        in_specs=(rows,) * 4 + (P("dp"),) * 2 + layer + layer,
        out_specs=(rows,) * 4 + layer + layer,
        check_vma=False,
    )
```
